256 devices in a mesh: seq: 64 (over y, z, core), head: 4 (over x).
Axes of the slice: x: 4, y: 4, z: 8, core: 2. Of those that a mesh axis runs over, the one named last changes fastest.
Arguments:
- queries: bfloat16 [8192, 4096], P('seq', 'head'), may hold values from -6 to 6
- keys: bfloat16 [8192, 4096], P('seq', 'head'), may hold values from -6 to 6
- values: bfloat16 [8192, 4096], P('seq', 'head'), may hold values from -6 to 6
- hazard_weight: bfloat16 [4096, 4096], P(None, 'head'), may hold values from -0.09375 to 0.09375
- log_base: float32 [32, 4096], P(None, 'head'), as said below
- time_bin: int32 [8192], P('seq'), may hold values from 0 to 31
- observed: int32 [8192], P('seq'), may hold values 0 or 1
- task_label: int32 [8192], P('seq'), may hold values from 0 to 4095
Outputs:
- grad_queries: bfloat16 [8192, 4096], P('seq', 'head')
- grad_keys: bfloat16 [8192, 4096], P('seq', 'head')
- grad_values: bfloat16 [8192, 4096], P('seq', 'head')
- event_loss: float32 [8192], P('seq')
The draws below stay inside these ranges and needn't reach their ends.
Inputs may be any that keep to these rules, and one draw needn't show every extreme that they name: `log_base`: each entry is the logarithm of a positive baseline rate.
All inputs are finite; a program needn't handle non-finite values. No bound on the sum of `observed` on one device may be relied on, other than what follows from the above.
Results may differ from the reference program's by a relative error of at most 0.02.
Values may be sent and summed in bfloat16 or wider, within the bound.
A program may use at most 128 MiB of HBM per device.

```python
import math
import jax
import jax.numpy as jnp
import numpy as np
from jax import lax

HEADS = 32
HEAD_DIM = 128
TASKS = 4096
BINS = 32
TOK_DEV = 128
D = 4096
TOKENS = 8192
N_SEQ = 64


def draw_log_base(key, part):
    noise_key = jax.random.fold_in(key, 17)
    position = jnp.arange(TASKS, dtype=jnp.float32) / TASKS
    rising = 5.0 ** (position - 0.5)
    factor = jnp.exp(jax.random.uniform(noise_key, (BINS, TASKS), jnp.float32, -0.6931, 0.6931))
    return jnp.log(8.0 / (TASKS * BINS) * rising[None, :] * factor)


def place_ends(result, stream_key, low, high):
    place = [jax.random.randint(jax.random.fold_in(stream_key, axis), (), 0, length) for axis, length in enumerate(result.shape)]
    widest = result.shape.index(max(result.shape))
    neighbour = place[:widest] + [(place[widest] + 1) % result.shape[widest]] + place[widest + 1:]
    return result.at[tuple(place)].set(low).at[tuple(neighbour)].set(high)


def level_of(key, shape, pieces, smallest, top_value):
    factor_of = 1.0
    for dim, parts in pieces:
        draws = jax.random.uniform(jax.random.fold_in(jax.random.fold_in(key, 6), dim), (parts,), jnp.float32, smallest / len(pieces), top_value / len(pieces))
        factor_of = factor_of * jnp.repeat(jnp.exp(draws), shape[dim] // parts).reshape((-1,) + (1,) * (len(shape) - 1 - dim))
    return factor_of


def rank_table(count, skew):
    loads = [(1 << 20) // math.isqrt(rank ** skew) + 1 for rank in range(1, count + 1)]
    scale = 1 + sum(loads) // (1 << 30)
    return np.cumsum(np.array([max(1, weight // scale) for weight in loads]))


def ranked(rng, shape, count, slope):
    table = rank_table(count, slope)
    ticket = jax.random.randint(jax.random.fold_in(rng, 1), shape, 0, int(table[count - 1]))
    grade = jnp.searchsorted(jnp.asarray(table, jnp.int32), ticket, side="right")
    return jax.random.permutation(jax.random.fold_in(rng, 2), count)[grade].astype(jnp.int32)


def gaussian(own_key, dims, deviation, reach, split=(), kind=jnp.bfloat16):
    gain = level_of(own_key, dims, split, -0.22, 0.18) if split else 1.0
    values = jax.random.normal(own_key, dims, jnp.float32) * deviation * gain
    return jnp.minimum(jnp.maximum(values, -reach), reach).astype(kind)


def setup_inputs(seed: int = 0) -> dict:
    splits = jax.random.split(jax.random.key(seed), 9)
    queries = gaussian(splits[0], (TOKENS, D), 1.0, 6.0, ((0, 64), (1, 4)))
    keys = gaussian(splits[1], (TOKENS, D), 1.0, 6.0, ((0, 64), (1, 4)))
    values = gaussian(splits[2], (TOKENS, D), 1.0, 6.0, ((0, 64), (1, 4)))
    hazard_weight = gaussian(splits[3], (D, TASKS), D ** -0.5, 0.09375, ((1, 4),))
    log_base = draw_log_base(jax.random.fold_in(splits[8], 71), 0)
    time_bin = place_ends(jax.random.randint(splits[5], (TOKENS,), 0, BINS), jax.random.fold_in(splits[5], 1), 0, BINS - 1).astype(jnp.int32)
    observed = place_ends((jax.random.randint(splits[6], (TOKENS,), 0, 2) < 1).astype(jnp.int32), jax.random.fold_in(splits[6], 1), 0, 1)
    task_label = place_ends(ranked(splits[7], (TOKENS,), TASKS, 2), jax.random.fold_in(splits[7], 3), 0, TASKS - 1).astype(jnp.int32)
    return {"queries": queries, "keys": keys, "values": values, "hazard_weight": hazard_weight, "log_base": log_base, "time_bin": time_bin, "observed": observed, "task_label": task_label}


norm_eps = 1e-06
grad_scale = 64.0

def reference(queries, keys, values, hazard_weight, log_base, time_bin, observed, task_label):
    highest = lax.Precision.HIGHEST
    shape_four = (N_SEQ, TOK_DEV, HEADS, HEAD_DIM)
    query_wide = queries.astype(jnp.float32).reshape(shape_four)
    key_wide = keys.astype(jnp.float32).reshape(shape_four)
    value_wide = values.astype(jnp.float32).reshape(shape_four)
    causal = jnp.tril(jnp.ones((TOK_DEV, TOK_DEV), jnp.float32))
    empty_state = jnp.zeros((HEADS, HEAD_DIM, HEAD_DIM), jnp.float32)

    def forward_block(state_prefix, block_in):
        query_blk, key_blk, value_blk = block_in
        scores = jnp.einsum('thd,shd->hts', query_blk, key_blk, precision=highest) * causal
        raw_out = jnp.einsum('hts,she->the', scores, value_blk, precision=highest)
        raw_out = raw_out + jnp.einsum('thd,hde->the', query_blk, state_prefix, precision=highest)
        state_next = state_prefix + jnp.einsum('thd,the->hde', key_blk, value_blk, precision=highest)
        return (state_next, (raw_out, state_prefix))
    unused_state, (raw_out, prefixes) = lax.scan(forward_block, empty_state, (query_wide, key_wide, value_wide))
    root_mean = jnp.sqrt(lax.optimization_barrier(jnp.mean(raw_out * raw_out, axis=-1, keepdims=True)) + norm_eps)
    normed = raw_out / root_mean
    hidden = normed.astype(jnp.bfloat16).reshape(TOKENS, D)
    log_rate = jnp.dot(hidden, hazard_weight, preferred_element_type=jnp.float32)
    cum_base = jnp.cumsum(jnp.exp(log_base), axis=0)
    hazard = jnp.exp(log_rate) * cum_base[time_bin]
    event_flag = observed.astype(jnp.float32)
    picked = jnp.take_along_axis(log_rate, task_label[:, None], axis=1)[:, 0] + log_base[time_bin, task_label]
    event_loss = lax.optimization_barrier(jnp.sum(hazard, axis=1)) - event_flag * picked
    label_hit = (task_label[:, None] == jnp.arange(TASKS, dtype=jnp.int32)[None, :]).astype(jnp.float32)
    dlogit = (grad_scale * (hazard - event_flag[:, None] * label_hit)).astype(jnp.bfloat16)
    grad_hidden = jnp.dot(dlogit, hazard_weight.T, preferred_element_type=jnp.float32).reshape(shape_four)
    grad_raw = (grad_hidden - normed * lax.optimization_barrier(jnp.mean(normed * grad_hidden, axis=-1, keepdims=True))) / root_mean
    grad_out = lax.optimization_barrier(grad_raw.astype(jnp.bfloat16)).astype(jnp.float32)

    def backward_block(suffix, block_in):
        query_blk, key_blk, value_blk, grad_blk, prefix_blk = block_in
        scores = jnp.einsum('thd,shd->hts', query_blk, key_blk, precision=highest) * causal
        back_scores = jnp.einsum('the,she->hts', grad_blk, value_blk, precision=highest) * causal
        grad_query = jnp.einsum('hts,shd->thd', back_scores, key_blk, precision=highest)
        grad_query = grad_query + jnp.einsum('the,hde->thd', grad_blk, prefix_blk, precision=highest)
        grad_key = jnp.einsum('hts,thd->shd', back_scores, query_blk, precision=highest)
        grad_key = grad_key + jnp.einsum('she,hde->shd', value_blk, suffix, precision=highest)
        grad_value = jnp.einsum('hts,the->she', scores, grad_blk, precision=highest)
        grad_value = grad_value + jnp.einsum('shd,hde->she', key_blk, suffix, precision=highest)
        suffix_next = suffix + jnp.einsum('thd,the->hde', query_blk, grad_blk, precision=highest)
        return (suffix_next, (grad_query, grad_key, grad_value))
    unused_suffix, (grad_query, grad_key, grad_value) = lax.scan(backward_block, empty_state, (query_wide, key_wide, value_wide, grad_out, prefixes), reverse=True)
    grad_queries = grad_query.reshape(TOKENS, D).astype(jnp.bfloat16)
    grad_keys = grad_key.reshape(TOKENS, D).astype(jnp.bfloat16)
    grad_values = grad_value.reshape(TOKENS, D).astype(jnp.bfloat16)
    return (grad_queries, grad_keys, grad_values, event_loss)
```

```python
import jax
import jax.numpy as jnp
from jax import lax
from jax.sharding import PartitionSpec as P

HEAD_DIM = 128
BINS = 32


norm_eps = 1e-06
grad_scale = 64.0


def exclusive_scan(shard, axis, reverse=False):
    count = lax.axis_size(axis)
    inclusive = shard
    exclusive = jnp.zeros_like(shard)
    distance = 1
    while distance < count:
        if reverse:
            pairs = [(i, i - distance) for i in range(distance, count)]
        else:
            pairs = [(i, i + distance) for i in range(count - distance)]
        arrived = lax.ppermute(inclusive, axis, pairs)
        exclusive = exclusive + arrived
        inclusive = inclusive + arrived
        distance *= 2
    return exclusive


def body(queries, keys, values, hazard_weight, log_base, time_bin, observed, task_label):
    highest = lax.Precision.HIGHEST
    three_pass = lax.Precision.HIGH
    f32 = jnp.float32
    rows_here = queries.shape[0]
    width_here = queries.shape[1]
    heads_here = width_here // HEAD_DIM
    tasks_here = hazard_weight.shape[1]
    shape_three = (rows_here, heads_here, HEAD_DIM)
    query_rows = queries.reshape(shape_three)
    key_rows = keys.reshape(shape_three)
    value_rows = values.reshape(shape_three)
    causal = jnp.tril(jnp.ones((rows_here, rows_here), f32))
    local_state = jnp.einsum("thd,the->hde", key_rows, value_rows, preferred_element_type=f32)
    prefix = exclusive_scan(local_state, "seq")
    scores = jnp.einsum("thd,shd->hts", query_rows, key_rows, preferred_element_type=f32) * causal
    raw_out = jnp.einsum(
        "hts,she->the", scores, value_rows, precision=three_pass, preferred_element_type=f32
    )
    raw_out = raw_out + jnp.einsum(
        "thd,hde->the", query_rows, prefix, precision=three_pass, preferred_element_type=f32
    )
    root_mean = jnp.sqrt(jnp.mean(raw_out * raw_out, axis=-1, keepdims=True) + norm_eps)
    normed = raw_out / root_mean
    hidden = normed.astype(jnp.bfloat16).reshape(rows_here, width_here)
    log_rate = jnp.dot(
        lax.all_gather(hidden, "head", axis=1, tiled=True),
        hazard_weight,
        preferred_element_type=f32,
    )
    offset = lax.axis_index("head") * tasks_here
    cum_base = jnp.cumsum(jnp.exp(log_base), axis=0)
    bin_hot = (time_bin[:, None] == jnp.arange(BINS, dtype=jnp.int32)[None, :]).astype(f32)
    base_rows = jnp.dot(bin_hot, log_base, precision=highest)
    cum_rows = jnp.dot(bin_hot, cum_base, precision=highest)
    hazard = jnp.exp(log_rate) * cum_rows
    columns = offset + jnp.arange(tasks_here, dtype=jnp.int32)
    label_hit = (task_label[:, None] == columns[None, :]).astype(f32)
    event_flag = observed.astype(f32)
    partial_value = jnp.sum(hazard, axis=1) - event_flag * jnp.sum(
        label_hit * (log_rate + base_rows), axis=1
    )
    dlogit = (grad_scale * (hazard - event_flag[:, None] * label_hit)).astype(jnp.bfloat16)
    term_full = lax.dot_general(
        dlogit, hazard_weight, (((1,), (1,)), ((), ())), preferred_element_type=f32
    )
    grad_hidden = lax.psum_scatter(
        term_full.astype(jnp.bfloat16), "head", scatter_dimension=1, tiled=True
    ).astype(f32)
    event_loss = lax.psum(partial_value, "head")
    grad_norm_in = grad_hidden.reshape(shape_three)
    grad_raw = (
        grad_norm_in - normed * jnp.mean(normed * grad_norm_in, axis=-1, keepdims=True)
    ) / root_mean
    grad_out = grad_raw.astype(jnp.bfloat16)
    local_adjoint = jnp.einsum("thd,the->hde", query_rows, grad_out, preferred_element_type=f32)
    suffix = exclusive_scan(local_adjoint, "seq", reverse=True)
    back_scores = (
        jnp.einsum("the,she->hts", grad_out, value_rows, preferred_element_type=f32) * causal
    )
    grad_query = jnp.einsum(
        "hts,shd->thd", back_scores, key_rows, precision=three_pass, preferred_element_type=f32
    )
    grad_query = grad_query + jnp.einsum(
        "the,hde->thd", grad_out, prefix, precision=three_pass, preferred_element_type=f32
    )
    grad_key = jnp.einsum(
        "hts,thd->shd", back_scores, query_rows, precision=three_pass, preferred_element_type=f32
    )
    grad_key = grad_key + jnp.einsum(
        "she,hde->shd", value_rows, suffix, precision=three_pass, preferred_element_type=f32
    )
    grad_value = jnp.einsum(
        "hts,the->she", scores, grad_out, precision=three_pass, preferred_element_type=f32
    )
    grad_value = grad_value + jnp.einsum(
        "shd,hde->she", key_rows, suffix, precision=three_pass, preferred_element_type=f32
    )
    grad_queries = grad_query.reshape(rows_here, width_here).astype(jnp.bfloat16)
    grad_keys = grad_key.reshape(rows_here, width_here).astype(jnp.bfloat16)
    grad_values = grad_value.reshape(rows_here, width_here).astype(jnp.bfloat16)
    return (grad_queries, grad_keys, grad_values, event_loss)


def solution(mesh):
    placed = (
        P("seq", "head"),
        P("seq", "head"),
        P("seq", "head"),
        P(None, "head"),
        P(None, "head"),
        P("seq"),
        P("seq"),
        P("seq"),
    )
    return jax.shard_map(
        body,
        mesh=mesh,
        in_specs=placed,
        out_specs=(P("seq", "head"), P("seq", "head"), P("seq", "head"), P("seq")),
        check_vma=False,
    )
```

```python
import jax
import jax.numpy as jnp
from jax import lax
from jax.sharding import PartitionSpec as P

HEAD_DIM = 128
BINS = 32


norm_eps = 1e-06
grad_scale = 64.0


def exclusive_scan(shard, axis, reverse=False):
    count = lax.axis_size(axis)
    core = lax.axis_index(axis) % 2
    pair = [(i, i ^ 1) for i in range(count)]
    other = lax.ppermute(shard, axis, pair)
    keep_other = (core == 0) if reverse else (core == 1)
    within = jnp.where(keep_other, other, jnp.zeros_like(other))
    half = shard.shape[0] // 2
    inclusive = lax.dynamic_slice_in_dim(shard + other, core * half, half, 0)
    exclusive = jnp.zeros_like(inclusive)
    distance = 2
    while distance < count:
        if reverse:
            pairs = [(i, i - distance) for i in range(distance, count)]
        else:
            pairs = [(i, i + distance) for i in range(count - distance)]
        arrived = lax.ppermute(inclusive, axis, pairs)
        exclusive = exclusive + arrived
        inclusive = inclusive + arrived
        distance *= 2
    partner = lax.ppermute(exclusive, axis, pair)
    joined = jnp.where(
        core == 0,
        jnp.concatenate([exclusive, partner], axis=0),
        jnp.concatenate([partner, exclusive], axis=0),
    )
    return joined + within


def body(queries, keys, values, hazard_weight, log_base, time_bin, observed, task_label):
    highest = lax.Precision.HIGHEST
    three_pass = lax.Precision.HIGH
    f32 = jnp.float32
    rows_here = queries.shape[0]
    width_here = queries.shape[1]
    heads_here = width_here // HEAD_DIM
    tasks_here = hazard_weight.shape[1]
    shape_three = (rows_here, heads_here, HEAD_DIM)
    query_rows = queries.reshape(shape_three)
    key_rows = keys.reshape(shape_three)
    value_rows = values.reshape(shape_three)
    causal = jnp.tril(jnp.ones((rows_here, rows_here), f32))
    local_state = jnp.einsum("thd,the->hde", key_rows, value_rows, preferred_element_type=f32)
    prefix = exclusive_scan(local_state, "seq")
    scores = jnp.einsum("thd,shd->hts", query_rows, key_rows, preferred_element_type=f32) * causal
    raw_out = jnp.einsum(
        "hts,she->the", scores, value_rows, precision=three_pass, preferred_element_type=f32
    )
    raw_out = raw_out + jnp.einsum(
        "thd,hde->the", query_rows, prefix, precision=three_pass, preferred_element_type=f32
    )
    root_mean = jnp.sqrt(jnp.mean(raw_out * raw_out, axis=-1, keepdims=True) + norm_eps)
    normed = raw_out / root_mean
    hidden = normed.astype(jnp.bfloat16).reshape(rows_here, width_here)
    log_rate = jnp.dot(
        lax.all_gather(hidden, "head", axis=1, tiled=True),
        hazard_weight,
        preferred_element_type=f32,
    )
    offset = lax.axis_index("head") * tasks_here
    cum_base = jnp.cumsum(jnp.exp(log_base), axis=0)
    bin_hot = (time_bin[:, None] == jnp.arange(BINS, dtype=jnp.int32)[None, :]).astype(f32)
    base_rows = jnp.dot(bin_hot, log_base, precision=highest)
    cum_rows = jnp.dot(bin_hot, cum_base, precision=highest)
    hazard = jnp.exp(log_rate) * cum_rows
    columns = offset + jnp.arange(tasks_here, dtype=jnp.int32)
    label_hit = (task_label[:, None] == columns[None, :]).astype(f32)
    event_flag = observed.astype(f32)
    partial_value = jnp.sum(hazard, axis=1) - event_flag * jnp.sum(
        label_hit * (log_rate + base_rows), axis=1
    )
    dlogit = (grad_scale * (hazard - event_flag[:, None] * label_hit)).astype(jnp.bfloat16)
    term_full = lax.dot_general(
        dlogit, hazard_weight, (((1,), (1,)), ((), ())), preferred_element_type=f32
    )
    grad_hidden = lax.psum_scatter(
        term_full.astype(jnp.bfloat16), "head", scatter_dimension=1, tiled=True
    ).astype(f32)
    event_loss = lax.psum(partial_value, "head")
    grad_norm_in = grad_hidden.reshape(shape_three)
    grad_raw = (
        grad_norm_in - normed * jnp.mean(normed * grad_norm_in, axis=-1, keepdims=True)
    ) / root_mean
    grad_out = grad_raw.astype(jnp.bfloat16)
    local_adjoint = jnp.einsum("thd,the->hde", query_rows, grad_out, preferred_element_type=f32)
    suffix = exclusive_scan(local_adjoint, "seq", reverse=True)
    back_scores = (
        jnp.einsum("the,she->hts", grad_out, value_rows, preferred_element_type=f32) * causal
    )
    grad_query = jnp.einsum(
        "hts,shd->thd", back_scores, key_rows, precision=three_pass, preferred_element_type=f32
    )
    grad_query = grad_query + jnp.einsum(
        "the,hde->thd", grad_out, prefix, precision=three_pass, preferred_element_type=f32
    )
    grad_key = jnp.einsum(
        "hts,thd->shd", back_scores, query_rows, precision=three_pass, preferred_element_type=f32
    )
    grad_key = grad_key + jnp.einsum(
        "she,hde->shd", value_rows, suffix, precision=three_pass, preferred_element_type=f32
    )
    grad_value = jnp.einsum(
        "hts,the->she", scores, grad_out, precision=three_pass, preferred_element_type=f32
    )
    grad_value = grad_value + jnp.einsum(
        "shd,hde->she", key_rows, suffix, precision=three_pass, preferred_element_type=f32
    )
    grad_queries = grad_query.reshape(rows_here, width_here).astype(jnp.bfloat16)
    grad_keys = grad_key.reshape(rows_here, width_here).astype(jnp.bfloat16)
    grad_values = grad_value.reshape(rows_here, width_here).astype(jnp.bfloat16)
    return (grad_queries, grad_keys, grad_values, event_loss)


def solution(mesh):
    placed = (
        P("seq", "head"),
        P("seq", "head"),
        P("seq", "head"),
        P(None, "head"),
        P(None, "head"),
        P("seq"),
        P("seq"),
        P("seq"),
    )
    return jax.shard_map(
        body,
        mesh=mesh,
        in_specs=placed,
        out_specs=(P("seq", "head"), P("seq", "head"), P("seq", "head"), P("seq")),
        check_vma=False,
    )
```

```python
import jax
import jax.numpy as jnp
from jax import lax
from jax.sharding import PartitionSpec as P

HEAD_DIM = 128
BINS = 32


norm_eps = 1e-06
grad_scale = 64.0


def exclusive_scan(shard, axis, reverse=False):
    count = lax.axis_size(axis)
    core = lax.axis_index(axis) % 2
    pair = [(i, i ^ 1) for i in range(count)]
    other = lax.ppermute(shard, axis, pair)
    keep_other = (core == 0) if reverse else (core == 1)
    within = jnp.where(keep_other, other, jnp.zeros_like(other))
    half = shard.shape[0] // 2
    inclusive = lax.dynamic_slice_in_dim(shard + other, core * half, half, 0)
    exclusive = jnp.zeros_like(inclusive)
    distance = 2
    while distance < count:
        if reverse:
            pairs = [(i, i - distance) for i in range(distance, count)]
        else:
            pairs = [(i, i + distance) for i in range(count - distance)]
        arrived = lax.ppermute(inclusive, axis, pairs)
        exclusive = exclusive + arrived
        inclusive = inclusive + arrived
        distance *= 2
    partner = lax.ppermute(exclusive, axis, pair)
    joined = jnp.where(
        core == 0,
        jnp.concatenate([exclusive, partner], axis=0),
        jnp.concatenate([partner, exclusive], axis=0),
    )
    return joined + within


def body(queries, keys, values, hazard_weight, log_base, time_bin, observed, task_label):
    highest = lax.Precision.HIGHEST
    three_pass = lax.Precision.HIGH
    f32 = jnp.float32
    rows_here = queries.shape[0]
    width_here = queries.shape[1]
    heads_here = width_here // HEAD_DIM
    tasks_here = hazard_weight.shape[1]
    shape_three = (rows_here, heads_here, HEAD_DIM)
    query_rows = queries.reshape(shape_three)
    key_rows = keys.reshape(shape_three)
    value_rows = values.reshape(shape_three)
    causal = jnp.tril(jnp.ones((rows_here, rows_here), f32))
    local_state = jnp.einsum("thd,the->hde", key_rows, value_rows, preferred_element_type=f32)
    prefix = exclusive_scan(local_state, "seq")
    scores = jnp.einsum("thd,shd->hts", query_rows, key_rows, preferred_element_type=f32) * causal
    raw_out = jnp.einsum(
        "hts,she->the", scores, value_rows, precision=three_pass, preferred_element_type=f32
    )
    raw_out = raw_out + jnp.einsum(
        "thd,hde->the", query_rows, prefix, precision=three_pass, preferred_element_type=f32
    )
    root_mean = jnp.sqrt(jnp.mean(raw_out * raw_out, axis=-1, keepdims=True) + norm_eps)
    normed = raw_out / root_mean
    hidden = normed.astype(jnp.bfloat16).reshape(rows_here, width_here)
    head_count = lax.axis_size("head")
    head_index = lax.axis_index("head")

    def shifted(x, k):
        return lax.ppermute(x, "head", [(m, (m + k) % head_count) for m in range(head_count)])

    def weight_rows(owner):
        return lax.dynamic_slice_in_dim(hazard_weight, owner * width_here, width_here, 0)

    log_rate = jnp.dot(hidden, weight_rows(head_index), preferred_element_type=f32)
    for k in range(1, head_count):
        log_rate = log_rate + jnp.dot(
            shifted(hidden, k),
            weight_rows((head_index - k + head_count) % head_count),
            preferred_element_type=f32,
        )
    offset = head_index * tasks_here
    cum_base = jnp.cumsum(jnp.exp(log_base), axis=0)
    bin_hot = (time_bin[:, None] == jnp.arange(BINS, dtype=jnp.int32)[None, :]).astype(f32)
    base_rows = jnp.dot(bin_hot, log_base, precision=highest)
    cum_rows = jnp.dot(bin_hot, cum_base, precision=highest)
    hazard = jnp.exp(log_rate) * cum_rows
    columns = offset + jnp.arange(tasks_here, dtype=jnp.int32)
    label_hit = (task_label[:, None] == columns[None, :]).astype(f32)
    event_flag = observed.astype(f32)
    partial_value = jnp.sum(hazard, axis=1) - event_flag * jnp.sum(
        label_hit * (log_rate + base_rows), axis=1
    )
    dlogit = (grad_scale * (hazard - event_flag[:, None] * label_hit)).astype(jnp.bfloat16)
    def block_term(owner):
        return lax.dot_general(
            dlogit, weight_rows(owner), (((1,), (1,)), ((), ())), preferred_element_type=f32
        )

    grad_hidden = block_term(head_index)
    event_loss = partial_value
    for k in range(1, head_count):
        sent = block_term((head_index + k) % head_count).astype(jnp.bfloat16)
        grad_hidden = grad_hidden + shifted(sent, k).astype(f32)
        event_loss = event_loss + shifted(partial_value, k)
    grad_norm_in = grad_hidden.reshape(shape_three)
    grad_raw = (
        grad_norm_in - normed * jnp.mean(normed * grad_norm_in, axis=-1, keepdims=True)
    ) / root_mean
    grad_out = grad_raw.astype(jnp.bfloat16)
    local_adjoint = jnp.einsum("thd,the->hde", query_rows, grad_out, preferred_element_type=f32)
    suffix = exclusive_scan(local_adjoint, "seq", reverse=True)
    back_scores = (
        jnp.einsum("the,she->hts", grad_out, value_rows, preferred_element_type=f32) * causal
    )
    grad_query = jnp.einsum(
        "hts,shd->thd", back_scores, key_rows, precision=three_pass, preferred_element_type=f32
    )
    grad_query = grad_query + jnp.einsum(
        "the,hde->thd", grad_out, prefix, precision=three_pass, preferred_element_type=f32
    )
    grad_key = jnp.einsum(
        "hts,thd->shd", back_scores, query_rows, precision=three_pass, preferred_element_type=f32
    )
    grad_key = grad_key + jnp.einsum(
        "she,hde->shd", value_rows, suffix, precision=three_pass, preferred_element_type=f32
    )
    grad_value = jnp.einsum(
        "hts,the->she", scores, grad_out, precision=three_pass, preferred_element_type=f32
    )
    grad_value = grad_value + jnp.einsum(
        "shd,hde->she", key_rows, suffix, precision=three_pass, preferred_element_type=f32
    )
    grad_queries = grad_query.reshape(rows_here, width_here).astype(jnp.bfloat16)
    grad_keys = grad_key.reshape(rows_here, width_here).astype(jnp.bfloat16)
    grad_values = grad_value.reshape(rows_here, width_here).astype(jnp.bfloat16)
    return (grad_queries, grad_keys, grad_values, event_loss)


def solution(mesh):
    placed = (
        P("seq", "head"),
        P("seq", "head"),
        P("seq", "head"),
        P(None, "head"),
        P(None, "head"),
        P("seq"),
        P("seq"),
        P("seq"),
    )
    return jax.shard_map(
        body,
        mesh=mesh,
        in_specs=placed,
        out_specs=(P("seq", "head"), P("seq", "head"), P("seq", "head"), P("seq")),
        check_vma=False,
    )
```

```python
import functools

import jax
import jax.numpy as jnp
from jax import lax
from jax.experimental import pallas as pl
from jax.experimental.pallas import tpu as pltpu
from jax.sharding import PartitionSpec as P

HEAD_DIM = 128
BINS = 32
MESH = pl.DeviceIdType.MESH


norm_eps = 1e-06
grad_scale = 64.0


def scan_kernel(reverse, count, state_ref, out_ref, other, inclusive, arrived, exclusive, partner,
                send_sems, recv_sems):
    me = lax.axis_index("seq")
    head = lax.axis_index("head")
    core = me % 2
    mate = me + 1 - 2 * core
    half = exclusive.shape[0]
    distances = []
    distance = 2
    while distance < count:
        distances.append(distance)
        distance *= 2
    step = -1 if reverse else 1
    targets = [me + step * d for d in distances]
    sources = [me - step * d for d in distances]
    sends = [(t >= 0) & (t < count) for t in targets]
    receives = [(s >= 0) & (s < count) for s in sources]

    barrier = pltpu.get_barrier_semaphore()
    pl.semaphore_signal(barrier, 1, device_id=(mate, head), device_id_type=MESH)
    expected = jnp.int32(1)
    for target, source, send, receive in zip(targets, sources, sends, receives):
        @pl.when(send)
        def _():
            pl.semaphore_signal(barrier, 1, device_id=(target, head), device_id_type=MESH)

        @pl.when(receive)
        def _():
            pl.semaphore_signal(barrier, 1, device_id=(source, head), device_id_type=MESH)

        expected = expected + send.astype(jnp.int32) + receive.astype(jnp.int32)
    pl.semaphore_wait(barrier, expected)

    swap = pltpu.make_async_remote_copy(
        state_ref, other, send_sems.at[0], recv_sems.at[0], device_id=(mate, head), device_id_type=MESH
    )
    swap.start()
    swap.wait()
    mine = pl.ds(core * half, half)
    inclusive[0] = state_ref[mine] + other[mine]
    exclusive[...] = jnp.zeros_like(exclusive)
    copies = []
    for r, (target, send, receive) in enumerate(zip(targets, sends, receives)):
        copy = pltpu.make_async_remote_copy(
            inclusive.at[r], arrived.at[r], send_sems.at[r + 1], recv_sems.at[r + 1],
            device_id=(target, head), device_id_type=MESH,
        )
        copies.append(copy)

        @pl.when(send)
        def _():
            copy.start()

        @pl.when(receive)
        def _():
            copy.wait_recv()
            got = arrived[r]
            inclusive[r + 1] = inclusive[r] + got
            exclusive[...] = exclusive[...] + got

        @pl.when(jnp.logical_not(receive))
        def _():
            inclusive[r + 1] = inclusive[r]

    last = len(distances) + 1
    back = pltpu.make_async_remote_copy(
        exclusive, partner, send_sems.at[last], recv_sems.at[last], device_id=(mate, head), device_id_type=MESH
    )
    back.start()
    for copy, send in zip(copies, sends):
        @pl.when(send)
        def _():
            copy.wait_send()
    back.wait()
    theirs = pl.ds((1 - core) * half, half)
    take_other = (core == 0) if reverse else (core == 1)

    @pl.when(take_other)
    def _():
        out_ref[mine] = exclusive[...] + other[mine]
        out_ref[theirs] = partner[...] + other[theirs]

    @pl.when(jnp.logical_not(take_other))
    def _():
        out_ref[mine] = exclusive[...]
        out_ref[theirs] = partner[...]


def exclusive_scan(shard, axis, reverse=False):
    count = lax.axis_size(axis)
    heads, rows, cols = shard.shape
    half = heads // 2
    rounds = max(count.bit_length() - 2, 0)
    return pl.pallas_call(
        functools.partial(scan_kernel, reverse, count),
        out_shape=jax.ShapeDtypeStruct(shard.shape, shard.dtype),
        in_specs=[pl.BlockSpec(memory_space=pltpu.VMEM)],
        out_specs=pl.BlockSpec(memory_space=pltpu.VMEM),
        scratch_shapes=[
            pltpu.VMEM((heads, rows, cols), shard.dtype),
            pltpu.VMEM((rounds + 1, half, rows, cols), shard.dtype),
            pltpu.VMEM((max(rounds, 1), half, rows, cols), shard.dtype),
            pltpu.VMEM((half, rows, cols), shard.dtype),
            pltpu.VMEM((half, rows, cols), shard.dtype),
            pltpu.SemaphoreType.DMA((rounds + 2,)),
            pltpu.SemaphoreType.DMA((rounds + 2,)),
        ],
        compiler_params=pltpu.CompilerParams(collective_id=1 if reverse else 0, has_side_effects=True),
    )(shard)


def body(queries, keys, values, hazard_weight, log_base, time_bin, observed, task_label):
    highest = lax.Precision.HIGHEST
    three_pass = lax.Precision.HIGH
    f32 = jnp.float32
    rows_here = queries.shape[0]
    width_here = queries.shape[1]
    heads_here = width_here // HEAD_DIM
    tasks_here = hazard_weight.shape[1]
    shape_three = (rows_here, heads_here, HEAD_DIM)
    query_rows = queries.reshape(shape_three)
    key_rows = keys.reshape(shape_three)
    value_rows = values.reshape(shape_three)
    causal = jnp.tril(jnp.ones((rows_here, rows_here), f32))
    local_state = jnp.einsum("thd,the->hde", key_rows, value_rows, preferred_element_type=f32)
    prefix = exclusive_scan(local_state, "seq")
    scores = jnp.einsum("thd,shd->hts", query_rows, key_rows, preferred_element_type=f32) * causal
    raw_out = jnp.einsum(
        "hts,she->the", scores, value_rows, precision=three_pass, preferred_element_type=f32
    )
    raw_out = raw_out + jnp.einsum(
        "thd,hde->the", query_rows, prefix, precision=three_pass, preferred_element_type=f32
    )
    root_mean = jnp.sqrt(jnp.mean(raw_out * raw_out, axis=-1, keepdims=True) + norm_eps)
    normed = raw_out / root_mean
    hidden = normed.astype(jnp.bfloat16).reshape(rows_here, width_here)
    head_count = lax.axis_size("head")
    head_index = lax.axis_index("head")

    def shifted(x, k):
        return lax.ppermute(x, "head", [(m, (m + k) % head_count) for m in range(head_count)])

    def weight_rows(owner):
        return lax.dynamic_slice_in_dim(hazard_weight, owner * width_here, width_here, 0)

    log_rate = jnp.dot(hidden, weight_rows(head_index), preferred_element_type=f32)
    for k in range(1, head_count):
        log_rate = log_rate + jnp.dot(
            shifted(hidden, k),
            weight_rows((head_index - k + head_count) % head_count),
            preferred_element_type=f32,
        )
    offset = head_index * tasks_here
    cum_base = jnp.cumsum(jnp.exp(log_base), axis=0)
    bin_hot = (time_bin[:, None] == jnp.arange(BINS, dtype=jnp.int32)[None, :]).astype(f32)
    base_rows = jnp.dot(bin_hot, log_base, precision=highest)
    cum_rows = jnp.dot(bin_hot, cum_base, precision=highest)
    hazard = jnp.exp(log_rate) * cum_rows
    columns = offset + jnp.arange(tasks_here, dtype=jnp.int32)
    label_hit = (task_label[:, None] == columns[None, :]).astype(f32)
    event_flag = observed.astype(f32)
    partial_value = jnp.sum(hazard, axis=1) - event_flag * jnp.sum(
        label_hit * (log_rate + base_rows), axis=1
    )
    dlogit = (grad_scale * (hazard - event_flag[:, None] * label_hit)).astype(jnp.bfloat16)
    def block_term(owner):
        return lax.dot_general(
            dlogit, weight_rows(owner), (((1,), (1,)), ((), ())), preferred_element_type=f32
        )

    grad_hidden = block_term(head_index)
    event_loss = partial_value
    for k in range(1, head_count):
        sent = block_term((head_index + k) % head_count).astype(jnp.bfloat16)
        grad_hidden = grad_hidden + shifted(sent, k).astype(f32)
        event_loss = event_loss + shifted(partial_value, k)
    grad_norm_in = grad_hidden.reshape(shape_three)
    grad_raw = (
        grad_norm_in - normed * jnp.mean(normed * grad_norm_in, axis=-1, keepdims=True)
    ) / root_mean
    grad_out = grad_raw.astype(jnp.bfloat16)
    local_adjoint = jnp.einsum("thd,the->hde", query_rows, grad_out, preferred_element_type=f32)
    suffix = exclusive_scan(local_adjoint, "seq", reverse=True)
    back_scores = (
        jnp.einsum("the,she->hts", grad_out, value_rows, preferred_element_type=f32) * causal
    )
    grad_query = jnp.einsum(
        "hts,shd->thd", back_scores, key_rows, precision=three_pass, preferred_element_type=f32
    )
    grad_query = grad_query + jnp.einsum(
        "the,hde->thd", grad_out, prefix, precision=three_pass, preferred_element_type=f32
    )
    grad_key = jnp.einsum(
        "hts,thd->shd", back_scores, query_rows, precision=three_pass, preferred_element_type=f32
    )
    grad_key = grad_key + jnp.einsum(
        "she,hde->shd", value_rows, suffix, precision=three_pass, preferred_element_type=f32
    )
    grad_value = jnp.einsum(
        "hts,the->she", scores, grad_out, precision=three_pass, preferred_element_type=f32
    )
    grad_value = grad_value + jnp.einsum(
        "shd,hde->she", key_rows, suffix, precision=three_pass, preferred_element_type=f32
    )
    grad_queries = grad_query.reshape(rows_here, width_here).astype(jnp.bfloat16)
    grad_keys = grad_key.reshape(rows_here, width_here).astype(jnp.bfloat16)
    grad_values = grad_value.reshape(rows_here, width_here).astype(jnp.bfloat16)
    return (grad_queries, grad_keys, grad_values, event_loss)


def solution(mesh):
    placed = (
        P("seq", "head"),
        P("seq", "head"),
        P("seq", "head"),
        P(None, "head"),
        P(None, "head"),
        P("seq"),
        P("seq"),
        P("seq"),
    )
    return jax.shard_map(
        body,
        mesh=mesh,
        in_specs=placed,
        out_specs=(P("seq", "head"), P("seq", "head"), P("seq", "head"), P("seq")),
        check_vma=False,
    )
```

```python
import functools

import jax
import jax.numpy as jnp
from jax import lax
from jax.experimental import pallas as pl
from jax.experimental.pallas import tpu as pltpu
from jax.sharding import PartitionSpec as P

HEAD_DIM = 128
BINS = 32
MESH = pl.DeviceIdType.MESH


norm_eps = 1e-06
grad_scale = 64.0


def scan_kernel(reverse, count, state_ref, out_ref, other, running, exclusive, outgoing, arrived, handed, partner,
                send_sems, recv_sems):
    me = lax.axis_index("seq")
    head = lax.axis_index("head")
    core = me % 2
    mate = me + 1 - 2 * core
    half = exclusive.shape[0]
    wire = outgoing.dtype
    distances = []
    distance = 2
    while distance < count:
        distances.append(distance)
        distance *= 2
    step = -1 if reverse else 1
    targets = [me + step * d for d in distances]
    sources = [me - step * d for d in distances]
    sends = [(t >= 0) & (t < count) for t in targets]
    receives = [(s >= 0) & (s < count) for s in sources]

    barrier = pltpu.get_barrier_semaphore()
    pl.semaphore_signal(barrier, 1, device_id=(mate, head), device_id_type=MESH)
    expected = jnp.int32(1)
    for target, source, send, receive in zip(targets, sources, sends, receives):
        @pl.when(send)
        def _():
            pl.semaphore_signal(barrier, 1, device_id=(target, head), device_id_type=MESH)

        @pl.when(receive)
        def _():
            pl.semaphore_signal(barrier, 1, device_id=(source, head), device_id_type=MESH)

        expected = expected + send.astype(jnp.int32) + receive.astype(jnp.int32)
    pl.semaphore_wait(barrier, expected)

    swap = pltpu.make_async_remote_copy(
        state_ref, other, send_sems.at[0], recv_sems.at[0], device_id=(mate, head), device_id_type=MESH
    )
    swap.start()
    swap.wait()
    mine = pl.ds(core * half, half)
    running[...] = state_ref[mine] + other[mine]
    exclusive[...] = jnp.zeros_like(exclusive)
    copies = []
    for r, (target, send, receive) in enumerate(zip(targets, sends, receives)):
        outgoing[r] = running[...].astype(wire)
        copy = pltpu.make_async_remote_copy(
            outgoing.at[r], arrived.at[r], send_sems.at[r + 1], recv_sems.at[r + 1],
            device_id=(target, head), device_id_type=MESH,
        )
        copies.append(copy)

        @pl.when(send)
        def _():
            copy.start()

        @pl.when(receive)
        def _():
            copy.wait_recv()
            got = arrived[r].astype(running.dtype)
            running[...] = running[...] + got
            exclusive[...] = exclusive[...] + got

    last = len(distances) + 1
    handed[...] = exclusive[...].astype(wire)
    back = pltpu.make_async_remote_copy(
        handed, partner, send_sems.at[last], recv_sems.at[last], device_id=(mate, head), device_id_type=MESH
    )
    back.start()
    for copy, send in zip(copies, sends):
        @pl.when(send)
        def _():
            copy.wait_send()
    back.wait()
    theirs = pl.ds((1 - core) * half, half)
    take_other = (core == 0) if reverse else (core == 1)

    @pl.when(take_other)
    def _():
        out_ref[mine] = exclusive[...] + other[mine]
        out_ref[theirs] = partner[...].astype(out_ref.dtype) + other[theirs]

    @pl.when(jnp.logical_not(take_other))
    def _():
        out_ref[mine] = exclusive[...]
        out_ref[theirs] = partner[...].astype(out_ref.dtype)


def exclusive_scan(shard, axis, reverse=False, wire=jnp.float32):
    count = lax.axis_size(axis)
    heads, rows, cols = shard.shape
    half = heads // 2
    rounds = max(count.bit_length() - 2, 1)
    block = (half, rows, cols)
    return pl.pallas_call(
        functools.partial(scan_kernel, reverse, count),
        out_shape=jax.ShapeDtypeStruct(shard.shape, shard.dtype),
        in_specs=[pl.BlockSpec(memory_space=pltpu.VMEM)],
        out_specs=pl.BlockSpec(memory_space=pltpu.VMEM),
        scratch_shapes=[
            pltpu.VMEM((heads, rows, cols), shard.dtype),
            pltpu.VMEM(block, shard.dtype),
            pltpu.VMEM(block, shard.dtype),
            pltpu.VMEM((rounds,) + block, wire),
            pltpu.VMEM((rounds,) + block, wire),
            pltpu.VMEM(block, wire),
            pltpu.VMEM(block, wire),
            pltpu.SemaphoreType.DMA((rounds + 2,)),
            pltpu.SemaphoreType.DMA((rounds + 2,)),
        ],
        compiler_params=pltpu.CompilerParams(collective_id=1 if reverse else 0, has_side_effects=True),
    )(shard)


def body(queries, keys, values, hazard_weight, log_base, time_bin, observed, task_label):
    highest = lax.Precision.HIGHEST
    three_pass = lax.Precision.HIGH
    f32 = jnp.float32
    rows_here = queries.shape[0]
    width_here = queries.shape[1]
    heads_here = width_here // HEAD_DIM
    tasks_here = hazard_weight.shape[1]
    shape_three = (rows_here, heads_here, HEAD_DIM)
    query_rows = queries.reshape(shape_three)
    key_rows = keys.reshape(shape_three)
    value_rows = values.reshape(shape_three)
    causal = jnp.tril(jnp.ones((rows_here, rows_here), f32))
    local_state = jnp.einsum("thd,the->hde", key_rows, value_rows, preferred_element_type=f32)
    prefix = exclusive_scan(local_state, "seq")
    scores = jnp.einsum("thd,shd->hts", query_rows, key_rows, preferred_element_type=f32) * causal
    raw_out = jnp.einsum(
        "hts,she->the", scores, value_rows, precision=three_pass, preferred_element_type=f32
    )
    raw_out = raw_out + jnp.einsum(
        "thd,hde->the", query_rows, prefix, precision=three_pass, preferred_element_type=f32
    )
    root_mean = jnp.sqrt(jnp.mean(raw_out * raw_out, axis=-1, keepdims=True) + norm_eps)
    normed = raw_out / root_mean
    hidden = normed.astype(jnp.bfloat16).reshape(rows_here, width_here)
    head_count = lax.axis_size("head")
    head_index = lax.axis_index("head")

    def shifted(x, k):
        return lax.ppermute(x, "head", [(m, (m + k) % head_count) for m in range(head_count)])

    def weight_rows(owner):
        return lax.dynamic_slice_in_dim(hazard_weight, owner * width_here, width_here, 0)

    log_rate = jnp.dot(hidden, weight_rows(head_index), preferred_element_type=f32)
    for k in range(1, head_count):
        log_rate = log_rate + jnp.dot(
            shifted(hidden, k),
            weight_rows((head_index - k + head_count) % head_count),
            preferred_element_type=f32,
        )
    offset = head_index * tasks_here
    cum_base = jnp.cumsum(jnp.exp(log_base), axis=0)
    bin_hot = (time_bin[:, None] == jnp.arange(BINS, dtype=jnp.int32)[None, :]).astype(f32)
    base_rows = jnp.dot(bin_hot, log_base, precision=highest)
    cum_rows = jnp.dot(bin_hot, cum_base, precision=highest)
    hazard = jnp.exp(log_rate) * cum_rows
    columns = offset + jnp.arange(tasks_here, dtype=jnp.int32)
    label_hit = (task_label[:, None] == columns[None, :]).astype(f32)
    event_flag = observed.astype(f32)
    partial_value = jnp.sum(hazard, axis=1) - event_flag * jnp.sum(
        label_hit * (log_rate + base_rows), axis=1
    )
    dlogit = (grad_scale * (hazard - event_flag[:, None] * label_hit)).astype(jnp.bfloat16)
    def block_term(owner):
        return lax.dot_general(
            dlogit, weight_rows(owner), (((1,), (1,)), ((), ())), preferred_element_type=f32
        )

    grad_hidden = block_term(head_index)
    event_loss = partial_value
    for k in range(1, head_count):
        sent = block_term((head_index + k) % head_count).astype(jnp.bfloat16)
        grad_hidden = grad_hidden + shifted(sent, k).astype(f32)
        event_loss = event_loss + shifted(partial_value, k)
    grad_norm_in = grad_hidden.reshape(shape_three)
    grad_raw = (
        grad_norm_in - normed * jnp.mean(normed * grad_norm_in, axis=-1, keepdims=True)
    ) / root_mean
    grad_out = grad_raw.astype(jnp.bfloat16)
    local_adjoint = jnp.einsum("thd,the->hde", query_rows, grad_out, preferred_element_type=f32)
    suffix = exclusive_scan(local_adjoint, "seq", reverse=True, wire=jnp.bfloat16)
    back_scores = (
        jnp.einsum("the,she->hts", grad_out, value_rows, preferred_element_type=f32) * causal
    )
    grad_query = jnp.einsum(
        "hts,shd->thd", back_scores, key_rows, precision=three_pass, preferred_element_type=f32
    )
    grad_query = grad_query + jnp.einsum(
        "the,hde->thd", grad_out, prefix, precision=three_pass, preferred_element_type=f32
    )
    grad_key = jnp.einsum(
        "hts,thd->shd", back_scores, query_rows, precision=three_pass, preferred_element_type=f32
    )
    grad_key = grad_key + jnp.einsum(
        "she,hde->shd", value_rows, suffix, precision=three_pass, preferred_element_type=f32
    )
    grad_value = jnp.einsum(
        "hts,the->she", scores, grad_out, precision=three_pass, preferred_element_type=f32
    )
    grad_value = grad_value + jnp.einsum(
        "shd,hde->she", key_rows, suffix, precision=three_pass, preferred_element_type=f32
    )
    grad_queries = grad_query.reshape(rows_here, width_here).astype(jnp.bfloat16)
    grad_keys = grad_key.reshape(rows_here, width_here).astype(jnp.bfloat16)
    grad_values = grad_value.reshape(rows_here, width_here).astype(jnp.bfloat16)
    return (grad_queries, grad_keys, grad_values, event_loss)


def solution(mesh):
    placed = (
        P("seq", "head"),
        P("seq", "head"),
        P("seq", "head"),
        P(None, "head"),
        P(None, "head"),
        P("seq"),
        P("seq"),
        P("seq"),
    )
    return jax.shard_map(
        body,
        mesh=mesh,
        in_specs=placed,
        out_specs=(P("seq", "head"), P("seq", "head"), P("seq", "head"), P("seq")),
        check_vma=False,
    )
```

```python
import functools

import jax
import jax.numpy as jnp
from jax import lax
from jax.experimental import pallas as pl
from jax.experimental.pallas import tpu as pltpu
from jax.sharding import PartitionSpec as P

HEAD_DIM = 128
BINS = 32
MESH = pl.DeviceIdType.MESH


norm_eps = 1e-06
grad_scale = 64.0


def scan_kernel(reverse, count, state_ref, out_ref, other, running, exclusive, outgoing, arrived, handed, partner,
                send_sems, recv_sems):
    me = lax.axis_index("seq")
    head = lax.axis_index("head")
    core = me % 2
    mate = me + 1 - 2 * core
    half = exclusive.shape[0]
    wire = outgoing.dtype
    distances = []
    distance = 2
    while distance < count:
        distances.append(distance)
        distance *= 2
    step = -1 if reverse else 1
    targets = [me + step * d for d in distances]
    sources = [me - step * d for d in distances]
    sends = [(t >= 0) & (t < count) for t in targets]
    receives = [(s >= 0) & (s < count) for s in sources]

    barrier = pltpu.get_barrier_semaphore()
    pl.semaphore_signal(barrier, 1, device_id=(mate, head), device_id_type=MESH)
    expected = jnp.int32(1)
    for target, source, send, receive in zip(targets, sources, sends, receives):
        @pl.when(send)
        def _():
            pl.semaphore_signal(barrier, 1, device_id=(target, head), device_id_type=MESH)

        @pl.when(receive)
        def _():
            pl.semaphore_signal(barrier, 1, device_id=(source, head), device_id_type=MESH)

        expected = expected + send.astype(jnp.int32) + receive.astype(jnp.int32)
    pl.semaphore_wait(barrier, expected)

    swap = pltpu.make_async_remote_copy(
        state_ref, other, send_sems.at[0], recv_sems.at[0], device_id=(mate, head), device_id_type=MESH
    )
    swap.start()
    swap.wait()
    mine = pl.ds(core * half, half)
    running[...] = state_ref[mine] + other[mine]
    exclusive[...] = jnp.zeros_like(exclusive)
    copies = []
    for r, (target, send, receive) in enumerate(zip(targets, sends, receives)):
        outgoing[r] = running[...].astype(wire)
        copy = pltpu.make_async_remote_copy(
            outgoing.at[r], arrived.at[r], send_sems.at[r + 1], recv_sems.at[r + 1],
            device_id=(target, head), device_id_type=MESH,
        )
        copies.append(copy)

        @pl.when(send)
        def _():
            copy.start()

        @pl.when(receive)
        def _():
            copy.wait_recv()
            got = arrived[r].astype(running.dtype)
            running[...] = running[...] + got
            exclusive[...] = exclusive[...] + got

    last = len(distances) + 1
    handed[...] = exclusive[...].astype(wire)
    back = pltpu.make_async_remote_copy(
        handed, partner, send_sems.at[last], recv_sems.at[last], device_id=(mate, head), device_id_type=MESH
    )
    back.start()
    for copy, send in zip(copies, sends):
        @pl.when(send)
        def _():
            copy.wait_send()
    back.wait()
    theirs = pl.ds((1 - core) * half, half)
    take_other = (core == 0) if reverse else (core == 1)

    @pl.when(take_other)
    def _():
        out_ref[mine] = exclusive[...] + other[mine]
        out_ref[theirs] = partner[...].astype(out_ref.dtype) + other[theirs]

    @pl.when(jnp.logical_not(take_other))
    def _():
        out_ref[mine] = exclusive[...]
        out_ref[theirs] = partner[...].astype(out_ref.dtype)


def exclusive_scan(shard, axis, reverse=False, wire=jnp.float32):
    count = lax.axis_size(axis)
    heads, rows, cols = shard.shape
    half = heads // 2
    rounds = max(count.bit_length() - 2, 1)
    block = (half, rows, cols)
    return pl.pallas_call(
        functools.partial(scan_kernel, reverse, count),
        out_shape=jax.ShapeDtypeStruct(shard.shape, shard.dtype),
        in_specs=[pl.BlockSpec(memory_space=pltpu.VMEM)],
        out_specs=pl.BlockSpec(memory_space=pltpu.VMEM),
        scratch_shapes=[
            pltpu.VMEM((heads, rows, cols), shard.dtype),
            pltpu.VMEM(block, shard.dtype),
            pltpu.VMEM(block, shard.dtype),
            pltpu.VMEM((rounds,) + block, wire),
            pltpu.VMEM((rounds,) + block, wire),
            pltpu.VMEM(block, wire),
            pltpu.VMEM(block, wire),
            pltpu.SemaphoreType.DMA((rounds + 2,)),
            pltpu.SemaphoreType.DMA((rounds + 2,)),
        ],
        compiler_params=pltpu.CompilerParams(collective_id=1 if reverse else 0, has_side_effects=True),
    )(shard)


def body(queries, keys, values, hazard_weight, log_base, time_bin, observed, task_label):
    highest = lax.Precision.HIGHEST
    three_pass = lax.Precision.HIGH
    f32 = jnp.float32
    rows_here = queries.shape[0]
    width_here = queries.shape[1]
    heads_here = width_here // HEAD_DIM
    tasks_here = hazard_weight.shape[1]
    shape_three = (rows_here, heads_here, HEAD_DIM)
    query_rows = queries.reshape(shape_three)
    key_rows = keys.reshape(shape_three)
    value_rows = values.reshape(shape_three)
    causal = jnp.tril(jnp.ones((rows_here, rows_here), f32))
    local_state = jnp.einsum("thd,the->hde", key_rows, value_rows, preferred_element_type=f32)
    prefix = exclusive_scan(local_state, "seq", wire=jnp.bfloat16)
    scores = jnp.einsum("thd,shd->hts", query_rows, key_rows, preferred_element_type=f32) * causal
    raw_out = jnp.einsum(
        "hts,she->the", scores, value_rows, precision=three_pass, preferred_element_type=f32
    )
    raw_out = raw_out + jnp.einsum(
        "thd,hde->the", query_rows, prefix, precision=three_pass, preferred_element_type=f32
    )
    root_mean = jnp.sqrt(jnp.mean(raw_out * raw_out, axis=-1, keepdims=True) + norm_eps)
    normed = raw_out / root_mean
    hidden = normed.astype(jnp.bfloat16).reshape(rows_here, width_here)
    head_count = lax.axis_size("head")
    head_index = lax.axis_index("head")

    def shifted(x, k):
        return lax.ppermute(x, "head", [(m, (m + k) % head_count) for m in range(head_count)])

    def weight_rows(owner):
        return lax.dynamic_slice_in_dim(hazard_weight, owner * width_here, width_here, 0)

    log_rate = jnp.dot(hidden, weight_rows(head_index), preferred_element_type=f32)
    for k in range(1, head_count):
        log_rate = log_rate + jnp.dot(
            shifted(hidden, k),
            weight_rows((head_index - k + head_count) % head_count),
            preferred_element_type=f32,
        )
    offset = head_index * tasks_here
    cum_base = jnp.cumsum(jnp.exp(log_base), axis=0)
    bin_hot = (time_bin[:, None] == jnp.arange(BINS, dtype=jnp.int32)[None, :]).astype(f32)
    base_rows = jnp.dot(bin_hot, log_base, precision=highest)
    cum_rows = jnp.dot(bin_hot, cum_base, precision=highest)
    hazard = jnp.exp(log_rate) * cum_rows
    columns = offset + jnp.arange(tasks_here, dtype=jnp.int32)
    label_hit = (task_label[:, None] == columns[None, :]).astype(f32)
    event_flag = observed.astype(f32)
    partial_value = jnp.sum(hazard, axis=1) - event_flag * jnp.sum(
        label_hit * (log_rate + base_rows), axis=1
    )
    dlogit = (grad_scale * (hazard - event_flag[:, None] * label_hit)).astype(jnp.bfloat16)
    def block_term(owner):
        return lax.dot_general(
            dlogit, weight_rows(owner), (((1,), (1,)), ((), ())), preferred_element_type=f32
        )

    grad_hidden = block_term(head_index)
    event_loss = partial_value
    for k in range(1, head_count):
        sent = block_term((head_index + k) % head_count).astype(jnp.bfloat16)
        grad_hidden = grad_hidden + shifted(sent, k).astype(f32)
        event_loss = event_loss + shifted(partial_value, k)
    grad_norm_in = grad_hidden.reshape(shape_three)
    grad_raw = (
        grad_norm_in - normed * jnp.mean(normed * grad_norm_in, axis=-1, keepdims=True)
    ) / root_mean
    grad_out = grad_raw.astype(jnp.bfloat16)
    local_adjoint = jnp.einsum("thd,the->hde", query_rows, grad_out, preferred_element_type=f32)
    suffix = exclusive_scan(local_adjoint, "seq", reverse=True, wire=jnp.bfloat16)
    back_scores = (
        jnp.einsum("the,she->hts", grad_out, value_rows, preferred_element_type=f32) * causal
    )
    grad_query = jnp.einsum(
        "hts,shd->thd", back_scores, key_rows, precision=three_pass, preferred_element_type=f32
    )
    grad_query = grad_query + jnp.einsum(
        "the,hde->thd", grad_out, prefix, precision=three_pass, preferred_element_type=f32
    )
    grad_key = jnp.einsum(
        "hts,thd->shd", back_scores, query_rows, precision=three_pass, preferred_element_type=f32
    )
    grad_key = grad_key + jnp.einsum(
        "she,hde->shd", value_rows, suffix, precision=three_pass, preferred_element_type=f32
    )
    grad_value = jnp.einsum(
        "hts,the->she", scores, grad_out, precision=three_pass, preferred_element_type=f32
    )
    grad_value = grad_value + jnp.einsum(
        "shd,hde->she", key_rows, suffix, precision=three_pass, preferred_element_type=f32
    )
    grad_queries = grad_query.reshape(rows_here, width_here).astype(jnp.bfloat16)
    grad_keys = grad_key.reshape(rows_here, width_here).astype(jnp.bfloat16)
    grad_values = grad_value.reshape(rows_here, width_here).astype(jnp.bfloat16)
    return (grad_queries, grad_keys, grad_values, event_loss)


def solution(mesh):
    placed = (
        P("seq", "head"),
        P("seq", "head"),
        P("seq", "head"),
        P(None, "head"),
        P(None, "head"),
        P("seq"),
        P("seq"),
        P("seq"),
    )
    return jax.shard_map(
        body,
        mesh=mesh,
        in_specs=placed,
        out_specs=(P("seq", "head"), P("seq", "head"), P("seq", "head"), P("seq")),
        check_vma=False,
    )
```

```python
import functools

import jax
import jax.numpy as jnp
from jax import lax
from jax.experimental import pallas as pl
from jax.experimental.pallas import tpu as pltpu
from jax.sharding import PartitionSpec as P

HEAD_DIM = 128
BINS = 32
MESH = pl.DeviceIdType.MESH


norm_eps = 1e-06
grad_scale = 64.0


def scan_kernel(reverse, count, state_ref, out_ref, other, running, exclusive, outgoing, arrived, handed, partner,
                send_sems, recv_sems):
    me = lax.axis_index("seq")
    head = lax.axis_index("head")
    core = me % 2
    mate = me + 1 - 2 * core
    half = exclusive.shape[0]
    wire = outgoing.dtype
    distances = []
    distance = 2
    while distance < count:
        distances.append(distance)
        distance *= 2
    step = -1 if reverse else 1
    targets = [me + step * d for d in distances]
    sources = [me - step * d for d in distances]
    sends = [(t >= 0) & (t < count) for t in targets]
    receives = [(s >= 0) & (s < count) for s in sources]

    barrier = pltpu.get_barrier_semaphore()
    pl.semaphore_signal(barrier, 1, device_id=(mate, head), device_id_type=MESH)
    expected = jnp.int32(1)
    for target, source, send, receive in zip(targets, sources, sends, receives):
        @pl.when(send)
        def _():
            pl.semaphore_signal(barrier, 1, device_id=(target, head), device_id_type=MESH)

        @pl.when(receive)
        def _():
            pl.semaphore_signal(barrier, 1, device_id=(source, head), device_id_type=MESH)

        expected = expected + send.astype(jnp.int32) + receive.astype(jnp.int32)
    pl.semaphore_wait(barrier, expected)

    swap = pltpu.make_async_remote_copy(
        state_ref, other, send_sems.at[0], recv_sems.at[0], device_id=(mate, head), device_id_type=MESH
    )
    swap.start()
    swap.wait()
    mine = pl.ds(core * half, half)
    running[...] = state_ref[mine] + other[mine]
    exclusive[...] = jnp.zeros_like(exclusive)
    copies = []
    for r, (target, send, receive) in enumerate(zip(targets, sends, receives)):
        outgoing[r] = running[...].astype(wire)
        copy = pltpu.make_async_remote_copy(
            outgoing.at[r], arrived.at[r], send_sems.at[r + 1], recv_sems.at[r + 1],
            device_id=(target, head), device_id_type=MESH,
        )
        copies.append(copy)

        @pl.when(send)
        def _():
            copy.start()

        @pl.when(receive)
        def _():
            copy.wait_recv()
            got = arrived[r].astype(running.dtype)
            running[...] = running[...] + got
            exclusive[...] = exclusive[...] + got

    last = len(distances) + 1
    handed[...] = exclusive[...].astype(wire)
    back = pltpu.make_async_remote_copy(
        handed, partner, send_sems.at[last], recv_sems.at[last], device_id=(mate, head), device_id_type=MESH
    )
    back.start()
    for copy, send in zip(copies, sends):
        @pl.when(send)
        def _():
            copy.wait_send()
    back.wait()
    theirs = pl.ds((1 - core) * half, half)
    take_other = (core == 0) if reverse else (core == 1)

    @pl.when(take_other)
    def _():
        out_ref[mine] = exclusive[...] + other[mine]
        out_ref[theirs] = partner[...].astype(out_ref.dtype) + other[theirs]

    @pl.when(jnp.logical_not(take_other))
    def _():
        out_ref[mine] = exclusive[...]
        out_ref[theirs] = partner[...].astype(out_ref.dtype)


def exclusive_scan(shard, axis, reverse=False, wire=jnp.float32):
    count = lax.axis_size(axis)
    heads, rows, cols = shard.shape
    half = heads // 2
    rounds = max(count.bit_length() - 2, 1)
    block = (half, rows, cols)
    return pl.pallas_call(
        functools.partial(scan_kernel, reverse, count),
        out_shape=jax.ShapeDtypeStruct(shard.shape, shard.dtype),
        in_specs=[pl.BlockSpec(memory_space=pltpu.VMEM)],
        out_specs=pl.BlockSpec(memory_space=pltpu.VMEM),
        scratch_shapes=[
            pltpu.VMEM((heads, rows, cols), shard.dtype),
            pltpu.VMEM(block, shard.dtype),
            pltpu.VMEM(block, shard.dtype),
            pltpu.VMEM((rounds,) + block, wire),
            pltpu.VMEM((rounds,) + block, wire),
            pltpu.VMEM(block, wire),
            pltpu.VMEM(block, wire),
            pltpu.SemaphoreType.DMA((rounds + 2,)),
            pltpu.SemaphoreType.DMA((rounds + 2,)),
        ],
        compiler_params=pltpu.CompilerParams(collective_id=1 if reverse else 0, has_side_effects=True),
    )(shard)


def head_barrier(count):
    me = lax.axis_index("head")
    seq = lax.axis_index("seq")
    barrier = pltpu.get_barrier_semaphore()
    for k in range(1, count):
        pl.semaphore_signal(barrier, 1, device_id=(seq, (me + k) % count), device_id_type=MESH)
    pl.semaphore_wait(barrier, count - 1)
    return me, seq


def gather_kernel(count, block_ref, out_ref, slots, send_sems, recv_sems):
    me, seq = head_barrier(count)
    copies = []
    for k in range(1, count):
        copy = pltpu.make_async_remote_copy(
            block_ref, slots.at[k], send_sems.at[k], recv_sems.at[k],
            device_id=(seq, (me + k) % count), device_id_type=MESH,
        )
        copy.start()
        copies.append(copy)
    out_ref[0] = block_ref[...]
    for k, copy in enumerate(copies, start=1):
        copy.wait()
        out_ref[k] = slots[k]


def head_gather(block, count):
    return pl.pallas_call(
        functools.partial(gather_kernel, count),
        out_shape=jax.ShapeDtypeStruct((count,) + block.shape, block.dtype),
        in_specs=[pl.BlockSpec(memory_space=pltpu.VMEM)],
        out_specs=pl.BlockSpec(memory_space=pltpu.VMEM),
        scratch_shapes=[
            pltpu.VMEM((count,) + block.shape, block.dtype),
            pltpu.SemaphoreType.DMA((count,)),
            pltpu.SemaphoreType.DMA((count,)),
        ],
        compiler_params=pltpu.CompilerParams(collective_id=2, has_side_effects=True),
    )(block)


def reduce_kernel(count, parts_ref, loss_ref, out_ref, loss_out, slots, loss_slots, send_sems, recv_sems):
    me, seq = head_barrier(count)
    copies = []
    for k in range(1, count):
        target = (seq, (me + k) % count)
        copy = pltpu.make_async_remote_copy(
            parts_ref.at[k], slots.at[k], send_sems.at[0, k], recv_sems.at[0, k],
            device_id=target, device_id_type=MESH,
        )
        copy.start()
        small = pltpu.make_async_remote_copy(
            loss_ref, loss_slots.at[k], send_sems.at[1, k], recv_sems.at[1, k],
            device_id=target, device_id_type=MESH,
        )
        small.start()
        copies.append((copy, small))
    total = jnp.zeros(out_ref.shape, jnp.float32)
    loss = loss_ref[...]
    for k, (copy, small) in enumerate(copies, start=1):
        copy.wait()
        total = total + slots[k].astype(jnp.float32)
        small.wait()
        loss = loss + loss_slots[k]
    out_ref[...] = total
    loss_out[...] = loss


def head_reduce(parts, loss, count):
    block = parts.shape[1:]
    return pl.pallas_call(
        functools.partial(reduce_kernel, count),
        out_shape=(
            jax.ShapeDtypeStruct(block, jnp.float32),
            jax.ShapeDtypeStruct(loss.shape, loss.dtype),
        ),
        in_specs=[pl.BlockSpec(memory_space=pltpu.VMEM)] * 2,
        out_specs=(pl.BlockSpec(memory_space=pltpu.VMEM),) * 2,
        scratch_shapes=[
            pltpu.VMEM(parts.shape, parts.dtype),
            pltpu.VMEM((count,) + loss.shape, loss.dtype),
            pltpu.SemaphoreType.DMA((2, count)),
            pltpu.SemaphoreType.DMA((2, count)),
        ],
        compiler_params=pltpu.CompilerParams(collective_id=3, has_side_effects=True),
    )(parts, loss)


def body(queries, keys, values, hazard_weight, log_base, time_bin, observed, task_label):
    highest = lax.Precision.HIGHEST
    three_pass = lax.Precision.HIGH
    f32 = jnp.float32
    rows_here = queries.shape[0]
    width_here = queries.shape[1]
    heads_here = width_here // HEAD_DIM
    tasks_here = hazard_weight.shape[1]
    shape_three = (rows_here, heads_here, HEAD_DIM)
    query_rows = queries.reshape(shape_three)
    key_rows = keys.reshape(shape_three)
    value_rows = values.reshape(shape_three)
    causal = jnp.tril(jnp.ones((rows_here, rows_here), f32))
    local_state = jnp.einsum("thd,the->hde", key_rows, value_rows, preferred_element_type=f32)
    prefix = exclusive_scan(local_state, "seq", wire=jnp.bfloat16)
    scores = jnp.einsum("thd,shd->hts", query_rows, key_rows, preferred_element_type=f32) * causal
    raw_out = jnp.einsum(
        "hts,she->the", scores, value_rows, precision=three_pass, preferred_element_type=f32
    )
    raw_out = raw_out + jnp.einsum(
        "thd,hde->the", query_rows, prefix, precision=three_pass, preferred_element_type=f32
    )
    root_mean = jnp.sqrt(jnp.mean(raw_out * raw_out, axis=-1, keepdims=True) + norm_eps)
    normed = raw_out / root_mean
    hidden = normed.astype(jnp.bfloat16).reshape(rows_here, width_here)
    head_count = lax.axis_size("head")
    head_index = lax.axis_index("head")

    def weight_rows(owner):
        return lax.dynamic_slice_in_dim(hazard_weight, owner * width_here, width_here, 0)

    gathered = head_gather(hidden, head_count)
    log_rate = jnp.dot(gathered[0], weight_rows(head_index), preferred_element_type=f32)
    for k in range(1, head_count):
        log_rate = log_rate + jnp.dot(
            gathered[k],
            weight_rows((head_index - k + head_count) % head_count),
            preferred_element_type=f32,
        )
    offset = head_index * tasks_here
    cum_base = jnp.cumsum(jnp.exp(log_base), axis=0)
    bin_hot = (time_bin[:, None] == jnp.arange(BINS, dtype=jnp.int32)[None, :]).astype(f32)
    base_rows = jnp.dot(bin_hot, log_base, precision=highest)
    cum_rows = jnp.dot(bin_hot, cum_base, precision=highest)
    hazard = jnp.exp(log_rate) * cum_rows
    columns = offset + jnp.arange(tasks_here, dtype=jnp.int32)
    label_hit = (task_label[:, None] == columns[None, :]).astype(f32)
    event_flag = observed.astype(f32)
    partial_value = jnp.sum(hazard, axis=1) - event_flag * jnp.sum(
        label_hit * (log_rate + base_rows), axis=1
    )
    dlogit = (grad_scale * (hazard - event_flag[:, None] * label_hit)).astype(jnp.bfloat16)
    def block_term(owner):
        return lax.dot_general(
            dlogit, weight_rows(owner), (((1,), (1,)), ((), ())), preferred_element_type=f32
        )

    parts = jnp.stack(
        [block_term((head_index + k) % head_count).astype(jnp.bfloat16) for k in range(head_count)]
    )
    received, loss_sum = head_reduce(parts, partial_value.reshape(1, -1), head_count)
    grad_hidden = block_term(head_index) + received
    event_loss = loss_sum.reshape(-1)
    grad_norm_in = grad_hidden.reshape(shape_three)
    grad_raw = (
        grad_norm_in - normed * jnp.mean(normed * grad_norm_in, axis=-1, keepdims=True)
    ) / root_mean
    grad_out = grad_raw.astype(jnp.bfloat16)
    local_adjoint = jnp.einsum("thd,the->hde", query_rows, grad_out, preferred_element_type=f32)
    suffix = exclusive_scan(local_adjoint, "seq", reverse=True, wire=jnp.bfloat16)
    back_scores = (
        jnp.einsum("the,she->hts", grad_out, value_rows, preferred_element_type=f32) * causal
    )
    grad_query = jnp.einsum(
        "hts,shd->thd", back_scores, key_rows, precision=three_pass, preferred_element_type=f32
    )
    grad_query = grad_query + jnp.einsum(
        "the,hde->thd", grad_out, prefix, precision=three_pass, preferred_element_type=f32
    )
    grad_key = jnp.einsum(
        "hts,thd->shd", back_scores, query_rows, precision=three_pass, preferred_element_type=f32
    )
    grad_key = grad_key + jnp.einsum(
        "she,hde->shd", value_rows, suffix, precision=three_pass, preferred_element_type=f32
    )
    grad_value = jnp.einsum(
        "hts,the->she", scores, grad_out, precision=three_pass, preferred_element_type=f32
    )
    grad_value = grad_value + jnp.einsum(
        "shd,hde->she", key_rows, suffix, precision=three_pass, preferred_element_type=f32
    )
    grad_queries = grad_query.reshape(rows_here, width_here).astype(jnp.bfloat16)
    grad_keys = grad_key.reshape(rows_here, width_here).astype(jnp.bfloat16)
    grad_values = grad_value.reshape(rows_here, width_here).astype(jnp.bfloat16)
    return (grad_queries, grad_keys, grad_values, event_loss)


def solution(mesh):
    placed = (
        P("seq", "head"),
        P("seq", "head"),
        P("seq", "head"),
        P(None, "head"),
        P(None, "head"),
        P("seq"),
        P("seq"),
        P("seq"),
    )
    return jax.shard_map(
        body,
        mesh=mesh,
        in_specs=placed,
        out_specs=(P("seq", "head"), P("seq", "head"), P("seq", "head"), P("seq")),
        check_vma=False,
    )
```

```python
import functools

import jax
import jax.numpy as jnp
from jax import lax
from jax.experimental import pallas as pl
from jax.experimental.pallas import tpu as pltpu
from jax.sharding import PartitionSpec as P

HEAD_DIM = 128
BINS = 32
MESH = pl.DeviceIdType.MESH


norm_eps = 1e-06
grad_scale = 64.0


def scan_kernel(reverse, count, state_ref, out_ref, other, running, exclusive, outgoing, arrived, handed, partner,
                send_sems, recv_sems):
    me = lax.axis_index("seq")
    head = lax.axis_index("head")
    core = me % 2
    mate = me + 1 - 2 * core
    half = exclusive.shape[0]
    wire = outgoing.dtype
    distances = []
    distance = 2
    while distance < count:
        distances.append(distance)
        distance *= 2
    step = -1 if reverse else 1
    targets = [me + step * d for d in distances]
    sources = [me - step * d for d in distances]
    sends = [(t >= 0) & (t < count) for t in targets]
    receives = [(s >= 0) & (s < count) for s in sources]

    barrier = pltpu.get_barrier_semaphore()
    pl.semaphore_signal(barrier, 1, device_id=(mate, head), device_id_type=MESH)
    expected = jnp.int32(1)
    for target, source, send, receive in zip(targets, sources, sends, receives):
        @pl.when(send)
        def _():
            pl.semaphore_signal(barrier, 1, device_id=(target, head), device_id_type=MESH)

        @pl.when(receive)
        def _():
            pl.semaphore_signal(barrier, 1, device_id=(source, head), device_id_type=MESH)

        expected = expected + send.astype(jnp.int32) + receive.astype(jnp.int32)
    pl.semaphore_wait(barrier, expected)

    swap = pltpu.make_async_remote_copy(
        state_ref, other, send_sems.at[0], recv_sems.at[0], device_id=(mate, head), device_id_type=MESH
    )
    swap.start()
    swap.wait()
    mine = pl.ds(core * half, half)
    running[...] = state_ref[mine] + other[mine]
    exclusive[...] = jnp.zeros_like(exclusive)
    copies = []
    for r, (target, send, receive) in enumerate(zip(targets, sends, receives)):
        outgoing[r] = running[...].astype(wire)
        copy = pltpu.make_async_remote_copy(
            outgoing.at[r], arrived.at[r], send_sems.at[r + 1], recv_sems.at[r + 1],
            device_id=(target, head), device_id_type=MESH,
        )
        copies.append(copy)

        @pl.when(send)
        def _():
            copy.start()

        @pl.when(receive)
        def _():
            copy.wait_recv()
            got = arrived[r].astype(running.dtype)
            running[...] = running[...] + got
            exclusive[...] = exclusive[...] + got

    last = len(distances) + 1
    handed[...] = exclusive[...].astype(wire)
    back = pltpu.make_async_remote_copy(
        handed, partner, send_sems.at[last], recv_sems.at[last], device_id=(mate, head), device_id_type=MESH
    )
    back.start()
    for copy, send in zip(copies, sends):
        @pl.when(send)
        def _():
            copy.wait_send()
    back.wait()
    theirs = pl.ds((1 - core) * half, half)
    take_other = (core == 0) if reverse else (core == 1)

    @pl.when(take_other)
    def _():
        out_ref[mine] = exclusive[...] + other[mine]
        out_ref[theirs] = partner[...].astype(out_ref.dtype) + other[theirs]

    @pl.when(jnp.logical_not(take_other))
    def _():
        out_ref[mine] = exclusive[...]
        out_ref[theirs] = partner[...].astype(out_ref.dtype)


def exclusive_scan(shard, axis, reverse=False, wire=jnp.float32):
    count = lax.axis_size(axis)
    heads, rows, cols = shard.shape
    half = heads // 2
    rounds = max(count.bit_length() - 2, 1)
    block = (half, rows, cols)
    return pl.pallas_call(
        functools.partial(scan_kernel, reverse, count),
        out_shape=jax.ShapeDtypeStruct(shard.shape, shard.dtype),
        in_specs=[pl.BlockSpec(memory_space=pltpu.VMEM)],
        out_specs=pl.BlockSpec(memory_space=pltpu.VMEM),
        scratch_shapes=[
            pltpu.VMEM((heads, rows, cols), shard.dtype),
            pltpu.VMEM(block, shard.dtype),
            pltpu.VMEM(block, shard.dtype),
            pltpu.VMEM((rounds,) + block, wire),
            pltpu.VMEM((rounds,) + block, wire),
            pltpu.VMEM(block, wire),
            pltpu.VMEM(block, wire),
            pltpu.SemaphoreType.DMA((rounds + 2,)),
            pltpu.SemaphoreType.DMA((rounds + 2,)),
        ],
        compiler_params=pltpu.CompilerParams(collective_id=1 if reverse else 0, has_side_effects=True),
    )(shard)


def body(queries, keys, values, hazard_weight, log_base, time_bin, observed, task_label):
    highest = lax.Precision.HIGHEST
    three_pass = lax.Precision.HIGH
    f32 = jnp.float32
    rows_here = queries.shape[0]
    width_here = queries.shape[1]
    heads_here = width_here // HEAD_DIM
    tasks_here = hazard_weight.shape[1]
    shape_three = (rows_here, heads_here, HEAD_DIM)
    query_rows = queries.reshape(shape_three)
    key_rows = keys.reshape(shape_three)
    value_rows = values.reshape(shape_three)
    causal = jnp.tril(jnp.ones((rows_here, rows_here), f32))
    local_state = jnp.einsum("thd,the->hde", key_rows, value_rows, preferred_element_type=f32)
    prefix = exclusive_scan(local_state, "seq", wire=jnp.bfloat16)
    scores = jnp.einsum("thd,shd->hts", query_rows, key_rows, preferred_element_type=f32) * causal
    raw_out = jnp.einsum(
        "hts,she->the", scores, value_rows, precision=three_pass, preferred_element_type=f32
    )
    raw_out = raw_out + jnp.einsum(
        "thd,hde->the", query_rows, prefix, precision=three_pass, preferred_element_type=f32
    )
    root_mean = jnp.sqrt(jnp.mean(raw_out * raw_out, axis=-1, keepdims=True) + norm_eps)
    normed = raw_out / root_mean
    hidden = normed.astype(jnp.bfloat16).reshape(rows_here, width_here)
    head_count = lax.axis_size("head")
    head_index = lax.axis_index("head")

    def weight_rows(owner):
        return lax.dynamic_slice_in_dim(hazard_weight, owner * width_here, width_here, 0)

    gathered = lax.all_to_all(
        jnp.broadcast_to(hidden[None], (head_count,) + hidden.shape), "head", 0, 0, tiled=True
    )
    log_rate = jnp.dot(gathered[0], weight_rows(0), preferred_element_type=f32)
    for owner in range(1, head_count):
        log_rate = log_rate + jnp.dot(gathered[owner], weight_rows(owner), preferred_element_type=f32)
    offset = head_index * tasks_here
    cum_base = jnp.cumsum(jnp.exp(log_base), axis=0)
    bin_hot = (time_bin[:, None] == jnp.arange(BINS, dtype=jnp.int32)[None, :]).astype(f32)
    base_rows = jnp.dot(bin_hot, log_base, precision=highest)
    cum_rows = jnp.dot(bin_hot, cum_base, precision=highest)
    hazard = jnp.exp(log_rate) * cum_rows
    columns = offset + jnp.arange(tasks_here, dtype=jnp.int32)
    label_hit = (task_label[:, None] == columns[None, :]).astype(f32)
    event_flag = observed.astype(f32)
    partial_value = jnp.sum(hazard, axis=1) - event_flag * jnp.sum(
        label_hit * (log_rate + base_rows), axis=1
    )
    dlogit = (grad_scale * (hazard - event_flag[:, None] * label_hit)).astype(jnp.bfloat16)
    def block_term(owner):
        return lax.dot_general(
            dlogit, weight_rows(owner), (((1,), (1,)), ((), ())), preferred_element_type=f32
        )

    parts = jnp.stack([block_term(owner).astype(jnp.bfloat16) for owner in range(head_count)])
    received = lax.all_to_all(parts, "head", 0, 0, tiled=True).astype(f32)
    own = block_term(head_index)
    grad_hidden = own
    for owner in range(head_count):
        grad_hidden = grad_hidden + jnp.where(owner == head_index, 0.0, received[owner])
    losses = lax.all_to_all(
        jnp.broadcast_to(partial_value[None], (head_count,) + partial_value.shape), "head", 0, 0, tiled=True
    )
    event_loss = jnp.sum(losses, axis=0)
    grad_norm_in = grad_hidden.reshape(shape_three)
    grad_raw = (
        grad_norm_in - normed * jnp.mean(normed * grad_norm_in, axis=-1, keepdims=True)
    ) / root_mean
    grad_out = grad_raw.astype(jnp.bfloat16)
    local_adjoint = jnp.einsum("thd,the->hde", query_rows, grad_out, preferred_element_type=f32)
    suffix = exclusive_scan(local_adjoint, "seq", reverse=True, wire=jnp.bfloat16)
    back_scores = (
        jnp.einsum("the,she->hts", grad_out, value_rows, preferred_element_type=f32) * causal
    )
    grad_query = jnp.einsum(
        "hts,shd->thd", back_scores, key_rows, precision=three_pass, preferred_element_type=f32
    )
    grad_query = grad_query + jnp.einsum(
        "the,hde->thd", grad_out, prefix, precision=three_pass, preferred_element_type=f32
    )
    grad_key = jnp.einsum(
        "hts,thd->shd", back_scores, query_rows, precision=three_pass, preferred_element_type=f32
    )
    grad_key = grad_key + jnp.einsum(
        "she,hde->shd", value_rows, suffix, precision=three_pass, preferred_element_type=f32
    )
    grad_value = jnp.einsum(
        "hts,the->she", scores, grad_out, precision=three_pass, preferred_element_type=f32
    )
    grad_value = grad_value + jnp.einsum(
        "shd,hde->she", key_rows, suffix, precision=three_pass, preferred_element_type=f32
    )
    grad_queries = grad_query.reshape(rows_here, width_here).astype(jnp.bfloat16)
    grad_keys = grad_key.reshape(rows_here, width_here).astype(jnp.bfloat16)
    grad_values = grad_value.reshape(rows_here, width_here).astype(jnp.bfloat16)
    return (grad_queries, grad_keys, grad_values, event_loss)


def solution(mesh):
    placed = (
        P("seq", "head"),
        P("seq", "head"),
        P("seq", "head"),
        P(None, "head"),
        P(None, "head"),
        P("seq"),
        P("seq"),
        P("seq"),
    )
    return jax.shard_map(
        body,
        mesh=mesh,
        in_specs=placed,
        out_specs=(P("seq", "head"), P("seq", "head"), P("seq", "head"), P("seq")),
        check_vma=False,
    )
```

```python
import functools

import jax
import jax.numpy as jnp
from jax import lax
from jax.experimental import pallas as pl
from jax.experimental.pallas import tpu as pltpu
from jax.sharding import PartitionSpec as P

HEAD_DIM = 128
BINS = 32
MESH = pl.DeviceIdType.MESH


norm_eps = 1e-06
grad_scale = 64.0


def scan_kernel(reverse, count, state_ref, out_ref, other, running, exclusive, outgoing, arrived, handed, partner,
                send_sems, recv_sems):
    me = lax.axis_index("seq")
    head = lax.axis_index("head")
    core = me % 2
    mate = me + 1 - 2 * core
    half = exclusive.shape[0]
    wire = outgoing.dtype
    distances = []
    distance = 2
    while distance < count:
        distances.append(distance)
        distance *= 2
    step = -1 if reverse else 1
    targets = [me + step * d for d in distances]
    sources = [me - step * d for d in distances]
    sends = [(t >= 0) & (t < count) for t in targets]
    receives = [(s >= 0) & (s < count) for s in sources]

    barrier = pltpu.get_barrier_semaphore()
    pl.semaphore_signal(barrier, 1, device_id=(mate, head), device_id_type=MESH)
    expected = jnp.int32(1)
    for target, source, send, receive in zip(targets, sources, sends, receives):
        @pl.when(send)
        def _():
            pl.semaphore_signal(barrier, 1, device_id=(target, head), device_id_type=MESH)

        @pl.when(receive)
        def _():
            pl.semaphore_signal(barrier, 1, device_id=(source, head), device_id_type=MESH)

        expected = expected + send.astype(jnp.int32) + receive.astype(jnp.int32)
    pl.semaphore_wait(barrier, expected)

    swap = pltpu.make_async_remote_copy(
        state_ref, other, send_sems.at[0], recv_sems.at[0], device_id=(mate, head), device_id_type=MESH
    )
    swap.start()
    swap.wait()
    mine = pl.ds(core * half, half)
    running[...] = state_ref[mine] + other[mine]
    exclusive[...] = jnp.zeros_like(exclusive)
    copies = []
    for r, (target, send, receive) in enumerate(zip(targets, sends, receives)):
        outgoing[r] = running[...].astype(wire)
        copy = pltpu.make_async_remote_copy(
            outgoing.at[r], arrived.at[r], send_sems.at[r + 1], recv_sems.at[r + 1],
            device_id=(target, head), device_id_type=MESH,
        )
        copies.append(copy)

        @pl.when(send)
        def _():
            copy.start()

        @pl.when(receive)
        def _():
            copy.wait_recv()
            got = arrived[r].astype(running.dtype)
            running[...] = running[...] + got
            exclusive[...] = exclusive[...] + got

    last = len(distances) + 1
    handed[...] = exclusive[...].astype(wire)
    back = pltpu.make_async_remote_copy(
        handed, partner, send_sems.at[last], recv_sems.at[last], device_id=(mate, head), device_id_type=MESH
    )
    back.start()
    for copy, send in zip(copies, sends):
        @pl.when(send)
        def _():
            copy.wait_send()
    back.wait()
    theirs = pl.ds((1 - core) * half, half)
    take_other = (core == 0) if reverse else (core == 1)

    @pl.when(take_other)
    def _():
        out_ref[mine] = exclusive[...] + other[mine]
        out_ref[theirs] = partner[...].astype(out_ref.dtype) + other[theirs]

    @pl.when(jnp.logical_not(take_other))
    def _():
        out_ref[mine] = exclusive[...]
        out_ref[theirs] = partner[...].astype(out_ref.dtype)


def exclusive_scan(shard, axis, reverse=False, wire=jnp.float32):
    count = lax.axis_size(axis)
    heads, rows, cols = shard.shape
    half = heads // 2
    rounds = max(count.bit_length() - 2, 1)
    block = (half, rows, cols)
    return pl.pallas_call(
        functools.partial(scan_kernel, reverse, count),
        out_shape=jax.ShapeDtypeStruct(shard.shape, shard.dtype),
        in_specs=[pl.BlockSpec(memory_space=pltpu.VMEM)],
        out_specs=pl.BlockSpec(memory_space=pltpu.VMEM),
        scratch_shapes=[
            pltpu.VMEM((heads, rows, cols), shard.dtype),
            pltpu.VMEM(block, shard.dtype),
            pltpu.VMEM(block, shard.dtype),
            pltpu.VMEM((rounds,) + block, wire),
            pltpu.VMEM((rounds,) + block, wire),
            pltpu.VMEM(block, wire),
            pltpu.VMEM(block, wire),
            pltpu.SemaphoreType.DMA((rounds + 2,)),
            pltpu.SemaphoreType.DMA((rounds + 2,)),
        ],
        compiler_params=pltpu.CompilerParams(collective_id=1 if reverse else 0, has_side_effects=True),
    )(shard)


def body(queries, keys, values, hazard_weight, log_base, time_bin, observed, task_label):
    highest = lax.Precision.HIGHEST
    three_pass = lax.Precision.HIGH
    f32 = jnp.float32
    rows_here = queries.shape[0]
    width_here = queries.shape[1]
    heads_here = width_here // HEAD_DIM
    tasks_here = hazard_weight.shape[1]
    shape_three = (rows_here, heads_here, HEAD_DIM)
    query_rows = queries.reshape(shape_three)
    key_rows = keys.reshape(shape_three)
    value_rows = values.reshape(shape_three)
    causal = jnp.tril(jnp.ones((rows_here, rows_here), f32))
    local_state = jnp.einsum("thd,the->hde", key_rows, value_rows, preferred_element_type=f32)
    prefix = exclusive_scan(local_state, "seq", wire=jnp.bfloat16)
    scores = jnp.einsum("thd,shd->hts", query_rows, key_rows, preferred_element_type=f32) * causal
    raw_out = jnp.einsum(
        "hts,she->the", scores, value_rows, precision=three_pass, preferred_element_type=f32
    )
    raw_out = raw_out + jnp.einsum(
        "thd,hde->the", query_rows, prefix, precision=three_pass, preferred_element_type=f32
    )
    root_mean = jnp.sqrt(jnp.mean(raw_out * raw_out, axis=-1, keepdims=True) + norm_eps)
    normed = raw_out / root_mean
    hidden = normed.astype(jnp.bfloat16).reshape(rows_here, width_here)
    head_count = lax.axis_size("head")
    head_index = lax.axis_index("head")

    def shifted(x, k):
        return lax.ppermute(x, "head", [(m, (m + k) % head_count) for m in range(head_count)])

    def weight_rows(owner):
        return lax.dynamic_slice_in_dim(hazard_weight, owner * width_here, width_here, 0)

    log_rate = jnp.dot(hidden, weight_rows(head_index), preferred_element_type=f32)
    for k in range(1, head_count):
        log_rate = log_rate + jnp.dot(
            shifted(hidden, k),
            weight_rows((head_index - k + head_count) % head_count),
            preferred_element_type=f32,
        )
    offset = head_index * tasks_here
    cum_base = jnp.cumsum(jnp.exp(log_base), axis=0)
    bin_hot = (time_bin[:, None] == jnp.arange(BINS, dtype=jnp.int32)[None, :]).astype(f32)
    base_rows = jnp.dot(bin_hot, log_base, precision=highest)
    cum_rows = jnp.dot(bin_hot, cum_base, precision=highest)
    hazard = jnp.exp(log_rate) * cum_rows
    columns = offset + jnp.arange(tasks_here, dtype=jnp.int32)
    label_hit = (task_label[:, None] == columns[None, :]).astype(f32)
    event_flag = observed.astype(f32)
    partial_value = jnp.sum(hazard, axis=1) - event_flag * jnp.sum(
        label_hit * (log_rate + base_rows), axis=1
    )
    dlogit = (grad_scale * (hazard - event_flag[:, None] * label_hit)).astype(jnp.bfloat16)
    def block_term(owner):
        return lax.dot_general(
            dlogit, weight_rows(owner), (((1,), (1,)), ((), ())), preferred_element_type=f32
        )

    blocks = jnp.stack([block_term(owner) for owner in range(head_count)])
    grad_hidden = lax.dynamic_index_in_dim(blocks, head_index, 0, False)
    event_loss = partial_value
    for k in range(1, head_count):
        sent = lax.dynamic_index_in_dim(blocks, (head_index + k) % head_count, 0, False)
        got, got_loss = shifted((sent.astype(jnp.bfloat16), partial_value), k)
        grad_hidden = grad_hidden + got.astype(f32)
        event_loss = event_loss + got_loss
    grad_norm_in = grad_hidden.reshape(shape_three)
    grad_raw = (
        grad_norm_in - normed * jnp.mean(normed * grad_norm_in, axis=-1, keepdims=True)
    ) / root_mean
    grad_out = grad_raw.astype(jnp.bfloat16)
    local_adjoint = jnp.einsum("thd,the->hde", query_rows, grad_out, preferred_element_type=f32)
    suffix = exclusive_scan(local_adjoint, "seq", reverse=True, wire=jnp.bfloat16)
    back_scores = (
        jnp.einsum("the,she->hts", grad_out, value_rows, preferred_element_type=f32) * causal
    )
    grad_query = jnp.einsum(
        "hts,shd->thd", back_scores, key_rows, precision=three_pass, preferred_element_type=f32
    )
    grad_query = grad_query + jnp.einsum(
        "the,hde->thd", grad_out, prefix, precision=three_pass, preferred_element_type=f32
    )
    grad_key = jnp.einsum(
        "hts,thd->shd", back_scores, query_rows, precision=three_pass, preferred_element_type=f32
    )
    grad_key = grad_key + jnp.einsum(
        "she,hde->shd", value_rows, suffix, precision=three_pass, preferred_element_type=f32
    )
    grad_value = jnp.einsum(
        "hts,the->she", scores, grad_out, precision=three_pass, preferred_element_type=f32
    )
    grad_value = grad_value + jnp.einsum(
        "shd,hde->she", key_rows, suffix, precision=three_pass, preferred_element_type=f32
    )
    grad_queries = grad_query.reshape(rows_here, width_here).astype(jnp.bfloat16)
    grad_keys = grad_key.reshape(rows_here, width_here).astype(jnp.bfloat16)
    grad_values = grad_value.reshape(rows_here, width_here).astype(jnp.bfloat16)
    return (grad_queries, grad_keys, grad_values, event_loss)


def solution(mesh):
    placed = (
        P("seq", "head"),
        P("seq", "head"),
        P("seq", "head"),
        P(None, "head"),
        P(None, "head"),
        P("seq"),
        P("seq"),
        P("seq"),
    )
    return jax.shard_map(
        body,
        mesh=mesh,
        in_specs=placed,
        out_specs=(P("seq", "head"), P("seq", "head"), P("seq", "head"), P("seq")),
        check_vma=False,
    )
```

```python
import functools

import jax
import jax.numpy as jnp
from jax import lax
from jax.experimental import pallas as pl
from jax.experimental.pallas import tpu as pltpu
from jax.sharding import PartitionSpec as P

HEAD_DIM = 128
BINS = 32
MESH = pl.DeviceIdType.MESH


norm_eps = 1e-06
grad_scale = 64.0


def scan_kernel(reverse, count, state_ref, out_ref, other, running, exclusive, outgoing, arrived, handed, partner,
                send_sems, recv_sems):
    me = lax.axis_index("seq")
    head = lax.axis_index("head")
    core = me % 2
    mate = me + 1 - 2 * core
    half = exclusive.shape[0]
    wire = outgoing.dtype
    rounds = scan_rounds(count)
    step = -1 if reverse else 1
    flat = [(r, d) for r, group in enumerate(rounds) for d in group]
    targets = [me + step * d for _, d in flat]
    sources = [me - step * d for _, d in flat]
    sends = [(t >= 0) & (t < count) for t in targets]
    receives = [(s >= 0) & (s < count) for s in sources]

    barrier = pltpu.get_barrier_semaphore()
    pl.semaphore_signal(barrier, 1, device_id=(mate, head), device_id_type=MESH)
    expected = jnp.int32(1)
    for target, source, send, receive in zip(targets, sources, sends, receives):
        @pl.when(send)
        def _():
            pl.semaphore_signal(barrier, 1, device_id=(target, head), device_id_type=MESH)

        @pl.when(receive)
        def _():
            pl.semaphore_signal(barrier, 1, device_id=(source, head), device_id_type=MESH)

        expected = expected + send.astype(jnp.int32) + receive.astype(jnp.int32)
    pl.semaphore_wait(barrier, expected)

    swap = pltpu.make_async_remote_copy(
        state_ref, other, send_sems.at[0], recv_sems.at[0], device_id=(mate, head), device_id_type=MESH
    )
    swap.start()
    swap.wait()
    mine = pl.ds(core * half, half)
    running[...] = state_ref[mine] + other[mine]
    exclusive[...] = jnp.zeros_like(exclusive)
    copies = []
    for r, group in enumerate(rounds):
        outgoing[r] = running[...].astype(wire)
        members = [c for c, (owner, _) in enumerate(flat) if owner == r]
        for c in members:
            copy = pltpu.make_async_remote_copy(
                outgoing.at[r], arrived.at[c], send_sems.at[c + 1], recv_sems.at[c + 1],
                device_id=(targets[c], head), device_id_type=MESH,
            )
            copies.append(copy)

            @pl.when(sends[c])
            def _():
                copy.start()

        for c in members:
            @pl.when(receives[c])
            def _():
                copies[c].wait_recv()
                got = arrived[c].astype(running.dtype)
                running[...] = running[...] + got
                exclusive[...] = exclusive[...] + got

    last = len(flat) + 1
    handed[...] = exclusive[...].astype(wire)
    back = pltpu.make_async_remote_copy(
        handed, partner, send_sems.at[last], recv_sems.at[last], device_id=(mate, head), device_id_type=MESH
    )
    back.start()
    for copy, send in zip(copies, sends):
        @pl.when(send)
        def _():
            copy.wait_send()
    back.wait()
    theirs = pl.ds((1 - core) * half, half)
    take_other = (core == 0) if reverse else (core == 1)

    @pl.when(take_other)
    def _():
        out_ref[mine] = exclusive[...] + other[mine]
        out_ref[theirs] = partner[...].astype(out_ref.dtype) + other[theirs]

    @pl.when(jnp.logical_not(take_other))
    def _():
        out_ref[mine] = exclusive[...]
        out_ref[theirs] = partner[...].astype(out_ref.dtype)


def scan_rounds(count):
    chips = count // 2
    rounds = []
    window = 1
    while window < chips:
        if chips == 4 * window:
            rounds.append([2 * window, 4 * window, 6 * window])
            window *= 4
        else:
            rounds.append([2 * window])
            window *= 2
    return rounds


def exclusive_scan(shard, axis, reverse=False, wire=jnp.float32):
    count = lax.axis_size(axis)
    heads, rows, cols = shard.shape
    half = heads // 2
    rounds = scan_rounds(count)
    copies = max(sum(len(group) for group in rounds), 1)
    block = (half, rows, cols)
    return pl.pallas_call(
        functools.partial(scan_kernel, reverse, count),
        out_shape=jax.ShapeDtypeStruct(shard.shape, shard.dtype),
        in_specs=[pl.BlockSpec(memory_space=pltpu.VMEM)],
        out_specs=pl.BlockSpec(memory_space=pltpu.VMEM),
        scratch_shapes=[
            pltpu.VMEM((heads, rows, cols), shard.dtype),
            pltpu.VMEM(block, shard.dtype),
            pltpu.VMEM(block, shard.dtype),
            pltpu.VMEM((max(len(rounds), 1),) + block, wire),
            pltpu.VMEM((copies,) + block, wire),
            pltpu.VMEM(block, wire),
            pltpu.VMEM(block, wire),
            pltpu.SemaphoreType.DMA((copies + 2,)),
            pltpu.SemaphoreType.DMA((copies + 2,)),
        ],
        compiler_params=pltpu.CompilerParams(collective_id=1 if reverse else 0, has_side_effects=True),
    )(shard)


def body(queries, keys, values, hazard_weight, log_base, time_bin, observed, task_label):
    highest = lax.Precision.HIGHEST
    three_pass = lax.Precision.HIGH
    f32 = jnp.float32
    rows_here = queries.shape[0]
    width_here = queries.shape[1]
    heads_here = width_here // HEAD_DIM
    tasks_here = hazard_weight.shape[1]
    shape_three = (rows_here, heads_here, HEAD_DIM)
    query_rows = queries.reshape(shape_three)
    key_rows = keys.reshape(shape_three)
    value_rows = values.reshape(shape_three)
    causal = jnp.tril(jnp.ones((rows_here, rows_here), f32))
    local_state = jnp.einsum("thd,the->hde", key_rows, value_rows, preferred_element_type=f32)
    prefix = exclusive_scan(local_state, "seq")
    scores = jnp.einsum("thd,shd->hts", query_rows, key_rows, preferred_element_type=f32) * causal
    raw_out = jnp.einsum(
        "hts,she->the", scores, value_rows, precision=three_pass, preferred_element_type=f32
    )
    raw_out = raw_out + jnp.einsum(
        "thd,hde->the", query_rows, prefix, precision=three_pass, preferred_element_type=f32
    )
    root_mean = jnp.sqrt(jnp.mean(raw_out * raw_out, axis=-1, keepdims=True) + norm_eps)
    normed = raw_out / root_mean
    hidden = normed.astype(jnp.bfloat16).reshape(rows_here, width_here)
    head_count = lax.axis_size("head")
    head_index = lax.axis_index("head")

    def shifted(x, k):
        return lax.ppermute(x, "head", [(m, (m + k) % head_count) for m in range(head_count)])

    def weight_rows(owner):
        return lax.dynamic_slice_in_dim(hazard_weight, owner * width_here, width_here, 0)

    log_rate = jnp.dot(hidden, weight_rows(head_index), preferred_element_type=f32)
    for k in range(1, head_count):
        log_rate = log_rate + jnp.dot(
            shifted(hidden, k),
            weight_rows((head_index - k + head_count) % head_count),
            preferred_element_type=f32,
        )
    offset = head_index * tasks_here
    cum_base = jnp.cumsum(jnp.exp(log_base), axis=0)
    bin_hot = (time_bin[:, None] == jnp.arange(BINS, dtype=jnp.int32)[None, :]).astype(f32)
    base_rows = jnp.dot(bin_hot, log_base, precision=highest)
    cum_rows = jnp.dot(bin_hot, cum_base, precision=highest)
    hazard = jnp.exp(log_rate) * cum_rows
    columns = offset + jnp.arange(tasks_here, dtype=jnp.int32)
    label_hit = (task_label[:, None] == columns[None, :]).astype(f32)
    event_flag = observed.astype(f32)
    partial_value = jnp.sum(hazard, axis=1) - event_flag * jnp.sum(
        label_hit * (log_rate + base_rows), axis=1
    )
    dlogit = (grad_scale * (hazard - event_flag[:, None] * label_hit)).astype(jnp.bfloat16)
    def block_term(owner):
        return lax.dot_general(
            dlogit, weight_rows(owner), (((1,), (1,)), ((), ())), preferred_element_type=f32
        )

    grad_hidden = block_term(head_index)
    event_loss = partial_value
    for k in range(1, head_count):
        sent = block_term((head_index + k) % head_count).astype(jnp.bfloat16)
        grad_hidden = grad_hidden + shifted(sent, k).astype(f32)
        event_loss = event_loss + shifted(partial_value, k)
    grad_norm_in = grad_hidden.reshape(shape_three)
    grad_raw = (
        grad_norm_in - normed * jnp.mean(normed * grad_norm_in, axis=-1, keepdims=True)
    ) / root_mean
    grad_out = grad_raw.astype(jnp.bfloat16)
    local_adjoint = jnp.einsum("thd,the->hde", query_rows, grad_out, preferred_element_type=f32)
    suffix = exclusive_scan(local_adjoint, "seq", reverse=True)
    back_scores = (
        jnp.einsum("the,she->hts", grad_out, value_rows, preferred_element_type=f32) * causal
    )
    grad_query = jnp.einsum(
        "hts,shd->thd", back_scores, key_rows, precision=three_pass, preferred_element_type=f32
    )
    grad_query = grad_query + jnp.einsum(
        "the,hde->thd", grad_out, prefix, precision=three_pass, preferred_element_type=f32
    )
    grad_key = jnp.einsum(
        "hts,thd->shd", back_scores, query_rows, precision=three_pass, preferred_element_type=f32
    )
    grad_key = grad_key + jnp.einsum(
        "she,hde->shd", value_rows, suffix, precision=three_pass, preferred_element_type=f32
    )
    grad_value = jnp.einsum(
        "hts,the->she", scores, grad_out, precision=three_pass, preferred_element_type=f32
    )
    grad_value = grad_value + jnp.einsum(
        "shd,hde->she", key_rows, suffix, precision=three_pass, preferred_element_type=f32
    )
    grad_queries = grad_query.reshape(rows_here, width_here).astype(jnp.bfloat16)
    grad_keys = grad_key.reshape(rows_here, width_here).astype(jnp.bfloat16)
    grad_values = grad_value.reshape(rows_here, width_here).astype(jnp.bfloat16)
    return (grad_queries, grad_keys, grad_values, event_loss)


def solution(mesh):
    placed = (
        P("seq", "head"),
        P("seq", "head"),
        P("seq", "head"),
        P(None, "head"),
        P(None, "head"),
        P("seq"),
        P("seq"),
        P("seq"),
    )
    return jax.shard_map(
        body,
        mesh=mesh,
        in_specs=placed,
        out_specs=(P("seq", "head"), P("seq", "head"), P("seq", "head"), P("seq")),
        check_vma=False,
    )
```

```python
import functools

import jax
import jax.numpy as jnp
from jax import lax
from jax.experimental import pallas as pl
from jax.experimental.pallas import tpu as pltpu
from jax.sharding import PartitionSpec as P

HEAD_DIM = 128
BINS = 32
MESH = pl.DeviceIdType.MESH


norm_eps = 1e-06
grad_scale = 64.0


def scan_kernel(reverse, count, state_ref, out_ref, other, running, exclusive, outgoing, arrived, handed, partner,
                send_sems, recv_sems):
    me = lax.axis_index("seq")
    head = lax.axis_index("head")
    core = me % 2
    mate = me + 1 - 2 * core
    half = exclusive.shape[0]
    wire = outgoing.dtype
    first = scan_rounds(count)
    second = first[-1:] + first[:-1]
    width = max(len(group) for group in first)
    rounds = list(range(len(first)))
    step = -1 if reverse else 1
    flat = []
    targets, sources, sends, receives = [], [], [], []
    for r in rounds:
        for s in range(width):
            flat.append((r, s))
            d0 = first[r][s] if s < len(first[r]) else 0
            d1 = second[r][s] if s < len(second[r]) else 0
            distance = jnp.where(core == 0, d0, d1)
            used = (distance > 0)
            target = me + step * distance
            source = me - step * distance
            targets.append(target)
            sources.append(source)
            sends.append(used & (target >= 0) & (target < count))
            receives.append(used & (source >= 0) & (source < count))

    barrier = pltpu.get_barrier_semaphore()
    pl.semaphore_signal(barrier, 1, device_id=(mate, head), device_id_type=MESH)
    expected = jnp.int32(1)
    for target, source, send, receive in zip(targets, sources, sends, receives):
        @pl.when(send)
        def _():
            pl.semaphore_signal(barrier, 1, device_id=(target, head), device_id_type=MESH)

        @pl.when(receive)
        def _():
            pl.semaphore_signal(barrier, 1, device_id=(source, head), device_id_type=MESH)

        expected = expected + send.astype(jnp.int32) + receive.astype(jnp.int32)
    pl.semaphore_wait(barrier, expected)

    swap = pltpu.make_async_remote_copy(
        state_ref, other, send_sems.at[0], recv_sems.at[0], device_id=(mate, head), device_id_type=MESH
    )
    swap.start()
    swap.wait()
    mine = pl.ds(core * half, half)
    running[...] = state_ref[mine] + other[mine]
    exclusive[...] = jnp.zeros_like(exclusive)
    copies = []
    for r, group in enumerate(rounds):
        outgoing[r] = running[...].astype(wire)
        members = [c for c, (owner, _) in enumerate(flat) if owner == r]
        for c in members:
            copy = pltpu.make_async_remote_copy(
                outgoing.at[r], arrived.at[c], send_sems.at[c + 1], recv_sems.at[c + 1],
                device_id=(targets[c], head), device_id_type=MESH,
            )
            copies.append(copy)

            @pl.when(sends[c])
            def _():
                copy.start()

        for c in members:
            @pl.when(receives[c])
            def _():
                copies[c].wait_recv()
                got = arrived[c].astype(running.dtype)
                running[...] = running[...] + got
                exclusive[...] = exclusive[...] + got

    last = len(flat) + 1
    handed[...] = exclusive[...].astype(wire)
    back = pltpu.make_async_remote_copy(
        handed, partner, send_sems.at[last], recv_sems.at[last], device_id=(mate, head), device_id_type=MESH
    )
    back.start()
    for copy, send in zip(copies, sends):
        @pl.when(send)
        def _():
            copy.wait_send()
    back.wait()
    theirs = pl.ds((1 - core) * half, half)
    take_other = (core == 0) if reverse else (core == 1)

    @pl.when(take_other)
    def _():
        out_ref[mine] = exclusive[...] + other[mine]
        out_ref[theirs] = partner[...].astype(out_ref.dtype) + other[theirs]

    @pl.when(jnp.logical_not(take_other))
    def _():
        out_ref[mine] = exclusive[...]
        out_ref[theirs] = partner[...].astype(out_ref.dtype)


def scan_rounds(count):
    chips = count // 2
    rounds = []
    window = 1
    while window < chips:
        if chips == 4 * window:
            rounds.append([2 * window, 4 * window, 6 * window])
            window *= 4
        else:
            rounds.append([2 * window])
            window *= 2
    return rounds


def exclusive_scan(shard, axis, reverse=False, wire=jnp.float32):
    count = lax.axis_size(axis)
    heads, rows, cols = shard.shape
    half = heads // 2
    rounds = scan_rounds(count)
    copies = max(len(rounds) * max(len(group) for group in rounds), 1)
    block = (half, rows, cols)
    return pl.pallas_call(
        functools.partial(scan_kernel, reverse, count),
        out_shape=jax.ShapeDtypeStruct(shard.shape, shard.dtype),
        in_specs=[pl.BlockSpec(memory_space=pltpu.VMEM)],
        out_specs=pl.BlockSpec(memory_space=pltpu.VMEM),
        scratch_shapes=[
            pltpu.VMEM((heads, rows, cols), shard.dtype),
            pltpu.VMEM(block, shard.dtype),
            pltpu.VMEM(block, shard.dtype),
            pltpu.VMEM((max(len(rounds), 1),) + block, wire),
            pltpu.VMEM((copies,) + block, wire),
            pltpu.VMEM(block, wire),
            pltpu.VMEM(block, wire),
            pltpu.SemaphoreType.DMA((copies + 2,)),
            pltpu.SemaphoreType.DMA((copies + 2,)),
        ],
        compiler_params=pltpu.CompilerParams(collective_id=1 if reverse else 0, has_side_effects=True),
    )(shard)


def body(queries, keys, values, hazard_weight, log_base, time_bin, observed, task_label):
    highest = lax.Precision.HIGHEST
    three_pass = lax.Precision.HIGH
    f32 = jnp.float32
    rows_here = queries.shape[0]
    width_here = queries.shape[1]
    heads_here = width_here // HEAD_DIM
    tasks_here = hazard_weight.shape[1]
    shape_three = (rows_here, heads_here, HEAD_DIM)
    query_rows = queries.reshape(shape_three)
    key_rows = keys.reshape(shape_three)
    value_rows = values.reshape(shape_three)
    causal = jnp.tril(jnp.ones((rows_here, rows_here), f32))
    local_state = jnp.einsum("thd,the->hde", key_rows, value_rows, preferred_element_type=f32)
    prefix = exclusive_scan(local_state, "seq")
    scores = jnp.einsum("thd,shd->hts", query_rows, key_rows, preferred_element_type=f32) * causal
    raw_out = jnp.einsum(
        "hts,she->the", scores, value_rows, precision=three_pass, preferred_element_type=f32
    )
    raw_out = raw_out + jnp.einsum(
        "thd,hde->the", query_rows, prefix, precision=three_pass, preferred_element_type=f32
    )
    root_mean = jnp.sqrt(jnp.mean(raw_out * raw_out, axis=-1, keepdims=True) + norm_eps)
    normed = raw_out / root_mean
    hidden = normed.astype(jnp.bfloat16).reshape(rows_here, width_here)
    head_count = lax.axis_size("head")
    head_index = lax.axis_index("head")

    def shifted(x, k):
        return lax.ppermute(x, "head", [(m, (m + k) % head_count) for m in range(head_count)])

    def weight_rows(owner):
        return lax.dynamic_slice_in_dim(hazard_weight, owner * width_here, width_here, 0)

    log_rate = jnp.dot(hidden, weight_rows(head_index), preferred_element_type=f32)
    for k in range(1, head_count):
        log_rate = log_rate + jnp.dot(
            shifted(hidden, k),
            weight_rows((head_index - k + head_count) % head_count),
            preferred_element_type=f32,
        )
    offset = head_index * tasks_here
    cum_base = jnp.cumsum(jnp.exp(log_base), axis=0)
    bin_hot = (time_bin[:, None] == jnp.arange(BINS, dtype=jnp.int32)[None, :]).astype(f32)
    base_rows = jnp.dot(bin_hot, log_base, precision=highest)
    cum_rows = jnp.dot(bin_hot, cum_base, precision=highest)
    hazard = jnp.exp(log_rate) * cum_rows
    columns = offset + jnp.arange(tasks_here, dtype=jnp.int32)
    label_hit = (task_label[:, None] == columns[None, :]).astype(f32)
    event_flag = observed.astype(f32)
    partial_value = jnp.sum(hazard, axis=1) - event_flag * jnp.sum(
        label_hit * (log_rate + base_rows), axis=1
    )
    dlogit = (grad_scale * (hazard - event_flag[:, None] * label_hit)).astype(jnp.bfloat16)
    def block_term(owner):
        return lax.dot_general(
            dlogit, weight_rows(owner), (((1,), (1,)), ((), ())), preferred_element_type=f32
        )

    grad_hidden = block_term(head_index)
    event_loss = partial_value
    for k in range(1, head_count):
        sent = block_term((head_index + k) % head_count).astype(jnp.bfloat16)
        grad_hidden = grad_hidden + shifted(sent, k).astype(f32)
        event_loss = event_loss + shifted(partial_value, k)
    grad_norm_in = grad_hidden.reshape(shape_three)
    grad_raw = (
        grad_norm_in - normed * jnp.mean(normed * grad_norm_in, axis=-1, keepdims=True)
    ) / root_mean
    grad_out = grad_raw.astype(jnp.bfloat16)
    local_adjoint = jnp.einsum("thd,the->hde", query_rows, grad_out, preferred_element_type=f32)
    suffix = exclusive_scan(local_adjoint, "seq", reverse=True)
    back_scores = (
        jnp.einsum("the,she->hts", grad_out, value_rows, preferred_element_type=f32) * causal
    )
    grad_query = jnp.einsum(
        "hts,shd->thd", back_scores, key_rows, precision=three_pass, preferred_element_type=f32
    )
    grad_query = grad_query + jnp.einsum(
        "the,hde->thd", grad_out, prefix, precision=three_pass, preferred_element_type=f32
    )
    grad_key = jnp.einsum(
        "hts,thd->shd", back_scores, query_rows, precision=three_pass, preferred_element_type=f32
    )
    grad_key = grad_key + jnp.einsum(
        "she,hde->shd", value_rows, suffix, precision=three_pass, preferred_element_type=f32
    )
    grad_value = jnp.einsum(
        "hts,the->she", scores, grad_out, precision=three_pass, preferred_element_type=f32
    )
    grad_value = grad_value + jnp.einsum(
        "shd,hde->she", key_rows, suffix, precision=three_pass, preferred_element_type=f32
    )
    grad_queries = grad_query.reshape(rows_here, width_here).astype(jnp.bfloat16)
    grad_keys = grad_key.reshape(rows_here, width_here).astype(jnp.bfloat16)
    grad_values = grad_value.reshape(rows_here, width_here).astype(jnp.bfloat16)
    return (grad_queries, grad_keys, grad_values, event_loss)


def solution(mesh):
    placed = (
        P("seq", "head"),
        P("seq", "head"),
        P("seq", "head"),
        P(None, "head"),
        P(None, "head"),
        P("seq"),
        P("seq"),
        P("seq"),
    )
    return jax.shard_map(
        body,
        mesh=mesh,
        in_specs=placed,
        out_specs=(P("seq", "head"), P("seq", "head"), P("seq", "head"), P("seq")),
        check_vma=False,
    )
```

```python
import functools

import jax
import jax.numpy as jnp
from jax import lax
from jax.experimental import pallas as pl
from jax.experimental.pallas import tpu as pltpu
from jax.sharding import PartitionSpec as P

HEAD_DIM = 128
BINS = 32
MESH = pl.DeviceIdType.MESH


norm_eps = 1e-06
grad_scale = 64.0


def scan_kernel(reverse, count, state_ref, out_ref, other, running, exclusive, outgoing, arrived, handed, partner,
                send_sems, recv_sems):
    me = lax.axis_index("seq")
    head = lax.axis_index("head")
    core = me % 2
    mate = me + 1 - 2 * core
    half = exclusive.shape[0]
    wire = outgoing.dtype
    rounds = scan_rounds(count)
    step = -1 if reverse else 1
    flat = [(r, d) for r, group in enumerate(rounds) for d in group]
    targets = [me + step * d for _, d in flat]
    sources = [me - step * d for _, d in flat]
    sends = [(t >= 0) & (t < count) for t in targets]
    receives = [(s >= 0) & (s < count) for s in sources]

    barrier = pltpu.get_barrier_semaphore()
    pl.semaphore_signal(barrier, 1, device_id=(mate, head), device_id_type=MESH)
    expected = jnp.int32(1)
    for target, source, send, receive in zip(targets, sources, sends, receives):
        @pl.when(send)
        def _():
            pl.semaphore_signal(barrier, 1, device_id=(target, head), device_id_type=MESH)

        @pl.when(receive)
        def _():
            pl.semaphore_signal(barrier, 1, device_id=(source, head), device_id_type=MESH)

        expected = expected + send.astype(jnp.int32) + receive.astype(jnp.int32)
    pl.semaphore_wait(barrier, expected)

    swap = pltpu.make_async_remote_copy(
        state_ref, other, send_sems.at[0], recv_sems.at[0], device_id=(mate, head), device_id_type=MESH
    )
    swap.start()
    swap.wait()
    mine = pl.ds(core * half, half)
    running[...] = state_ref[mine] + other[mine]
    exclusive[...] = jnp.zeros_like(exclusive)
    copies = []
    for r, group in enumerate(rounds):
        outgoing[r] = running[...].astype(wire)
        members = [c for c, (owner, _) in enumerate(flat) if owner == r]
        for c in members:
            copy = pltpu.make_async_remote_copy(
                outgoing.at[r], arrived.at[c], send_sems.at[c + 1], recv_sems.at[c + 1],
                device_id=(targets[c], head), device_id_type=MESH,
            )
            copies.append(copy)

            @pl.when(sends[c])
            def _():
                copy.start()

        for c in members:
            @pl.when(receives[c])
            def _():
                copies[c].wait_recv()
                got = arrived[c].astype(running.dtype)
                running[...] = running[...] + got
                exclusive[...] = exclusive[...] + got

    last = len(flat) + 1
    handed[...] = exclusive[...].astype(wire)
    back = pltpu.make_async_remote_copy(
        handed, partner, send_sems.at[last], recv_sems.at[last], device_id=(mate, head), device_id_type=MESH
    )
    back.start()
    for copy, send in zip(copies, sends):
        @pl.when(send)
        def _():
            copy.wait_send()
    back.wait()
    theirs = pl.ds((1 - core) * half, half)
    take_other = (core == 0) if reverse else (core == 1)

    @pl.when(take_other)
    def _():
        out_ref[mine] = exclusive[...] + other[mine]
        out_ref[theirs] = partner[...].astype(out_ref.dtype) + other[theirs]

    @pl.when(jnp.logical_not(take_other))
    def _():
        out_ref[mine] = exclusive[...]
        out_ref[theirs] = partner[...].astype(out_ref.dtype)


def scan_rounds(count):
    chips = count // 2
    rounds = []
    window = 1
    while window < chips:
        if chips == 4 * window:
            rounds.append([2 * window, 4 * window, 6 * window])
            window *= 4
        else:
            rounds.append([2 * window])
            window *= 2
    return rounds


def exclusive_scan(shard, axis, reverse=False, wire=jnp.float32):
    count = lax.axis_size(axis)
    heads, rows, cols = shard.shape
    half = heads // 2
    rounds = scan_rounds(count)
    copies = max(sum(len(group) for group in rounds), 1)
    block = (half, rows, cols)
    return pl.pallas_call(
        functools.partial(scan_kernel, reverse, count),
        out_shape=jax.ShapeDtypeStruct(shard.shape, shard.dtype),
        in_specs=[pl.BlockSpec(memory_space=pltpu.VMEM)],
        out_specs=pl.BlockSpec(memory_space=pltpu.VMEM),
        scratch_shapes=[
            pltpu.VMEM((heads, rows, cols), shard.dtype),
            pltpu.VMEM(block, shard.dtype),
            pltpu.VMEM(block, shard.dtype),
            pltpu.VMEM((max(len(rounds), 1),) + block, wire),
            pltpu.VMEM((copies,) + block, wire),
            pltpu.VMEM(block, wire),
            pltpu.VMEM(block, wire),
            pltpu.SemaphoreType.DMA((copies + 2,)),
            pltpu.SemaphoreType.DMA((copies + 2,)),
        ],
        compiler_params=pltpu.CompilerParams(collective_id=1 if reverse else 0, has_side_effects=True),
    )(shard)


def body(queries, keys, values, hazard_weight, log_base, time_bin, observed, task_label):
    highest = lax.Precision.HIGHEST
    three_pass = lax.Precision.HIGH
    f32 = jnp.float32
    rows_here = queries.shape[0]
    width_here = queries.shape[1]
    heads_here = width_here // HEAD_DIM
    tasks_here = hazard_weight.shape[1]
    shape_three = (rows_here, heads_here, HEAD_DIM)
    query_rows = queries.reshape(shape_three)
    key_rows = keys.reshape(shape_three)
    value_rows = values.reshape(shape_three)
    causal = jnp.tril(jnp.ones((rows_here, rows_here), f32))
    local_state = jnp.einsum("thd,the->hde", key_rows, value_rows, preferred_element_type=f32)
    prefix = exclusive_scan(local_state, "seq")
    scores = jnp.einsum("thd,shd->hts", query_rows, key_rows, preferred_element_type=f32) * causal
    raw_out = jnp.einsum(
        "hts,she->the", scores, value_rows, precision=three_pass, preferred_element_type=f32
    )
    raw_out = raw_out + jnp.einsum(
        "thd,hde->the", query_rows, prefix, precision=three_pass, preferred_element_type=f32
    )
    root_mean = jnp.sqrt(jnp.mean(raw_out * raw_out, axis=-1, keepdims=True) + norm_eps)
    normed = raw_out / root_mean
    hidden = normed.astype(jnp.bfloat16).reshape(rows_here, width_here)
    head_count = lax.axis_size("head")
    head_index = lax.axis_index("head")

    def shifted(x, k):
        return lax.ppermute(x, "head", [(m, (m + k) % head_count) for m in range(head_count)])

    def weight_rows(owner):
        return lax.dynamic_slice_in_dim(hazard_weight, owner * width_here, width_here, 0)

    log_rate = jnp.dot(hidden, weight_rows(head_index), preferred_element_type=f32)
    for k in range(1, head_count):
        log_rate = log_rate + jnp.dot(
            shifted(hidden, k),
            weight_rows((head_index - k + head_count) % head_count),
            preferred_element_type=f32,
        )
    offset = head_index * tasks_here
    cum_base = jnp.cumsum(jnp.exp(log_base), axis=0)
    bin_hot = (time_bin[:, None] == jnp.arange(BINS, dtype=jnp.int32)[None, :]).astype(f32)
    base_rows = jnp.dot(bin_hot, log_base, precision=highest)
    cum_rows = jnp.dot(bin_hot, cum_base, precision=highest)
    hazard = jnp.exp(log_rate) * cum_rows
    columns = offset + jnp.arange(tasks_here, dtype=jnp.int32)
    label_hit = (task_label[:, None] == columns[None, :]).astype(f32)
    event_flag = observed.astype(f32)
    partial_value = jnp.sum(hazard, axis=1) - event_flag * jnp.sum(
        label_hit * (log_rate + base_rows), axis=1
    )
    dlogit = (grad_scale * (hazard - event_flag[:, None] * label_hit)).astype(jnp.bfloat16)
    def block_term(owner):
        return lax.dot_general(
            dlogit, weight_rows(owner), (((1,), (1,)), ((), ())), preferred_element_type=f32
        )

    grad_hidden = block_term(head_index)
    event_loss = partial_value
    high = partial_value.astype(jnp.bfloat16)
    low = (partial_value - high.astype(f32)).astype(jnp.bfloat16)
    rows_extra = jnp.zeros((8, width_here), jnp.bfloat16)
    rows_extra = rows_extra.at[0, :rows_here].set(high).at[1, :rows_here].set(low)
    for k in range(1, head_count):
        sent = block_term((head_index + k) % head_count).astype(jnp.bfloat16)
        got = shifted(jnp.concatenate([sent, rows_extra], axis=0), k)
        grad_hidden = grad_hidden + got[:rows_here].astype(f32)
        event_loss = event_loss + (
            got[rows_here, :rows_here].astype(f32) + got[rows_here + 1, :rows_here].astype(f32)
        )
    grad_norm_in = grad_hidden.reshape(shape_three)
    grad_raw = (
        grad_norm_in - normed * jnp.mean(normed * grad_norm_in, axis=-1, keepdims=True)
    ) / root_mean
    grad_out = grad_raw.astype(jnp.bfloat16)
    local_adjoint = jnp.einsum("thd,the->hde", query_rows, grad_out, preferred_element_type=f32)
    suffix = exclusive_scan(local_adjoint, "seq", reverse=True)
    back_scores = (
        jnp.einsum("the,she->hts", grad_out, value_rows, preferred_element_type=f32) * causal
    )
    grad_query = jnp.einsum(
        "hts,shd->thd", back_scores, key_rows, precision=three_pass, preferred_element_type=f32
    )
    grad_query = grad_query + jnp.einsum(
        "the,hde->thd", grad_out, prefix, precision=three_pass, preferred_element_type=f32
    )
    grad_key = jnp.einsum(
        "hts,thd->shd", back_scores, query_rows, precision=three_pass, preferred_element_type=f32
    )
    grad_key = grad_key + jnp.einsum(
        "she,hde->shd", value_rows, suffix, precision=three_pass, preferred_element_type=f32
    )
    grad_value = jnp.einsum(
        "hts,the->she", scores, grad_out, precision=three_pass, preferred_element_type=f32
    )
    grad_value = grad_value + jnp.einsum(
        "shd,hde->she", key_rows, suffix, precision=three_pass, preferred_element_type=f32
    )
    grad_queries = grad_query.reshape(rows_here, width_here).astype(jnp.bfloat16)
    grad_keys = grad_key.reshape(rows_here, width_here).astype(jnp.bfloat16)
    grad_values = grad_value.reshape(rows_here, width_here).astype(jnp.bfloat16)
    return (grad_queries, grad_keys, grad_values, event_loss)


def solution(mesh):
    placed = (
        P("seq", "head"),
        P("seq", "head"),
        P("seq", "head"),
        P(None, "head"),
        P(None, "head"),
        P("seq"),
        P("seq"),
        P("seq"),
    )
    return jax.shard_map(
        body,
        mesh=mesh,
        in_specs=placed,
        out_specs=(P("seq", "head"), P("seq", "head"), P("seq", "head"), P("seq")),
        check_vma=False,
    )
```

```python
import functools

import jax
import jax.numpy as jnp
from jax import lax
from jax.experimental import pallas as pl
from jax.experimental.pallas import tpu as pltpu
from jax.sharding import PartitionSpec as P

HEAD_DIM = 128
BINS = 32
MESH = pl.DeviceIdType.MESH


norm_eps = 1e-06
grad_scale = 64.0


def scan_kernel(reverse, count, state_ref, out_ref, other, running, exclusive, outgoing, arrived, handed, partner,
                send_sems, recv_sems):
    me = lax.axis_index("seq")
    head = lax.axis_index("head")
    core = me % 2
    mate = me + 1 - 2 * core
    half = exclusive.shape[0]
    wire = outgoing.dtype
    first = scan_rounds(count)
    turn = min(2, len(first) - 1)
    second = first[len(first) - turn:] + first[:len(first) - turn]
    width = max(len(group) for group in first)
    rounds = list(range(len(first)))
    step = -1 if reverse else 1
    flat = []
    targets, sources, sends, receives = [], [], [], []
    for r in rounds:
        for s in range(width):
            flat.append((r, s))
            d0 = first[r][s] if s < len(first[r]) else 0
            d1 = second[r][s] if s < len(second[r]) else 0
            distance = jnp.where(core == 0, d0, d1)
            used = (distance > 0)
            target = me + step * distance
            source = me - step * distance
            targets.append(target)
            sources.append(source)
            sends.append(used & (target >= 0) & (target < count))
            receives.append(used & (source >= 0) & (source < count))

    barrier = pltpu.get_barrier_semaphore()
    pl.semaphore_signal(barrier, 1, device_id=(mate, head), device_id_type=MESH)
    expected = jnp.int32(1)
    for target, source, send, receive in zip(targets, sources, sends, receives):
        @pl.when(send)
        def _():
            pl.semaphore_signal(barrier, 1, device_id=(target, head), device_id_type=MESH)

        @pl.when(receive)
        def _():
            pl.semaphore_signal(barrier, 1, device_id=(source, head), device_id_type=MESH)

        expected = expected + send.astype(jnp.int32) + receive.astype(jnp.int32)
    pl.semaphore_wait(barrier, expected)

    swap = pltpu.make_async_remote_copy(
        state_ref, other, send_sems.at[0], recv_sems.at[0], device_id=(mate, head), device_id_type=MESH
    )
    swap.start()
    swap.wait()
    mine = pl.ds(core * half, half)
    running[...] = state_ref[mine] + other[mine]
    exclusive[...] = jnp.zeros_like(exclusive)
    copies = []
    for r, group in enumerate(rounds):
        outgoing[r] = running[...].astype(wire)
        members = [c for c, (owner, _) in enumerate(flat) if owner == r]
        for c in members:
            copy = pltpu.make_async_remote_copy(
                outgoing.at[r], arrived.at[c], send_sems.at[c + 1], recv_sems.at[c + 1],
                device_id=(targets[c], head), device_id_type=MESH,
            )
            copies.append(copy)

            @pl.when(sends[c])
            def _():
                copy.start()

        for c in members:
            @pl.when(receives[c])
            def _():
                copies[c].wait_recv()
                got = arrived[c].astype(running.dtype)
                running[...] = running[...] + got
                exclusive[...] = exclusive[...] + got

    last = len(flat) + 1
    handed[...] = exclusive[...].astype(wire)
    back = pltpu.make_async_remote_copy(
        handed, partner, send_sems.at[last], recv_sems.at[last], device_id=(mate, head), device_id_type=MESH
    )
    back.start()
    for copy, send in zip(copies, sends):
        @pl.when(send)
        def _():
            copy.wait_send()
    back.wait()
    theirs = pl.ds((1 - core) * half, half)
    take_other = (core == 0) if reverse else (core == 1)

    @pl.when(take_other)
    def _():
        out_ref[mine] = exclusive[...] + other[mine]
        out_ref[theirs] = partner[...].astype(out_ref.dtype) + other[theirs]

    @pl.when(jnp.logical_not(take_other))
    def _():
        out_ref[mine] = exclusive[...]
        out_ref[theirs] = partner[...].astype(out_ref.dtype)


def scan_rounds(count):
    rounds = []
    distance = 2
    while distance < count:
        rounds.append([distance])
        distance *= 2
    return rounds


def exclusive_scan(shard, axis, reverse=False, wire=jnp.float32):
    count = lax.axis_size(axis)
    heads, rows, cols = shard.shape
    half = heads // 2
    rounds = scan_rounds(count)
    copies = max(len(rounds), 1)
    block = (half, rows, cols)
    return pl.pallas_call(
        functools.partial(scan_kernel, reverse, count),
        out_shape=jax.ShapeDtypeStruct(shard.shape, shard.dtype),
        in_specs=[pl.BlockSpec(memory_space=pltpu.VMEM)],
        out_specs=pl.BlockSpec(memory_space=pltpu.VMEM),
        scratch_shapes=[
            pltpu.VMEM((heads, rows, cols), shard.dtype),
            pltpu.VMEM(block, shard.dtype),
            pltpu.VMEM(block, shard.dtype),
            pltpu.VMEM((copies,) + block, wire),
            pltpu.VMEM((copies,) + block, wire),
            pltpu.VMEM(block, wire),
            pltpu.VMEM(block, wire),
            pltpu.SemaphoreType.DMA((copies + 2,)),
            pltpu.SemaphoreType.DMA((copies + 2,)),
        ],
        compiler_params=pltpu.CompilerParams(collective_id=1 if reverse else 0, has_side_effects=True),
    )(shard)


def body(queries, keys, values, hazard_weight, log_base, time_bin, observed, task_label):
    highest = lax.Precision.HIGHEST
    three_pass = lax.Precision.HIGH
    f32 = jnp.float32
    rows_here = queries.shape[0]
    width_here = queries.shape[1]
    heads_here = width_here // HEAD_DIM
    tasks_here = hazard_weight.shape[1]
    shape_three = (rows_here, heads_here, HEAD_DIM)
    query_rows = queries.reshape(shape_three)
    key_rows = keys.reshape(shape_three)
    value_rows = values.reshape(shape_three)
    causal = jnp.tril(jnp.ones((rows_here, rows_here), f32))
    local_state = jnp.einsum("thd,the->hde", key_rows, value_rows, preferred_element_type=f32)
    prefix = exclusive_scan(local_state, "seq")
    scores = jnp.einsum("thd,shd->hts", query_rows, key_rows, preferred_element_type=f32) * causal
    raw_out = jnp.einsum(
        "hts,she->the", scores, value_rows, precision=three_pass, preferred_element_type=f32
    )
    raw_out = raw_out + jnp.einsum(
        "thd,hde->the", query_rows, prefix, precision=three_pass, preferred_element_type=f32
    )
    root_mean = jnp.sqrt(jnp.mean(raw_out * raw_out, axis=-1, keepdims=True) + norm_eps)
    normed = raw_out / root_mean
    hidden = normed.astype(jnp.bfloat16).reshape(rows_here, width_here)
    head_count = lax.axis_size("head")
    head_index = lax.axis_index("head")

    def shifted(x, k):
        return lax.ppermute(x, "head", [(m, (m + k) % head_count) for m in range(head_count)])

    def weight_rows(owner):
        return lax.dynamic_slice_in_dim(hazard_weight, owner * width_here, width_here, 0)

    log_rate = jnp.dot(hidden, weight_rows(head_index), preferred_element_type=f32)
    for k in range(1, head_count):
        log_rate = log_rate + jnp.dot(
            shifted(hidden, k),
            weight_rows((head_index - k + head_count) % head_count),
            preferred_element_type=f32,
        )
    offset = head_index * tasks_here
    cum_base = jnp.cumsum(jnp.exp(log_base), axis=0)
    bin_hot = (time_bin[:, None] == jnp.arange(BINS, dtype=jnp.int32)[None, :]).astype(f32)
    base_rows = jnp.dot(bin_hot, log_base, precision=highest)
    cum_rows = jnp.dot(bin_hot, cum_base, precision=highest)
    hazard = jnp.exp(log_rate) * cum_rows
    columns = offset + jnp.arange(tasks_here, dtype=jnp.int32)
    label_hit = (task_label[:, None] == columns[None, :]).astype(f32)
    event_flag = observed.astype(f32)
    partial_value = jnp.sum(hazard, axis=1) - event_flag * jnp.sum(
        label_hit * (log_rate + base_rows), axis=1
    )
    dlogit = (grad_scale * (hazard - event_flag[:, None] * label_hit)).astype(jnp.bfloat16)
    def block_term(owner):
        return lax.dot_general(
            dlogit, weight_rows(owner), (((1,), (1,)), ((), ())), preferred_element_type=f32
        )

    grad_hidden = block_term(head_index)
    event_loss = partial_value
    for k in range(1, head_count):
        sent = block_term((head_index + k) % head_count).astype(jnp.bfloat16)
        grad_hidden = grad_hidden + shifted(sent, k).astype(f32)
        event_loss = event_loss + shifted(partial_value, k)
    grad_norm_in = grad_hidden.reshape(shape_three)
    grad_raw = (
        grad_norm_in - normed * jnp.mean(normed * grad_norm_in, axis=-1, keepdims=True)
    ) / root_mean
    grad_out = grad_raw.astype(jnp.bfloat16)
    local_adjoint = jnp.einsum("thd,the->hde", query_rows, grad_out, preferred_element_type=f32)
    suffix = exclusive_scan(local_adjoint, "seq", reverse=True)
    back_scores = (
        jnp.einsum("the,she->hts", grad_out, value_rows, preferred_element_type=f32) * causal
    )
    grad_query = jnp.einsum(
        "hts,shd->thd", back_scores, key_rows, precision=three_pass, preferred_element_type=f32
    )
    grad_query = grad_query + jnp.einsum(
        "the,hde->thd", grad_out, prefix, precision=three_pass, preferred_element_type=f32
    )
    grad_key = jnp.einsum(
        "hts,thd->shd", back_scores, query_rows, precision=three_pass, preferred_element_type=f32
    )
    grad_key = grad_key + jnp.einsum(
        "she,hde->shd", value_rows, suffix, precision=three_pass, preferred_element_type=f32
    )
    grad_value = jnp.einsum(
        "hts,the->she", scores, grad_out, precision=three_pass, preferred_element_type=f32
    )
    grad_value = grad_value + jnp.einsum(
        "shd,hde->she", key_rows, suffix, precision=three_pass, preferred_element_type=f32
    )
    grad_queries = grad_query.reshape(rows_here, width_here).astype(jnp.bfloat16)
    grad_keys = grad_key.reshape(rows_here, width_here).astype(jnp.bfloat16)
    grad_values = grad_value.reshape(rows_here, width_here).astype(jnp.bfloat16)
    return (grad_queries, grad_keys, grad_values, event_loss)


def solution(mesh):
    placed = (
        P("seq", "head"),
        P("seq", "head"),
        P("seq", "head"),
        P(None, "head"),
        P(None, "head"),
        P("seq"),
        P("seq"),
        P("seq"),
    )
    return jax.shard_map(
        body,
        mesh=mesh,
        in_specs=placed,
        out_specs=(P("seq", "head"), P("seq", "head"), P("seq", "head"), P("seq")),
        check_vma=False,
    )
```

```python
import functools

import jax
import jax.numpy as jnp
from jax import lax
from jax.experimental import pallas as pl
from jax.experimental.pallas import tpu as pltpu
from jax.sharding import PartitionSpec as P

HEAD_DIM = 128
BINS = 32
MESH = pl.DeviceIdType.MESH


norm_eps = 1e-06
grad_scale = 64.0


def scan_kernel(reverse, count, state_ref, out_ref, other, running, exclusive, outgoing, arrived, handed, partner,
                send_sems, recv_sems):
    me = lax.axis_index("seq")
    head = lax.axis_index("head")
    core = me % 2
    mate = me + 1 - 2 * core
    half = exclusive.shape[0]
    wire = outgoing.dtype
    rounds = scan_rounds(count)
    step = -1 if reverse else 1
    flat = [(r, d) for r, group in enumerate(rounds) for d in group]
    targets = [me + step * d for _, d in flat]
    sources = [me - step * d for _, d in flat]
    sends = [(t >= 0) & (t < count) for t in targets]
    receives = [(s >= 0) & (s < count) for s in sources]

    barrier = pltpu.get_barrier_semaphore()
    pl.semaphore_signal(barrier, 1, device_id=(mate, head), device_id_type=MESH)
    expected = jnp.int32(1)
    for target, source, send, receive in zip(targets, sources, sends, receives):
        @pl.when(send)
        def _():
            pl.semaphore_signal(barrier, 1, device_id=(target, head), device_id_type=MESH)

        @pl.when(receive)
        def _():
            pl.semaphore_signal(barrier, 1, device_id=(source, head), device_id_type=MESH)

        expected = expected + send.astype(jnp.int32) + receive.astype(jnp.int32)
    pl.semaphore_wait(barrier, expected)

    swap = pltpu.make_async_remote_copy(
        state_ref, other, send_sems.at[0], recv_sems.at[0], device_id=(mate, head), device_id_type=MESH
    )
    swap.start()
    swap.wait()
    mine = pl.ds(core * half, half)
    running[...] = state_ref[mine] + other[mine]
    exclusive[...] = jnp.zeros_like(exclusive)
    copies = []
    for r, group in enumerate(rounds):
        outgoing[r] = running[...].astype(wire)
        members = [c for c, (owner, _) in enumerate(flat) if owner == r]
        for c in members:
            copy = pltpu.make_async_remote_copy(
                outgoing.at[r], arrived.at[c], send_sems.at[c + 1], recv_sems.at[c + 1],
                device_id=(targets[c], head), device_id_type=MESH,
            )
            copies.append(copy)

            @pl.when(sends[c])
            def _():
                copy.start()

        for c in members:
            @pl.when(receives[c])
            def _():
                copies[c].wait_recv()
                got = arrived[c].astype(running.dtype)
                running[...] = running[...] + got
                exclusive[...] = exclusive[...] + got

    last = len(flat) + 1
    handed[...] = exclusive[...].astype(wire)
    back = pltpu.make_async_remote_copy(
        handed, partner, send_sems.at[last], recv_sems.at[last], device_id=(mate, head), device_id_type=MESH
    )
    back.start()
    for copy, send in zip(copies, sends):
        @pl.when(send)
        def _():
            copy.wait_send()
    back.wait()
    theirs = pl.ds((1 - core) * half, half)
    take_other = (core == 0) if reverse else (core == 1)

    @pl.when(take_other)
    def _():
        out_ref[mine] = exclusive[...] + other[mine]
        out_ref[theirs] = partner[...].astype(out_ref.dtype) + other[theirs]

    @pl.when(jnp.logical_not(take_other))
    def _():
        out_ref[mine] = exclusive[...]
        out_ref[theirs] = partner[...].astype(out_ref.dtype)


def scan_rounds(count):
    chips = count // 2
    rounds = []
    window = 1
    while window < chips:
        if chips == 4 * window:
            rounds.append([2 * window, 4 * window, 6 * window])
            window *= 4
        else:
            rounds.append([2 * window])
            window *= 2
    return rounds


def exclusive_scan(shard, axis, reverse=False, wire=jnp.float32):
    count = lax.axis_size(axis)
    heads, rows, cols = shard.shape
    half = heads // 2
    rounds = scan_rounds(count)
    copies = max(sum(len(group) for group in rounds), 1)
    block = (half, rows, cols)
    return pl.pallas_call(
        functools.partial(scan_kernel, reverse, count),
        out_shape=jax.ShapeDtypeStruct(shard.shape, shard.dtype),
        in_specs=[pl.BlockSpec(memory_space=pltpu.VMEM)],
        out_specs=pl.BlockSpec(memory_space=pltpu.VMEM),
        scratch_shapes=[
            pltpu.VMEM((heads, rows, cols), shard.dtype),
            pltpu.VMEM(block, shard.dtype),
            pltpu.VMEM(block, shard.dtype),
            pltpu.VMEM((max(len(rounds), 1),) + block, wire),
            pltpu.VMEM((copies,) + block, wire),
            pltpu.VMEM(block, wire),
            pltpu.VMEM(block, wire),
            pltpu.SemaphoreType.DMA((copies + 2,)),
            pltpu.SemaphoreType.DMA((copies + 2,)),
        ],
        compiler_params=pltpu.CompilerParams(collective_id=1 if reverse else 0, has_side_effects=True),
    )(shard)


def body(queries, keys, values, hazard_weight, log_base, time_bin, observed, task_label):
    highest = lax.Precision.HIGHEST
    three_pass = lax.Precision.HIGH
    f32 = jnp.float32
    rows_here = queries.shape[0]
    width_here = queries.shape[1]
    heads_here = width_here // HEAD_DIM
    tasks_here = hazard_weight.shape[1]
    shape_three = (rows_here, heads_here, HEAD_DIM)
    query_rows = queries.reshape(shape_three)
    key_rows = keys.reshape(shape_three)
    value_rows = values.reshape(shape_three)
    causal = jnp.tril(jnp.ones((rows_here, rows_here), f32))
    local_state = jnp.einsum("thd,the->hde", key_rows, value_rows, preferred_element_type=f32)
    prefix = exclusive_scan(local_state, "seq")
    scores = jnp.einsum("thd,shd->hts", query_rows, key_rows, preferred_element_type=f32) * causal
    raw_out = jnp.einsum(
        "hts,she->the", scores, value_rows, precision=three_pass, preferred_element_type=f32
    )
    raw_out = raw_out + jnp.einsum(
        "thd,hde->the", query_rows, prefix, precision=three_pass, preferred_element_type=f32
    )
    root_mean = jnp.sqrt(jnp.mean(raw_out * raw_out, axis=-1, keepdims=True) + norm_eps)
    normed = raw_out / root_mean
    hidden = normed.astype(jnp.bfloat16).reshape(rows_here, width_here)
    head_count = lax.axis_size("head")
    head_index = lax.axis_index("head")

    def shifted(x, k):
        return lax.ppermute(x, "head", [(m, (m + k) % head_count) for m in range(head_count)])

    def weight_rows(owner):
        return lax.dynamic_slice_in_dim(hazard_weight, owner * width_here, width_here, 0)

    log_rate = jnp.dot(hidden, weight_rows(head_index), preferred_element_type=f32)
    for k in range(1, head_count):
        log_rate = log_rate + jnp.dot(
            shifted(hidden, k),
            weight_rows((head_index - k + head_count) % head_count),
            preferred_element_type=f32,
        )
    offset = head_index * tasks_here
    cum_base = jnp.cumsum(jnp.exp(log_base), axis=0)
    bin_hot = (time_bin[:, None] == jnp.arange(BINS, dtype=jnp.int32)[None, :]).astype(f32)
    base_rows = jnp.dot(bin_hot, log_base, precision=highest)
    cum_rows = jnp.dot(bin_hot, cum_base, precision=highest)
    hazard = jnp.exp(log_rate) * cum_rows
    columns = offset + jnp.arange(tasks_here, dtype=jnp.int32)
    label_hit = (task_label[:, None] == columns[None, :]).astype(f32)
    event_flag = observed.astype(f32)
    partial_value = jnp.sum(hazard, axis=1) - event_flag * jnp.sum(
        label_hit * (log_rate + base_rows), axis=1
    )
    dlogit = (grad_scale * (hazard - event_flag[:, None] * label_hit)).astype(jnp.bfloat16)
    def block_term(owner):
        return lax.dot_general(
            dlogit, weight_rows(owner), (((1,), (1,)), ((), ())), preferred_element_type=f32
        )

    grad_hidden = block_term(head_index)
    event_loss = partial_value
    for k in range(1, head_count):
        event_loss = event_loss + shifted(partial_value, k)
    if head_count == 4:
        ahead = shifted(block_term((head_index + 1) % 4).astype(jnp.bfloat16), 1)
        relay = shifted(block_term((head_index + 2) % 4).astype(jnp.bfloat16), 3)
        carried = (relay.astype(f32) + block_term((head_index + 3) % 4)).astype(jnp.bfloat16)
        grad_hidden = grad_hidden + ahead.astype(f32) + shifted(carried, 3).astype(f32)
    else:
        for k in range(1, head_count):
            sent = block_term((head_index + k) % head_count).astype(jnp.bfloat16)
            grad_hidden = grad_hidden + shifted(sent, k).astype(f32)
    grad_norm_in = grad_hidden.reshape(shape_three)
    grad_raw = (
        grad_norm_in - normed * jnp.mean(normed * grad_norm_in, axis=-1, keepdims=True)
    ) / root_mean
    grad_out = grad_raw.astype(jnp.bfloat16)
    local_adjoint = jnp.einsum("thd,the->hde", query_rows, grad_out, preferred_element_type=f32)
    suffix = exclusive_scan(local_adjoint, "seq", reverse=True)
    back_scores = (
        jnp.einsum("the,she->hts", grad_out, value_rows, preferred_element_type=f32) * causal
    )
    grad_query = jnp.einsum(
        "hts,shd->thd", back_scores, key_rows, precision=three_pass, preferred_element_type=f32
    )
    grad_query = grad_query + jnp.einsum(
        "the,hde->thd", grad_out, prefix, precision=three_pass, preferred_element_type=f32
    )
    grad_key = jnp.einsum(
        "hts,thd->shd", back_scores, query_rows, precision=three_pass, preferred_element_type=f32
    )
    grad_key = grad_key + jnp.einsum(
        "she,hde->shd", value_rows, suffix, precision=three_pass, preferred_element_type=f32
    )
    grad_value = jnp.einsum(
        "hts,the->she", scores, grad_out, precision=three_pass, preferred_element_type=f32
    )
    grad_value = grad_value + jnp.einsum(
        "shd,hde->she", key_rows, suffix, precision=three_pass, preferred_element_type=f32
    )
    grad_queries = grad_query.reshape(rows_here, width_here).astype(jnp.bfloat16)
    grad_keys = grad_key.reshape(rows_here, width_here).astype(jnp.bfloat16)
    grad_values = grad_value.reshape(rows_here, width_here).astype(jnp.bfloat16)
    return (grad_queries, grad_keys, grad_values, event_loss)


def solution(mesh):
    placed = (
        P("seq", "head"),
        P("seq", "head"),
        P("seq", "head"),
        P(None, "head"),
        P(None, "head"),
        P("seq"),
        P("seq"),
        P("seq"),
    )
    return jax.shard_map(
        body,
        mesh=mesh,
        in_specs=placed,
        out_specs=(P("seq", "head"), P("seq", "head"), P("seq", "head"), P("seq")),
        check_vma=False,
    )
```

```python
import functools

import jax
import jax.numpy as jnp
from jax import lax
from jax.experimental import pallas as pl
from jax.experimental.pallas import tpu as pltpu
from jax.sharding import PartitionSpec as P

HEAD_DIM = 128
BINS = 32
MESH = pl.DeviceIdType.MESH


norm_eps = 1e-06
grad_scale = 64.0


def scan_kernel(reverse, count, state_ref, out_ref, other, running, exclusive, outgoing, arrived, handed, partner,
                send_sems, recv_sems):
    me = lax.axis_index("seq")
    head = lax.axis_index("head")
    core = me % 2
    mate = me + 1 - 2 * core
    half = exclusive.shape[0]
    wire = outgoing.dtype
    rounds = scan_rounds(count)
    step = -1 if reverse else 1
    flat = [(r, d) for r, group in enumerate(rounds) for d in group]
    targets = [me + step * d for _, d in flat]
    sources = [me - step * d for _, d in flat]
    sends = [(t >= 0) & (t < count) for t in targets]
    receives = [(s >= 0) & (s < count) for s in sources]

    barrier = pltpu.get_barrier_semaphore()
    pl.semaphore_signal(barrier, 1, device_id=(mate, head), device_id_type=MESH)
    expected = jnp.int32(1)
    for target, source, send, receive in zip(targets, sources, sends, receives):
        @pl.when(send)
        def _():
            pl.semaphore_signal(barrier, 1, device_id=(target, head), device_id_type=MESH)

        @pl.when(receive)
        def _():
            pl.semaphore_signal(barrier, 1, device_id=(source, head), device_id_type=MESH)

        expected = expected + send.astype(jnp.int32) + receive.astype(jnp.int32)
    pl.semaphore_wait(barrier, expected)

    swap = pltpu.make_async_remote_copy(
        state_ref, other, send_sems.at[0], recv_sems.at[0], device_id=(mate, head), device_id_type=MESH
    )
    swap.start()
    swap.wait()
    mine = pl.ds(core * half, half)
    running[...] = state_ref[mine] + other[mine]
    exclusive[...] = jnp.zeros_like(exclusive)
    copies = []
    for r, group in enumerate(rounds):
        outgoing[r] = running[...].astype(wire)
        members = [c for c, (owner, _) in enumerate(flat) if owner == r]
        for c in members:
            copy = pltpu.make_async_remote_copy(
                outgoing.at[r], arrived.at[c], send_sems.at[c + 1], recv_sems.at[c + 1],
                device_id=(targets[c], head), device_id_type=MESH,
            )
            copies.append(copy)

            @pl.when(sends[c])
            def _():
                copy.start()

        for c in members:
            @pl.when(receives[c])
            def _():
                copies[c].wait_recv()
                got = arrived[c].astype(running.dtype)
                running[...] = running[...] + got
                exclusive[...] = exclusive[...] + got

    last = len(flat) + 1
    handed[...] = exclusive[...].astype(wire)
    back = pltpu.make_async_remote_copy(
        handed, partner, send_sems.at[last], recv_sems.at[last], device_id=(mate, head), device_id_type=MESH
    )
    back.start()
    for copy, send in zip(copies, sends):
        @pl.when(send)
        def _():
            copy.wait_send()
    back.wait()
    theirs = pl.ds((1 - core) * half, half)
    take_other = (core == 0) if reverse else (core == 1)

    @pl.when(take_other)
    def _():
        out_ref[mine] = exclusive[...] + other[mine]
        out_ref[theirs] = partner[...].astype(out_ref.dtype) + other[theirs]

    @pl.when(jnp.logical_not(take_other))
    def _():
        out_ref[mine] = exclusive[...]
        out_ref[theirs] = partner[...].astype(out_ref.dtype)


def scan_rounds(count):
    chips = count // 2
    rounds = []
    window = 1
    while window < chips:
        if chips == 4 * window:
            rounds.append([2 * window, 4 * window, 6 * window])
            window *= 4
        else:
            rounds.append([2 * window])
            window *= 2
    return rounds


def exclusive_scan(shard, axis, reverse=False, wire=jnp.float32):
    count = lax.axis_size(axis)
    heads, rows, cols = shard.shape
    half = heads // 2
    rounds = scan_rounds(count)
    copies = max(sum(len(group) for group in rounds), 1)
    block = (half, rows, cols)
    return pl.pallas_call(
        functools.partial(scan_kernel, reverse, count),
        out_shape=jax.ShapeDtypeStruct(shard.shape, shard.dtype),
        in_specs=[pl.BlockSpec(memory_space=pltpu.VMEM)],
        out_specs=pl.BlockSpec(memory_space=pltpu.VMEM),
        scratch_shapes=[
            pltpu.VMEM((heads, rows, cols), shard.dtype),
            pltpu.VMEM(block, shard.dtype),
            pltpu.VMEM(block, shard.dtype),
            pltpu.VMEM((max(len(rounds), 1),) + block, wire),
            pltpu.VMEM((copies,) + block, wire),
            pltpu.VMEM(block, wire),
            pltpu.VMEM(block, wire),
            pltpu.SemaphoreType.DMA((copies + 2,)),
            pltpu.SemaphoreType.DMA((copies + 2,)),
        ],
        compiler_params=pltpu.CompilerParams(collective_id=1 if reverse else 0, has_side_effects=True),
    )(shard)


def body(queries, keys, values, hazard_weight, log_base, time_bin, observed, task_label):
    highest = lax.Precision.HIGHEST
    three_pass = lax.Precision.HIGH
    f32 = jnp.float32
    rows_here = queries.shape[0]
    width_here = queries.shape[1]
    heads_here = width_here // HEAD_DIM
    tasks_here = hazard_weight.shape[1]
    shape_three = (rows_here, heads_here, HEAD_DIM)
    query_rows = queries.reshape(shape_three)
    key_rows = keys.reshape(shape_three)
    value_rows = values.reshape(shape_three)
    causal = jnp.tril(jnp.ones((rows_here, rows_here), f32))
    local_state = jnp.einsum("thd,the->hde", key_rows, value_rows, preferred_element_type=f32)
    prefix = exclusive_scan(local_state, "seq")
    scores = jnp.einsum("thd,shd->hts", query_rows, key_rows, preferred_element_type=f32) * causal
    raw_out = jnp.einsum(
        "hts,she->the", scores, value_rows, precision=three_pass, preferred_element_type=f32
    )
    raw_out = raw_out + jnp.einsum(
        "thd,hde->the", query_rows, prefix, precision=three_pass, preferred_element_type=f32
    )
    root_mean = jnp.sqrt(jnp.mean(raw_out * raw_out, axis=-1, keepdims=True) + norm_eps)
    normed = raw_out / root_mean
    hidden = normed.astype(jnp.bfloat16).reshape(rows_here, width_here)
    head_count = lax.axis_size("head")
    head_index = lax.axis_index("head")

    def shifted(x, k):
        return lax.ppermute(x, "head", [(m, (m + k) % head_count) for m in range(head_count)])

    def weight_rows(owner):
        return lax.dynamic_slice_in_dim(hazard_weight, owner * width_here, width_here, 0)

    log_rate = jnp.dot(hidden, weight_rows(head_index), preferred_element_type=f32)
    if head_count == 4:
        behind = shifted(hidden, 1)
        received = {1: behind, 2: shifted(behind, 1), 3: shifted(hidden, 3)}
    else:
        received = {k: shifted(hidden, k) for k in range(1, head_count)}
    for k in range(1, head_count):
        log_rate = log_rate + jnp.dot(
            received[k],
            weight_rows((head_index - k + head_count) % head_count),
            preferred_element_type=f32,
        )
    offset = head_index * tasks_here
    cum_base = jnp.cumsum(jnp.exp(log_base), axis=0)
    bin_hot = (time_bin[:, None] == jnp.arange(BINS, dtype=jnp.int32)[None, :]).astype(f32)
    base_rows = jnp.dot(bin_hot, log_base, precision=highest)
    cum_rows = jnp.dot(bin_hot, cum_base, precision=highest)
    hazard = jnp.exp(log_rate) * cum_rows
    columns = offset + jnp.arange(tasks_here, dtype=jnp.int32)
    label_hit = (task_label[:, None] == columns[None, :]).astype(f32)
    event_flag = observed.astype(f32)
    partial_value = jnp.sum(hazard, axis=1) - event_flag * jnp.sum(
        label_hit * (log_rate + base_rows), axis=1
    )
    dlogit = (grad_scale * (hazard - event_flag[:, None] * label_hit)).astype(jnp.bfloat16)
    def block_term(owner):
        return lax.dot_general(
            dlogit, weight_rows(owner), (((1,), (1,)), ((), ())), preferred_element_type=f32
        )

    grad_hidden = block_term(head_index)
    event_loss = partial_value
    for k in range(1, head_count):
        event_loss = event_loss + shifted(partial_value, k)
    if head_count == 4:
        ahead = shifted(block_term((head_index + 1) % 4).astype(jnp.bfloat16), 1)
        relay = shifted(block_term((head_index + 2) % 4).astype(jnp.bfloat16), 3)
        carried = (relay.astype(f32) + block_term((head_index + 3) % 4)).astype(jnp.bfloat16)
        grad_hidden = grad_hidden + ahead.astype(f32) + shifted(carried, 3).astype(f32)
    else:
        for k in range(1, head_count):
            sent = block_term((head_index + k) % head_count).astype(jnp.bfloat16)
            grad_hidden = grad_hidden + shifted(sent, k).astype(f32)
    grad_norm_in = grad_hidden.reshape(shape_three)
    grad_raw = (
        grad_norm_in - normed * jnp.mean(normed * grad_norm_in, axis=-1, keepdims=True)
    ) / root_mean
    grad_out = grad_raw.astype(jnp.bfloat16)
    local_adjoint = jnp.einsum("thd,the->hde", query_rows, grad_out, preferred_element_type=f32)
    suffix = exclusive_scan(local_adjoint, "seq", reverse=True)
    back_scores = (
        jnp.einsum("the,she->hts", grad_out, value_rows, preferred_element_type=f32) * causal
    )
    grad_query = jnp.einsum(
        "hts,shd->thd", back_scores, key_rows, precision=three_pass, preferred_element_type=f32
    )
    grad_query = grad_query + jnp.einsum(
        "the,hde->thd", grad_out, prefix, precision=three_pass, preferred_element_type=f32
    )
    grad_key = jnp.einsum(
        "hts,thd->shd", back_scores, query_rows, precision=three_pass, preferred_element_type=f32
    )
    grad_key = grad_key + jnp.einsum(
        "she,hde->shd", value_rows, suffix, precision=three_pass, preferred_element_type=f32
    )
    grad_value = jnp.einsum(
        "hts,the->she", scores, grad_out, precision=three_pass, preferred_element_type=f32
    )
    grad_value = grad_value + jnp.einsum(
        "shd,hde->she", key_rows, suffix, precision=three_pass, preferred_element_type=f32
    )
    grad_queries = grad_query.reshape(rows_here, width_here).astype(jnp.bfloat16)
    grad_keys = grad_key.reshape(rows_here, width_here).astype(jnp.bfloat16)
    grad_values = grad_value.reshape(rows_here, width_here).astype(jnp.bfloat16)
    return (grad_queries, grad_keys, grad_values, event_loss)


def solution(mesh):
    placed = (
        P("seq", "head"),
        P("seq", "head"),
        P("seq", "head"),
        P(None, "head"),
        P(None, "head"),
        P("seq"),
        P("seq"),
        P("seq"),
    )
    return jax.shard_map(
        body,
        mesh=mesh,
        in_specs=placed,
        out_specs=(P("seq", "head"), P("seq", "head"), P("seq", "head"), P("seq")),
        check_vma=False,
    )
```

```python
import functools

import jax
import jax.numpy as jnp
from jax import lax
from jax.experimental import pallas as pl
from jax.experimental.pallas import tpu as pltpu
from jax.sharding import PartitionSpec as P

HEAD_DIM = 128
BINS = 32
MESH = pl.DeviceIdType.MESH


norm_eps = 1e-06
grad_scale = 64.0


def scan_kernel(reverse, count, state_ref, out_ref, other, running, exclusive, outgoing, arrived, handed, partner,
                send_sems, recv_sems):
    me = lax.axis_index("seq")
    head = lax.axis_index("head")
    core = me % 2
    mate = me + 1 - 2 * core
    half = exclusive.shape[0]
    wire = outgoing.dtype
    rounds = scan_rounds(count)
    step = -1 if reverse else 1
    flat = [(r, d) for r, group in enumerate(rounds) for d in group]
    targets = [me + step * d for _, d in flat]
    sources = [me - step * d for _, d in flat]
    sends = [(t >= 0) & (t < count) for t in targets]
    receives = [(s >= 0) & (s < count) for s in sources]

    barrier = pltpu.get_barrier_semaphore()
    pl.semaphore_signal(barrier, 1, device_id=(mate, head), device_id_type=MESH)
    expected = jnp.int32(1)
    for target, source, send, receive in zip(targets, sources, sends, receives):
        @pl.when(send)
        def _():
            pl.semaphore_signal(barrier, 1, device_id=(target, head), device_id_type=MESH)

        @pl.when(receive)
        def _():
            pl.semaphore_signal(barrier, 1, device_id=(source, head), device_id_type=MESH)

        expected = expected + send.astype(jnp.int32) + receive.astype(jnp.int32)
    pl.semaphore_wait(barrier, expected)

    swap = pltpu.make_async_remote_copy(
        state_ref, other, send_sems.at[0], recv_sems.at[0], device_id=(mate, head), device_id_type=MESH
    )
    swap.start()
    swap.wait()
    mine = pl.ds(core * half, half)
    running[...] = state_ref[mine] + other[mine]
    exclusive[...] = jnp.zeros_like(exclusive)
    copies = []
    for r, group in enumerate(rounds):
        outgoing[r] = running[...].astype(wire)
        members = [c for c, (owner, _) in enumerate(flat) if owner == r]
        for c in members:
            copy = pltpu.make_async_remote_copy(
                outgoing.at[r], arrived.at[c], send_sems.at[c + 1], recv_sems.at[c + 1],
                device_id=(targets[c], head), device_id_type=MESH,
            )
            copies.append(copy)

            @pl.when(sends[c])
            def _():
                copy.start()

        for c in members:
            @pl.when(receives[c])
            def _():
                copies[c].wait_recv()
                got = arrived[c].astype(running.dtype)
                running[...] = running[...] + got
                exclusive[...] = exclusive[...] + got

    last = len(flat) + 1
    handed[...] = exclusive[...].astype(wire)
    back = pltpu.make_async_remote_copy(
        handed, partner, send_sems.at[last], recv_sems.at[last], device_id=(mate, head), device_id_type=MESH
    )
    back.start()
    for copy, send in zip(copies, sends):
        @pl.when(send)
        def _():
            copy.wait_send()
    back.wait()
    theirs = pl.ds((1 - core) * half, half)
    take_other = (core == 0) if reverse else (core == 1)

    @pl.when(take_other)
    def _():
        out_ref[mine] = exclusive[...] + other[mine]
        out_ref[theirs] = partner[...].astype(out_ref.dtype) + other[theirs]

    @pl.when(jnp.logical_not(take_other))
    def _():
        out_ref[mine] = exclusive[...]
        out_ref[theirs] = partner[...].astype(out_ref.dtype)


def scan_rounds(count):
    chips = count // 2
    rounds = []
    window = 1
    while window < chips:
        if chips == 4 * window:
            rounds.append([2 * window, 4 * window, 6 * window])
            window *= 4
        else:
            rounds.append([2 * window])
            window *= 2
    return rounds


def exclusive_scan(shard, axis, reverse=False, wire=jnp.float32):
    count = lax.axis_size(axis)
    heads, rows, cols = shard.shape
    half = heads // 2
    rounds = scan_rounds(count)
    copies = max(sum(len(group) for group in rounds), 1)
    block = (half, rows, cols)
    return pl.pallas_call(
        functools.partial(scan_kernel, reverse, count),
        out_shape=jax.ShapeDtypeStruct(shard.shape, shard.dtype),
        in_specs=[pl.BlockSpec(memory_space=pltpu.VMEM)],
        out_specs=pl.BlockSpec(memory_space=pltpu.VMEM),
        scratch_shapes=[
            pltpu.VMEM((heads, rows, cols), shard.dtype),
            pltpu.VMEM(block, shard.dtype),
            pltpu.VMEM(block, shard.dtype),
            pltpu.VMEM((max(len(rounds), 1),) + block, wire),
            pltpu.VMEM((copies,) + block, wire),
            pltpu.VMEM(block, wire),
            pltpu.VMEM(block, wire),
            pltpu.SemaphoreType.DMA((copies + 2,)),
            pltpu.SemaphoreType.DMA((copies + 2,)),
        ],
        compiler_params=pltpu.CompilerParams(collective_id=1 if reverse else 0, has_side_effects=True),
    )(shard)


def body(queries, keys, values, hazard_weight, log_base, time_bin, observed, task_label):
    highest = lax.Precision.HIGHEST
    three_pass = lax.Precision.HIGH
    f32 = jnp.float32
    rows_here = queries.shape[0]
    width_here = queries.shape[1]
    heads_here = width_here // HEAD_DIM
    tasks_here = hazard_weight.shape[1]
    shape_three = (rows_here, heads_here, HEAD_DIM)
    query_rows = queries.reshape(shape_three)
    key_rows = keys.reshape(shape_three)
    value_rows = values.reshape(shape_three)
    causal = jnp.tril(jnp.ones((rows_here, rows_here), f32))
    local_state = jnp.einsum("thd,the->hde", key_rows, value_rows, preferred_element_type=f32)
    prefix = exclusive_scan(local_state, "seq")
    scores = jnp.einsum("thd,shd->hts", query_rows, key_rows, preferred_element_type=f32) * causal
    raw_out = jnp.einsum(
        "hts,she->the", scores, value_rows, precision=three_pass, preferred_element_type=f32
    )
    raw_out = raw_out + jnp.einsum(
        "thd,hde->the", query_rows, prefix, precision=three_pass, preferred_element_type=f32
    )
    root_mean = jnp.sqrt(jnp.mean(raw_out * raw_out, axis=-1, keepdims=True) + norm_eps)
    normed = raw_out / root_mean
    hidden = normed.astype(jnp.bfloat16).reshape(rows_here, width_here)
    head_count = lax.axis_size("head")
    head_index = lax.axis_index("head")

    def shifted(x, k):
        return lax.ppermute(x, "head", [(m, (m + k) % head_count) for m in range(head_count)])

    def weight_rows(owner):
        return lax.dynamic_slice_in_dim(hazard_weight, owner * width_here, width_here, 0)

    log_rate = jnp.dot(hidden, weight_rows(head_index), preferred_element_type=f32)
    if head_count == 4:
        split = width_here // 2
        behind = shifted(hidden, 1)
        ahead = shifted(hidden, 3)
        far = (head_index + 2) % 4
        near_half = shifted(behind[:, :split], 1)
        other_half = shifted(ahead[:, split:], 3)
        far_rows = weight_rows(far)
        log_rate = log_rate + jnp.dot(
            behind, weight_rows((head_index + 3) % 4), preferred_element_type=f32
        )
        log_rate = log_rate + (
            jnp.dot(near_half, far_rows[:split], preferred_element_type=f32)
            + jnp.dot(other_half, far_rows[split:], preferred_element_type=f32)
        )
        log_rate = log_rate + jnp.dot(
            ahead, weight_rows((head_index + 1) % 4), preferred_element_type=f32
        )
    else:
        for k in range(1, head_count):
            log_rate = log_rate + jnp.dot(
                shifted(hidden, k),
                weight_rows((head_index - k + head_count) % head_count),
                preferred_element_type=f32,
            )
    offset = head_index * tasks_here
    cum_base = jnp.cumsum(jnp.exp(log_base), axis=0)
    bin_hot = (time_bin[:, None] == jnp.arange(BINS, dtype=jnp.int32)[None, :]).astype(f32)
    base_rows = jnp.dot(bin_hot, log_base, precision=highest)
    cum_rows = jnp.dot(bin_hot, cum_base, precision=highest)
    hazard = jnp.exp(log_rate) * cum_rows
    columns = offset + jnp.arange(tasks_here, dtype=jnp.int32)
    label_hit = (task_label[:, None] == columns[None, :]).astype(f32)
    event_flag = observed.astype(f32)
    partial_value = jnp.sum(hazard, axis=1) - event_flag * jnp.sum(
        label_hit * (log_rate + base_rows), axis=1
    )
    dlogit = (grad_scale * (hazard - event_flag[:, None] * label_hit)).astype(jnp.bfloat16)
    def block_term(owner):
        return lax.dot_general(
            dlogit, weight_rows(owner), (((1,), (1,)), ((), ())), preferred_element_type=f32
        )

    grad_hidden = block_term(head_index)
    event_loss = partial_value
    for k in range(1, head_count):
        event_loss = event_loss + shifted(partial_value, k)
    if head_count == 4:
        ahead = shifted(block_term((head_index + 1) % 4).astype(jnp.bfloat16), 1)
        relay = shifted(block_term((head_index + 2) % 4).astype(jnp.bfloat16), 3)
        carried = (relay.astype(f32) + block_term((head_index + 3) % 4)).astype(jnp.bfloat16)
        grad_hidden = grad_hidden + ahead.astype(f32) + shifted(carried, 3).astype(f32)
    else:
        for k in range(1, head_count):
            sent = block_term((head_index + k) % head_count).astype(jnp.bfloat16)
            grad_hidden = grad_hidden + shifted(sent, k).astype(f32)
    grad_norm_in = grad_hidden.reshape(shape_three)
    grad_raw = (
        grad_norm_in - normed * jnp.mean(normed * grad_norm_in, axis=-1, keepdims=True)
    ) / root_mean
    grad_out = grad_raw.astype(jnp.bfloat16)
    local_adjoint = jnp.einsum("thd,the->hde", query_rows, grad_out, preferred_element_type=f32)
    suffix = exclusive_scan(local_adjoint, "seq", reverse=True)
    back_scores = (
        jnp.einsum("the,she->hts", grad_out, value_rows, preferred_element_type=f32) * causal
    )
    grad_query = jnp.einsum(
        "hts,shd->thd", back_scores, key_rows, precision=three_pass, preferred_element_type=f32
    )
    grad_query = grad_query + jnp.einsum(
        "the,hde->thd", grad_out, prefix, precision=three_pass, preferred_element_type=f32
    )
    grad_key = jnp.einsum(
        "hts,thd->shd", back_scores, query_rows, precision=three_pass, preferred_element_type=f32
    )
    grad_key = grad_key + jnp.einsum(
        "she,hde->shd", value_rows, suffix, precision=three_pass, preferred_element_type=f32
    )
    grad_value = jnp.einsum(
        "hts,the->she", scores, grad_out, precision=three_pass, preferred_element_type=f32
    )
    grad_value = grad_value + jnp.einsum(
        "shd,hde->she", key_rows, suffix, precision=three_pass, preferred_element_type=f32
    )
    grad_queries = grad_query.reshape(rows_here, width_here).astype(jnp.bfloat16)
    grad_keys = grad_key.reshape(rows_here, width_here).astype(jnp.bfloat16)
    grad_values = grad_value.reshape(rows_here, width_here).astype(jnp.bfloat16)
    return (grad_queries, grad_keys, grad_values, event_loss)


def solution(mesh):
    placed = (
        P("seq", "head"),
        P("seq", "head"),
        P("seq", "head"),
        P(None, "head"),
        P(None, "head"),
        P("seq"),
        P("seq"),
        P("seq"),
    )
    return jax.shard_map(
        body,
        mesh=mesh,
        in_specs=placed,
        out_specs=(P("seq", "head"), P("seq", "head"), P("seq", "head"), P("seq")),
        check_vma=False,
    )
```

```python
import functools

import jax
import jax.numpy as jnp
from jax import lax
from jax.experimental import pallas as pl
from jax.experimental.pallas import tpu as pltpu
from jax.sharding import PartitionSpec as P

HEAD_DIM = 128
BINS = 32
MESH = pl.DeviceIdType.MESH


norm_eps = 1e-06
grad_scale = 64.0


def scan_kernel(reverse, count, state_ref, out_ref, other, running, exclusive, outgoing, arrived, handed, partner,
                send_sems, recv_sems):
    me = lax.axis_index("seq")
    head = lax.axis_index("head")
    core = me % 2
    mate = me + 1 - 2 * core
    half = exclusive.shape[0]
    wire = outgoing.dtype
    rounds = scan_rounds(count)
    step = -1 if reverse else 1
    plan = []
    for r, group in enumerate(rounds):
        if len(group) == 3:
            w = group[0]
            plan.append((r, w, None, 0))
            plan.append((r, 3 * w, None, 0))
            plan.append((r, w, len(plan) - 2, w))
        else:
            plan.append((r, group[0], None, 0))

    def inside(i):
        return (i >= 0) & (i < count)

    targets = [me + step * d for _, d, _, _ in plan]
    sends = []
    receives = []
    for _, d, origin, extra in plan:
        if origin is None:
            sends.append(inside(me + step * d))
            receives.append(inside(me - step * d))
        else:
            sends.append(inside(me + step * d) & inside(me - step * extra))
            receives.append(inside(me - step * (d + extra)))
    fresh = [c for c, (_, _, origin, _) in enumerate(plan) if origin is None]

    barrier = pltpu.get_barrier_semaphore()
    pl.semaphore_signal(barrier, 1, device_id=(mate, head), device_id_type=MESH)
    expected = jnp.int32(1)
    for c in fresh:
        d = plan[c][1]
        source = me - step * d
        send = inside(targets[c])
        receive = inside(source)
        target = targets[c]

        @pl.when(send)
        def _():
            pl.semaphore_signal(barrier, 1, device_id=(target, head), device_id_type=MESH)

        @pl.when(receive)
        def _():
            pl.semaphore_signal(barrier, 1, device_id=(source, head), device_id_type=MESH)

        expected = expected + send.astype(jnp.int32) + receive.astype(jnp.int32)
    pl.semaphore_wait(barrier, expected)

    swap = pltpu.make_async_remote_copy(
        state_ref, other, send_sems.at[0], recv_sems.at[0], device_id=(mate, head), device_id_type=MESH
    )
    swap.start()
    swap.wait()
    mine = pl.ds(core * half, half)
    running[...] = state_ref[mine] + other[mine]
    exclusive[...] = jnp.zeros_like(exclusive)
    copies = []
    for r in range(len(rounds)):
        outgoing[r] = running[...].astype(wire)
        members = [c for c, entry in enumerate(plan) if entry[0] == r]
        for c in members:
            origin = plan[c][2]
            if origin is not None:
                @pl.when(receives[origin])
                def _():
                    copies[origin].wait_recv()
            source_ref = outgoing.at[r] if origin is None else arrived.at[origin]
            copy = pltpu.make_async_remote_copy(
                source_ref, arrived.at[c], send_sems.at[c + 1], recv_sems.at[c + 1],
                device_id=(targets[c], head), device_id_type=MESH,
            )
            copies.append(copy)

            @pl.when(sends[c])
            def _():
                copy.start()

        for c in members:
            origin_of = [e[2] for e in plan]
            if c in origin_of:
                continue_wait = False
            else:
                continue_wait = True

            @pl.when(receives[c])
            def _():
                if continue_wait:
                    copies[c].wait_recv()
                got = arrived[c].astype(running.dtype)
                running[...] = running[...] + got
                exclusive[...] = exclusive[...] + got

    flat = plan
    last = len(flat) + 1
    handed[...] = exclusive[...].astype(wire)
    back = pltpu.make_async_remote_copy(
        handed, partner, send_sems.at[last], recv_sems.at[last], device_id=(mate, head), device_id_type=MESH
    )
    back.start()
    for copy, send in zip(copies, sends):
        @pl.when(send)
        def _():
            copy.wait_send()
    back.wait()
    theirs = pl.ds((1 - core) * half, half)
    take_other = (core == 0) if reverse else (core == 1)

    @pl.when(take_other)
    def _():
        out_ref[mine] = exclusive[...] + other[mine]
        out_ref[theirs] = partner[...].astype(out_ref.dtype) + other[theirs]

    @pl.when(jnp.logical_not(take_other))
    def _():
        out_ref[mine] = exclusive[...]
        out_ref[theirs] = partner[...].astype(out_ref.dtype)


def scan_rounds(count):
    chips = count // 2
    rounds = []
    window = 1
    while window < chips:
        if chips == 4 * window:
            rounds.append([2 * window, 4 * window, 6 * window])
            window *= 4
        else:
            rounds.append([2 * window])
            window *= 2
    return rounds


def exclusive_scan(shard, axis, reverse=False, wire=jnp.float32):
    count = lax.axis_size(axis)
    heads, rows, cols = shard.shape
    half = heads // 2
    rounds = scan_rounds(count)
    copies = max(sum(len(group) for group in rounds), 1)
    block = (half, rows, cols)
    return pl.pallas_call(
        functools.partial(scan_kernel, reverse, count),
        out_shape=jax.ShapeDtypeStruct(shard.shape, shard.dtype),
        in_specs=[pl.BlockSpec(memory_space=pltpu.VMEM)],
        out_specs=pl.BlockSpec(memory_space=pltpu.VMEM),
        scratch_shapes=[
            pltpu.VMEM((heads, rows, cols), shard.dtype),
            pltpu.VMEM(block, shard.dtype),
            pltpu.VMEM(block, shard.dtype),
            pltpu.VMEM((max(len(rounds), 1),) + block, wire),
            pltpu.VMEM((copies,) + block, wire),
            pltpu.VMEM(block, wire),
            pltpu.VMEM(block, wire),
            pltpu.SemaphoreType.DMA((copies + 2,)),
            pltpu.SemaphoreType.DMA((copies + 2,)),
        ],
        compiler_params=pltpu.CompilerParams(collective_id=1 if reverse else 0, has_side_effects=True),
    )(shard)


def body(queries, keys, values, hazard_weight, log_base, time_bin, observed, task_label):
    highest = lax.Precision.HIGHEST
    three_pass = lax.Precision.HIGH
    f32 = jnp.float32
    rows_here = queries.shape[0]
    width_here = queries.shape[1]
    heads_here = width_here // HEAD_DIM
    tasks_here = hazard_weight.shape[1]
    shape_three = (rows_here, heads_here, HEAD_DIM)
    query_rows = queries.reshape(shape_three)
    key_rows = keys.reshape(shape_three)
    value_rows = values.reshape(shape_three)
    causal = jnp.tril(jnp.ones((rows_here, rows_here), f32))
    local_state = jnp.einsum("thd,the->hde", key_rows, value_rows, preferred_element_type=f32)
    prefix = exclusive_scan(local_state, "seq")
    scores = jnp.einsum("thd,shd->hts", query_rows, key_rows, preferred_element_type=f32) * causal
    raw_out = jnp.einsum(
        "hts,she->the", scores, value_rows, precision=three_pass, preferred_element_type=f32
    )
    raw_out = raw_out + jnp.einsum(
        "thd,hde->the", query_rows, prefix, precision=three_pass, preferred_element_type=f32
    )
    root_mean = jnp.sqrt(jnp.mean(raw_out * raw_out, axis=-1, keepdims=True) + norm_eps)
    normed = raw_out / root_mean
    hidden = normed.astype(jnp.bfloat16).reshape(rows_here, width_here)
    head_count = lax.axis_size("head")
    head_index = lax.axis_index("head")

    def shifted(x, k):
        return lax.ppermute(x, "head", [(m, (m + k) % head_count) for m in range(head_count)])

    def weight_rows(owner):
        return lax.dynamic_slice_in_dim(hazard_weight, owner * width_here, width_here, 0)

    log_rate = jnp.dot(hidden, weight_rows(head_index), preferred_element_type=f32)
    if head_count == 4:
        behind = shifted(hidden, 1)
        received = {1: behind, 2: shifted(behind, 1), 3: shifted(hidden, 3)}
    else:
        received = {k: shifted(hidden, k) for k in range(1, head_count)}
    for k in range(1, head_count):
        log_rate = log_rate + jnp.dot(
            received[k],
            weight_rows((head_index - k + head_count) % head_count),
            preferred_element_type=f32,
        )
    offset = head_index * tasks_here
    cum_base = jnp.cumsum(jnp.exp(log_base), axis=0)
    bin_hot = (time_bin[:, None] == jnp.arange(BINS, dtype=jnp.int32)[None, :]).astype(f32)
    base_rows = jnp.dot(bin_hot, log_base, precision=highest)
    cum_rows = jnp.dot(bin_hot, cum_base, precision=highest)
    hazard = jnp.exp(log_rate) * cum_rows
    columns = offset + jnp.arange(tasks_here, dtype=jnp.int32)
    label_hit = (task_label[:, None] == columns[None, :]).astype(f32)
    event_flag = observed.astype(f32)
    partial_value = jnp.sum(hazard, axis=1) - event_flag * jnp.sum(
        label_hit * (log_rate + base_rows), axis=1
    )
    dlogit = (grad_scale * (hazard - event_flag[:, None] * label_hit)).astype(jnp.bfloat16)
    def block_term(owner):
        return lax.dot_general(
            dlogit, weight_rows(owner), (((1,), (1,)), ((), ())), preferred_element_type=f32
        )

    grad_hidden = block_term(head_index)
    event_loss = partial_value
    for k in range(1, head_count):
        event_loss = event_loss + shifted(partial_value, k)
    if head_count == 4:
        ahead = shifted(block_term((head_index + 1) % 4).astype(jnp.bfloat16), 1)
        relay = shifted(block_term((head_index + 2) % 4).astype(jnp.bfloat16), 3)
        carried = (relay.astype(f32) + block_term((head_index + 3) % 4)).astype(jnp.bfloat16)
        grad_hidden = grad_hidden + ahead.astype(f32) + shifted(carried, 3).astype(f32)
    else:
        for k in range(1, head_count):
            sent = block_term((head_index + k) % head_count).astype(jnp.bfloat16)
            grad_hidden = grad_hidden + shifted(sent, k).astype(f32)
    grad_norm_in = grad_hidden.reshape(shape_three)
    grad_raw = (
        grad_norm_in - normed * jnp.mean(normed * grad_norm_in, axis=-1, keepdims=True)
    ) / root_mean
    grad_out = grad_raw.astype(jnp.bfloat16)
    local_adjoint = jnp.einsum("thd,the->hde", query_rows, grad_out, preferred_element_type=f32)
    suffix = exclusive_scan(local_adjoint, "seq", reverse=True)
    back_scores = (
        jnp.einsum("the,she->hts", grad_out, value_rows, preferred_element_type=f32) * causal
    )
    grad_query = jnp.einsum(
        "hts,shd->thd", back_scores, key_rows, precision=three_pass, preferred_element_type=f32
    )
    grad_query = grad_query + jnp.einsum(
        "the,hde->thd", grad_out, prefix, precision=three_pass, preferred_element_type=f32
    )
    grad_key = jnp.einsum(
        "hts,thd->shd", back_scores, query_rows, precision=three_pass, preferred_element_type=f32
    )
    grad_key = grad_key + jnp.einsum(
        "she,hde->shd", value_rows, suffix, precision=three_pass, preferred_element_type=f32
    )
    grad_value = jnp.einsum(
        "hts,the->she", scores, grad_out, precision=three_pass, preferred_element_type=f32
    )
    grad_value = grad_value + jnp.einsum(
        "shd,hde->she", key_rows, suffix, precision=three_pass, preferred_element_type=f32
    )
    grad_queries = grad_query.reshape(rows_here, width_here).astype(jnp.bfloat16)
    grad_keys = grad_key.reshape(rows_here, width_here).astype(jnp.bfloat16)
    grad_values = grad_value.reshape(rows_here, width_here).astype(jnp.bfloat16)
    return (grad_queries, grad_keys, grad_values, event_loss)


def solution(mesh):
    placed = (
        P("seq", "head"),
        P("seq", "head"),
        P("seq", "head"),
        P(None, "head"),
        P(None, "head"),
        P("seq"),
        P("seq"),
        P("seq"),
    )
    return jax.shard_map(
        body,
        mesh=mesh,
        in_specs=placed,
        out_specs=(P("seq", "head"), P("seq", "head"), P("seq", "head"), P("seq")),
        check_vma=False,
    )
```

```python
import functools

import jax
import jax.numpy as jnp
from jax import lax
from jax.experimental import pallas as pl
from jax.experimental.pallas import tpu as pltpu
from jax.sharding import PartitionSpec as P

HEAD_DIM = 128
BINS = 32
MESH = pl.DeviceIdType.MESH


norm_eps = 1e-06
grad_scale = 64.0


def scan_kernel(reverse, count, state_ref, out_ref, other, running, exclusive, outgoing, arrived, handed, partner,
                send_sems, recv_sems):
    me = lax.axis_index("seq")
    head = lax.axis_index("head")
    core = me % 2
    mate = me + 1 - 2 * core
    half = exclusive.shape[0]
    wire = outgoing.dtype
    rounds = scan_rounds(count)
    step = -1 if reverse else 1
    flat = [(r, d) for r, group in enumerate(rounds) for d in group]
    targets = [me + step * d for _, d in flat]
    sources = [me - step * d for _, d in flat]
    sends = [(t >= 0) & (t < count) for t in targets]
    receives = [(s >= 0) & (s < count) for s in sources]

    barrier = pltpu.get_barrier_semaphore()
    pl.semaphore_signal(barrier, 1, device_id=(mate, head), device_id_type=MESH)
    expected = jnp.int32(1)
    for target, source, send, receive in zip(targets, sources, sends, receives):
        @pl.when(send)
        def _():
            pl.semaphore_signal(barrier, 1, device_id=(target, head), device_id_type=MESH)

        @pl.when(receive)
        def _():
            pl.semaphore_signal(barrier, 1, device_id=(source, head), device_id_type=MESH)

        expected = expected + send.astype(jnp.int32) + receive.astype(jnp.int32)
    pl.semaphore_wait(barrier, expected)

    swap = pltpu.make_async_remote_copy(
        state_ref, other, send_sems.at[0], recv_sems.at[0], device_id=(mate, head), device_id_type=MESH
    )
    swap.start()
    swap.wait()
    mine = pl.ds(core * half, half)
    running[...] = state_ref[mine] + other[mine]
    exclusive[...] = jnp.zeros_like(exclusive)
    copies = []
    for r, group in enumerate(rounds):
        outgoing[r] = running[...].astype(wire)
        members = [c for c, (owner, _) in enumerate(flat) if owner == r]
        for c in members:
            copy = pltpu.make_async_remote_copy(
                outgoing.at[r], arrived.at[c], send_sems.at[c + 1], recv_sems.at[c + 1],
                device_id=(targets[c], head), device_id_type=MESH,
            )
            copies.append(copy)

            @pl.when(sends[c])
            def _():
                copy.start()

        for c in members:
            @pl.when(receives[c])
            def _():
                copies[c].wait_recv()
                got = arrived[c].astype(running.dtype)
                running[...] = running[...] + got
                exclusive[...] = exclusive[...] + got

    last = len(flat) + 1
    handed[...] = exclusive[...].astype(wire)
    back = pltpu.make_async_remote_copy(
        handed, partner, send_sems.at[last], recv_sems.at[last], device_id=(mate, head), device_id_type=MESH
    )
    back.start()
    for copy, send in zip(copies, sends):
        @pl.when(send)
        def _():
            copy.wait_send()
    back.wait()
    theirs = pl.ds((1 - core) * half, half)
    take_other = (core == 0) if reverse else (core == 1)

    @pl.when(take_other)
    def _():
        out_ref[mine] = exclusive[...] + other[mine]
        out_ref[theirs] = partner[...].astype(out_ref.dtype) + other[theirs]

    @pl.when(jnp.logical_not(take_other))
    def _():
        out_ref[mine] = exclusive[...]
        out_ref[theirs] = partner[...].astype(out_ref.dtype)


def scan_rounds(count):
    chips = count // 2
    rounds = []
    window = 1
    while window < chips:
        if chips == 4 * window:
            rounds.append([2 * window, 4 * window, 6 * window])
            window *= 4
        else:
            rounds.append([2 * window])
            window *= 2
    return rounds


def exclusive_scan(shard, axis, reverse=False, wire=jnp.float32):
    count = lax.axis_size(axis)
    heads, rows, cols = shard.shape
    half = heads // 2
    rounds = scan_rounds(count)
    copies = max(sum(len(group) for group in rounds), 1)
    block = (half, rows, cols)
    return pl.pallas_call(
        functools.partial(scan_kernel, reverse, count),
        out_shape=jax.ShapeDtypeStruct(shard.shape, shard.dtype),
        in_specs=[pl.BlockSpec(memory_space=pltpu.VMEM)],
        out_specs=pl.BlockSpec(memory_space=pltpu.VMEM),
        scratch_shapes=[
            pltpu.VMEM((heads, rows, cols), shard.dtype),
            pltpu.VMEM(block, shard.dtype),
            pltpu.VMEM(block, shard.dtype),
            pltpu.VMEM((max(len(rounds), 1),) + block, wire),
            pltpu.VMEM((copies,) + block, wire),
            pltpu.VMEM(block, wire),
            pltpu.VMEM(block, wire),
            pltpu.SemaphoreType.DMA((copies + 2,)),
            pltpu.SemaphoreType.DMA((copies + 2,)),
        ],
        compiler_params=pltpu.CompilerParams(collective_id=1 if reverse else 0, has_side_effects=True),
    )(shard)


def body(queries, keys, values, hazard_weight, log_base, time_bin, observed, task_label):
    highest = lax.Precision.HIGHEST
    three_pass = lax.Precision.HIGH
    f32 = jnp.float32
    rows_here = queries.shape[0]
    width_here = queries.shape[1]
    heads_here = width_here // HEAD_DIM
    tasks_here = hazard_weight.shape[1]
    shape_three = (rows_here, heads_here, HEAD_DIM)
    query_rows = queries.reshape(shape_three)
    key_rows = keys.reshape(shape_three)
    value_rows = values.reshape(shape_three)
    causal = jnp.tril(jnp.ones((rows_here, rows_here), f32))
    local_state = jnp.einsum("thd,the->hde", key_rows, value_rows, preferred_element_type=f32)
    prefix = exclusive_scan(local_state, "seq")
    scores = jnp.einsum("thd,shd->hts", query_rows, key_rows, preferred_element_type=f32) * causal
    raw_out = jnp.einsum(
        "hts,she->the", scores, value_rows, precision=three_pass, preferred_element_type=f32
    )
    raw_out = raw_out + jnp.einsum(
        "thd,hde->the", query_rows, prefix, precision=three_pass, preferred_element_type=f32
    )
    root_mean = jnp.sqrt(jnp.mean(raw_out * raw_out, axis=-1, keepdims=True) + norm_eps)
    normed = raw_out / root_mean
    hidden = normed.astype(jnp.bfloat16).reshape(rows_here, width_here)
    head_count = lax.axis_size("head")
    head_index = lax.axis_index("head")

    def shifted(x, k):
        return lax.ppermute(x, "head", [(m, (m + k) % head_count) for m in range(head_count)])

    def weight_rows(owner):
        return lax.dynamic_slice_in_dim(hazard_weight, owner * width_here, width_here, 0)

    log_rate = jnp.dot(hidden, weight_rows(head_index), preferred_element_type=f32)
    if head_count == 4:
        behind = shifted(hidden, 1)
        received = {1: behind, 2: shifted(behind, 1), 3: shifted(hidden, 3)}
    else:
        received = {k: shifted(hidden, k) for k in range(1, head_count)}
    for k in range(1, head_count):
        log_rate = log_rate + jnp.dot(
            received[k],
            weight_rows((head_index - k + head_count) % head_count),
            preferred_element_type=f32,
        )
    offset = head_index * tasks_here
    cum_base = jnp.cumsum(jnp.exp(log_base), axis=0)
    bin_hot = (time_bin[:, None] == jnp.arange(BINS, dtype=jnp.int32)[None, :]).astype(f32)
    base_rows = jnp.dot(bin_hot, log_base, precision=highest)
    cum_rows = jnp.dot(bin_hot, cum_base, precision=highest)
    hazard = jnp.exp(log_rate) * cum_rows
    columns = offset + jnp.arange(tasks_here, dtype=jnp.int32)
    label_hit = (task_label[:, None] == columns[None, :]).astype(f32)
    event_flag = observed.astype(f32)
    partial_value = jnp.sum(hazard, axis=1) - event_flag * jnp.sum(
        label_hit * (log_rate + base_rows), axis=1
    )
    dlogit = (grad_scale * (hazard - event_flag[:, None] * label_hit)).astype(jnp.bfloat16)
    def block_term(owner):
        return lax.dot_general(
            dlogit, weight_rows(owner), (((1,), (1,)), ((), ())), preferred_element_type=f32
        )

    grad_hidden = block_term(head_index)
    loss_parts = [shifted(partial_value, k) for k in range(1, head_count)]
    if head_count == 4:
        ahead = shifted(block_term((head_index + 1) % 4).astype(jnp.bfloat16), 1)
        relay = shifted(block_term((head_index + 2) % 4).astype(jnp.bfloat16), 3)
        carried = (relay.astype(f32) + block_term((head_index + 3) % 4)).astype(jnp.bfloat16)
        grad_hidden = grad_hidden + ahead.astype(f32) + shifted(carried, 3).astype(f32)
    else:
        for k in range(1, head_count):
            sent = block_term((head_index + k) % head_count).astype(jnp.bfloat16)
            grad_hidden = grad_hidden + shifted(sent, k).astype(f32)
    grad_norm_in = grad_hidden.reshape(shape_three)
    grad_raw = (
        grad_norm_in - normed * jnp.mean(normed * grad_norm_in, axis=-1, keepdims=True)
    ) / root_mean
    grad_out = grad_raw.astype(jnp.bfloat16)
    local_adjoint = jnp.einsum("thd,the->hde", query_rows, grad_out, preferred_element_type=f32)
    suffix = exclusive_scan(local_adjoint, "seq", reverse=True)
    loss_parts, suffix = lax.optimization_barrier((loss_parts, suffix))
    event_loss = partial_value
    for part in loss_parts:
        event_loss = event_loss + part
    back_scores = (
        jnp.einsum("the,she->hts", grad_out, value_rows, preferred_element_type=f32) * causal
    )
    grad_query = jnp.einsum(
        "hts,shd->thd", back_scores, key_rows, precision=three_pass, preferred_element_type=f32
    )
    grad_query = grad_query + jnp.einsum(
        "the,hde->thd", grad_out, prefix, precision=three_pass, preferred_element_type=f32
    )
    grad_key = jnp.einsum(
        "hts,thd->shd", back_scores, query_rows, precision=three_pass, preferred_element_type=f32
    )
    grad_key = grad_key + jnp.einsum(
        "she,hde->shd", value_rows, suffix, precision=three_pass, preferred_element_type=f32
    )
    grad_value = jnp.einsum(
        "hts,the->she", scores, grad_out, precision=three_pass, preferred_element_type=f32
    )
    grad_value = grad_value + jnp.einsum(
        "shd,hde->she", key_rows, suffix, precision=three_pass, preferred_element_type=f32
    )
    grad_queries = grad_query.reshape(rows_here, width_here).astype(jnp.bfloat16)
    grad_keys = grad_key.reshape(rows_here, width_here).astype(jnp.bfloat16)
    grad_values = grad_value.reshape(rows_here, width_here).astype(jnp.bfloat16)
    return (grad_queries, grad_keys, grad_values, event_loss)


def solution(mesh):
    placed = (
        P("seq", "head"),
        P("seq", "head"),
        P("seq", "head"),
        P(None, "head"),
        P(None, "head"),
        P("seq"),
        P("seq"),
        P("seq"),
    )
    return jax.shard_map(
        body,
        mesh=mesh,
        in_specs=placed,
        out_specs=(P("seq", "head"), P("seq", "head"), P("seq", "head"), P("seq")),
        check_vma=False,
    )
```

```python
import functools

import jax
import jax.numpy as jnp
from jax import lax
from jax.experimental import pallas as pl
from jax.experimental.pallas import tpu as pltpu
from jax.sharding import PartitionSpec as P

HEAD_DIM = 128
BINS = 32
MESH = pl.DeviceIdType.MESH


norm_eps = 1e-06
grad_scale = 64.0


def scan_kernel(reverse, count, state_ref, out_ref, other, running, exclusive, outgoing, arrived, handed, partner,
                send_sems, recv_sems):
    me = lax.axis_index("seq")
    head = lax.axis_index("head")
    core = me % 2
    mate = me + 1 - 2 * core
    half = exclusive.shape[0]
    wire = outgoing.dtype
    rounds = scan_rounds(count)
    step = -1 if reverse else 1
    flat = [(r, d) for r, group in enumerate(rounds) for d in group]
    targets = [me + step * d for _, d in flat]
    sources = [me - step * d for _, d in flat]
    sends = [(t >= 0) & (t < count) for t in targets]
    receives = [(s >= 0) & (s < count) for s in sources]

    barrier = pltpu.get_barrier_semaphore()
    pl.semaphore_signal(barrier, 1, device_id=(mate, head), device_id_type=MESH)
    expected = jnp.int32(1)
    for target, source, send, receive in zip(targets, sources, sends, receives):
        @pl.when(send)
        def _():
            pl.semaphore_signal(barrier, 1, device_id=(target, head), device_id_type=MESH)

        @pl.when(receive)
        def _():
            pl.semaphore_signal(barrier, 1, device_id=(source, head), device_id_type=MESH)

        expected = expected + send.astype(jnp.int32) + receive.astype(jnp.int32)
    pl.semaphore_wait(barrier, expected)

    swap = pltpu.make_async_remote_copy(
        state_ref, other, send_sems.at[0], recv_sems.at[0], device_id=(mate, head), device_id_type=MESH
    )
    swap.start()
    swap.wait()
    mine = pl.ds(core * half, half)
    running[...] = state_ref[mine] + other[mine]
    exclusive[...] = jnp.zeros_like(exclusive)
    copies = []
    for r, group in enumerate(rounds):
        outgoing[r] = running[...].astype(wire)
        members = [c for c, (owner, _) in enumerate(flat) if owner == r]
        for c in members:
            copy = pltpu.make_async_remote_copy(
                outgoing.at[r], arrived.at[c], send_sems.at[c + 1], recv_sems.at[c + 1],
                device_id=(targets[c], head), device_id_type=MESH,
            )
            copies.append(copy)

            @pl.when(sends[c])
            def _():
                copy.start()

        for c in members:
            @pl.when(receives[c])
            def _():
                copies[c].wait_recv()
                got = arrived[c].astype(running.dtype)
                running[...] = running[...] + got
                exclusive[...] = exclusive[...] + got

    last = len(flat) + 1
    handed[...] = exclusive[...].astype(wire)
    back = pltpu.make_async_remote_copy(
        handed, partner, send_sems.at[last], recv_sems.at[last], device_id=(mate, head), device_id_type=MESH
    )
    back.start()
    for copy, send in zip(copies, sends):
        @pl.when(send)
        def _():
            copy.wait_send()
    back.wait()
    theirs = pl.ds((1 - core) * half, half)
    take_other = (core == 0) if reverse else (core == 1)

    @pl.when(take_other)
    def _():
        out_ref[mine] = exclusive[...] + other[mine]
        out_ref[theirs] = partner[...].astype(out_ref.dtype) + other[theirs]

    @pl.when(jnp.logical_not(take_other))
    def _():
        out_ref[mine] = exclusive[...]
        out_ref[theirs] = partner[...].astype(out_ref.dtype)


def scan_rounds(count):
    chips = count // 2
    rounds = []
    window = 1
    while window < chips:
        if chips == 4 * window:
            rounds.append([2 * window, 4 * window, 6 * window])
            window *= 4
        else:
            rounds.append([2 * window])
            window *= 2
    return rounds


def exclusive_scan(shard, axis, reverse=False, wire=jnp.float32):
    count = lax.axis_size(axis)
    heads, rows, cols = shard.shape
    half = heads // 2
    rounds = scan_rounds(count)
    copies = max(sum(len(group) for group in rounds), 1)
    block = (half, rows, cols)
    return pl.pallas_call(
        functools.partial(scan_kernel, reverse, count),
        out_shape=jax.ShapeDtypeStruct(shard.shape, shard.dtype),
        in_specs=[pl.BlockSpec(memory_space=pltpu.VMEM)],
        out_specs=pl.BlockSpec(memory_space=pltpu.VMEM),
        scratch_shapes=[
            pltpu.VMEM((heads, rows, cols), shard.dtype),
            pltpu.VMEM(block, shard.dtype),
            pltpu.VMEM(block, shard.dtype),
            pltpu.VMEM((max(len(rounds), 1),) + block, wire),
            pltpu.VMEM((copies,) + block, wire),
            pltpu.VMEM(block, wire),
            pltpu.VMEM(block, wire),
            pltpu.SemaphoreType.DMA((copies + 2,)),
            pltpu.SemaphoreType.DMA((copies + 2,)),
        ],
        compiler_params=pltpu.CompilerParams(collective_id=1 if reverse else 0, has_side_effects=True),
    )(shard)


def body(queries, keys, values, hazard_weight, log_base, time_bin, observed, task_label):
    highest = lax.Precision.HIGHEST
    three_pass = lax.Precision.HIGH
    f32 = jnp.float32
    rows_here = queries.shape[0]
    width_here = queries.shape[1]
    heads_here = width_here // HEAD_DIM
    tasks_here = hazard_weight.shape[1]
    shape_three = (rows_here, heads_here, HEAD_DIM)
    query_rows = queries.reshape(shape_three)
    key_rows = keys.reshape(shape_three)
    value_rows = values.reshape(shape_three)
    causal = jnp.tril(jnp.ones((rows_here, rows_here), f32))
    local_state = jnp.einsum("thd,the->hde", key_rows, value_rows, preferred_element_type=f32)
    prefix = exclusive_scan(local_state, "seq")
    scores = jnp.einsum("thd,shd->hts", query_rows, key_rows, preferred_element_type=f32) * causal
    raw_out = jnp.einsum(
        "hts,she->the", scores, value_rows, precision=three_pass, preferred_element_type=f32
    )
    raw_out = raw_out + jnp.einsum(
        "thd,hde->the", query_rows, prefix, precision=three_pass, preferred_element_type=f32
    )
    root_mean = jnp.sqrt(jnp.mean(raw_out * raw_out, axis=-1, keepdims=True) + norm_eps)
    normed = raw_out / root_mean
    hidden = normed.astype(jnp.bfloat16).reshape(rows_here, width_here)
    head_count = lax.axis_size("head")
    head_index = lax.axis_index("head")

    def shifted(x, k):
        return lax.ppermute(x, "head", [(m, (m + k) % head_count) for m in range(head_count)])

    def weight_rows(owner):
        return lax.dynamic_slice_in_dim(hazard_weight, owner * width_here, width_here, 0)

    log_rate = jnp.dot(hidden, weight_rows(head_index), preferred_element_type=f32)
    if head_count == 4:
        behind = shifted(hidden, 1)
        received = {1: behind, 2: shifted(behind, 1), 3: shifted(hidden, 3)}
    else:
        received = {k: shifted(hidden, k) for k in range(1, head_count)}
    for k in range(1, head_count):
        log_rate = log_rate + jnp.dot(
            received[k],
            weight_rows((head_index - k + head_count) % head_count),
            preferred_element_type=f32,
        )
    offset = head_index * tasks_here
    cum_base = jnp.cumsum(jnp.exp(log_base), axis=0)
    bin_hot = (time_bin[:, None] == jnp.arange(BINS, dtype=jnp.int32)[None, :]).astype(f32)
    base_rows = jnp.dot(bin_hot, log_base, precision=highest)
    cum_rows = jnp.dot(bin_hot, cum_base, precision=highest)
    hazard = jnp.exp(log_rate) * cum_rows
    columns = offset + jnp.arange(tasks_here, dtype=jnp.int32)
    label_hit = (task_label[:, None] == columns[None, :]).astype(f32)
    event_flag = observed.astype(f32)
    partial_value = jnp.sum(hazard, axis=1) - event_flag * jnp.sum(
        label_hit * (log_rate + base_rows), axis=1
    )
    dlogit = (grad_scale * (hazard - event_flag[:, None] * label_hit)).astype(jnp.bfloat16)
    def block_term(owner):
        return lax.dot_general(
            dlogit, weight_rows(owner), (((1,), (1,)), ((), ())), preferred_element_type=f32
        )

    grad_hidden = block_term(head_index)
    loss_parts = [shifted(partial_value, k) for k in range(1, head_count)]
    if head_count == 4:
        ahead = shifted(block_term((head_index + 1) % 4).astype(jnp.bfloat16), 1)
        relay = shifted(block_term((head_index + 2) % 4).astype(jnp.bfloat16), 3)
        carried = (relay.astype(f32) + block_term((head_index + 3) % 4)).astype(jnp.bfloat16)
        grad_hidden = grad_hidden + ahead.astype(f32) + shifted(carried, 3).astype(f32)
    else:
        for k in range(1, head_count):
            sent = block_term((head_index + k) % head_count).astype(jnp.bfloat16)
            grad_hidden = grad_hidden + shifted(sent, k).astype(f32)
    grad_norm_in = grad_hidden.reshape(shape_three)
    grad_raw = (
        grad_norm_in - normed * jnp.mean(normed * grad_norm_in, axis=-1, keepdims=True)
    ) / root_mean
    grad_out = grad_raw.astype(jnp.bfloat16)
    local_adjoint = jnp.einsum("thd,the->hde", query_rows, grad_out, preferred_element_type=f32)
    back_scores = (
        jnp.einsum("the,she->hts", grad_out, value_rows, preferred_element_type=f32) * causal
    )
    grad_query = jnp.einsum(
        "hts,shd->thd", back_scores, key_rows, precision=three_pass, preferred_element_type=f32
    )
    grad_query = grad_query + jnp.einsum(
        "the,hde->thd", grad_out, prefix, precision=three_pass, preferred_element_type=f32
    )
    grad_queries = grad_query.reshape(rows_here, width_here).astype(jnp.bfloat16)
    grad_queries, local_adjoint = lax.optimization_barrier((grad_queries, local_adjoint))
    suffix = exclusive_scan(local_adjoint, "seq", reverse=True)
    loss_parts, suffix = lax.optimization_barrier((loss_parts, suffix))
    event_loss = partial_value
    for part in loss_parts:
        event_loss = event_loss + part
    grad_key = jnp.einsum(
        "hts,thd->shd", back_scores, query_rows, precision=three_pass, preferred_element_type=f32
    )
    grad_key = grad_key + jnp.einsum(
        "she,hde->shd", value_rows, suffix, precision=three_pass, preferred_element_type=f32
    )
    grad_value = jnp.einsum(
        "hts,the->she", scores, grad_out, precision=three_pass, preferred_element_type=f32
    )
    grad_value = grad_value + jnp.einsum(
        "shd,hde->she", key_rows, suffix, precision=three_pass, preferred_element_type=f32
    )
    grad_keys = grad_key.reshape(rows_here, width_here).astype(jnp.bfloat16)
    grad_values = grad_value.reshape(rows_here, width_here).astype(jnp.bfloat16)
    return (grad_queries, grad_keys, grad_values, event_loss)


def solution(mesh):
    placed = (
        P("seq", "head"),
        P("seq", "head"),
        P("seq", "head"),
        P(None, "head"),
        P(None, "head"),
        P("seq"),
        P("seq"),
        P("seq"),
    )
    return jax.shard_map(
        body,
        mesh=mesh,
        in_specs=placed,
        out_specs=(P("seq", "head"), P("seq", "head"), P("seq", "head"), P("seq")),
        check_vma=False,
    )
```
